512 devices in a mesh: member: 8 (over y_lo, core), slab: 64 (over y_hi, x, z).
Axes of the slice: x: 4, y: 8 (y_hi: 2, y_lo: 4; y = y_hi * 4 + y_lo), z: 8, core: 2. Of those that a mesh axis runs over, the one named last changes fastest.
Arguments:
- base_field: bfloat16 [32, 512, 2, 512], P(None, 'slab'), may hold values from -6 to 6
- forcing: bfloat16 [512, 2, 512], P('slab'), may hold values from -6 to 6
- load: float32 [32], replicated, may hold values from 0.25 to 1.75
- amplitudes: float32 [16], replicated, may hold values from 0.25 to 2
- amp_index: int32 [8], P('member'), may hold values from 0 to 15
- mode_count: int32 [8], P('member'), may hold values from 32 to 64, as said below
- point_weight: bfloat16 [32, 32], replicated, may hold values from -1 to 1
- point_bias: float32 [32], replicated, may hold values from -3 to 3
- spectral_weight: bfloat16 [64, 64, 2, 32, 32], P('slab'), may hold values from -6 to 6
Outputs:
- dependence: bfloat16 [32, 512, 2, 512], P('member', 'slab')
The draws below stay inside these ranges and needn't reach their ends.
Inputs may be any that keep to these rules, and one draw needn't show every extreme that they name: `mode_count`: each member keeps the second-dimension modes below its count; some member keeps all 64.
All inputs are finite; a program needn't handle non-finite values.
Results may differ from the reference program's by a relative error of at most 0.015.
Values may be sent and summed in bfloat16 or wider, within the bound.
A program may use at most 64 MiB of HBM per device.

```python
import math
import jax
import jax.numpy as jnp
from jax import lax

C = 32
NX = 512
NY = 512
KX = 64
KY = 64
ZP = 2
LEVELS = 16
MEMBERS = 8


def draw_mode_count(key, part):
    count_key = jax.random.fold_in(key, 11)
    order_key = jax.random.fold_in(key, 23)
    counts = jax.random.randint(count_key, (MEMBERS,), KY // 2, KY + 1)
    order = jax.random.permutation(order_key, MEMBERS)
    counts = counts.at[order[0]].set(KY)
    if MEMBERS > 2:
        counts = counts.at[order[1]].set(KY // 2)
    return counts.astype(jnp.int32)


def place_ends(result, key, smallest, top_value):
    extent = result.shape
    spot = [jax.random.randint(jax.random.fold_in(key, axis), (), 0, extent[axis]) for axis in range(len(extent))]
    result = result.at[tuple(spot)].set(smallest)
    longest = extent.index(max(extent))
    spot[longest] = (spot[longest] + 1) % extent[longest]
    return result.at[tuple(spot)].set(top_value)


def block_scale(rng, extent, split, least, top_value):
    def one(dim, shards_of):
        heights = jax.random.uniform(jax.random.fold_in(jax.random.fold_in(rng, 6), dim), (shards_of,), jnp.float32, least / len(split), top_value / len(split))
        return jnp.repeat(jnp.exp(heights), extent[dim] // shards_of).reshape((-1,) + (1,) * (len(extent) - dim - 1))

    gain = one(*split[0])
    for cut in split[1:]:
        gain = gain * one(*cut)
    return gain


def bell_draw(stream_key, extent, deviation, most, cuts=(), kind=jnp.bfloat16):
    entries = deviation * jax.random.normal(stream_key, extent, jnp.float32)
    if cuts:
        entries = entries * block_scale(stream_key, extent, cuts, -0.22, 0.18)
    return jnp.clip(entries, -most, most).astype(kind)


def setup_inputs(seed: int = 0) -> dict:
    key_of = jax.random.split(jax.random.key(seed), 10)
    return {
        "base_field": bell_draw(key_of[0], (C, NX, ZP, NY), 1.0, 6.0, ((1, 64),)),
        "forcing": bell_draw(key_of[1], (NX, ZP, NY), 1.0, 6.0, ((0, 64),)),
        "load": jnp.clip(1.0 + 0.15 * jax.random.normal(key_of[2], (C,), jnp.float32), 0.25, 1.75),
        "amplitudes": jnp.clip(jnp.exp(jax.random.uniform(key_of[3], (LEVELS,), jnp.float32, math.log(0.25), math.log(2.0))), 0.25, 2.0),
        "amp_index": place_ends(jax.random.randint(key_of[4], (MEMBERS,), 0, LEVELS), jax.random.fold_in(key_of[4], 1), 0, LEVELS - 1).astype(jnp.int32),
        "mode_count": draw_mode_count(jax.random.fold_in(key_of[9], 71), 0),
        "point_weight": bell_draw(key_of[6], (C, C), C ** -0.5, 1.0),
        "point_bias": bell_draw(key_of[7], (C,), 0.5, 3.0, (), jnp.float32),
        "spectral_weight": bell_draw(key_of[8], (KY, KX, 2, C, C), (max(1, NX * NY // (2 * C * KX * KY))) ** -0.5, 6.0, ((0, 64),)),
    }


TWO_PI = 2.0 * math.pi


def phases(frequency, positions, length):
    product = (frequency[:, None] * positions[None, :]) % length
    angles = product.astype(jnp.float32) * (TWO_PI / length)
    return jnp.cos(angles), jnp.sin(angles)


def rounded(values):
    return lax.optimization_barrier(values.astype(jnp.bfloat16)).astype(jnp.float32)


def reference(base_field, forcing, load, amplitudes, amp_index, mode_count, point_weight, point_bias, spectral_weight):
    y_cos, y_sin = phases(jnp.arange(KY, dtype=jnp.int32), jnp.arange(NY, dtype=jnp.int32), NY)
    fwd_cos_y = y_cos.astype(jnp.bfloat16).astype(jnp.float32)
    fwd_sin_y = y_sin.astype(jnp.bfloat16).astype(jnp.float32)
    scale_y = jnp.where(jnp.arange(KY) == 0, 1.0, 2.0).astype(jnp.float32) / (NX * NY)
    inv_cos_y = (scale_y[:, None] * y_cos).astype(jnp.bfloat16).astype(jnp.float32)
    inv_sin_y = (scale_y[:, None] * y_sin).astype(jnp.bfloat16).astype(jnp.float32)
    frequency_x = jnp.concatenate([jnp.arange(KX // 2, dtype=jnp.int32), jnp.arange(NX - KX // 2, NX, dtype=jnp.int32)])
    x_cos, x_sin = phases(frequency_x, jnp.arange(NX, dtype=jnp.int32), NX)
    x_cos = x_cos.astype(jnp.bfloat16).astype(jnp.float32)
    x_sin = x_sin.astype(jnp.bfloat16).astype(jnp.float32)
    weight_f = point_weight.astype(jnp.float32)
    spec_f = spectral_weight.astype(jnp.float32)
    weight_real = spec_f[:, :, 0]
    weight_imag = spec_f[:, :, 1]
    base_f = base_field.astype(jnp.float32)
    forcing_f = forcing.astype(jnp.float32)
    levels = amplitudes[amp_index]

    def mixing(weights, values):
        return jnp.einsum("kmoi,kmiz->kmoz", weights, values)

    def member_step(total, member_data):
        amplitude, keep_count = member_data
        driven = base_f + amplitude * load[:, None, None, None] * forcing_f[None]
        field_now = (2.0 * jnp.tanh(0.5 * driven)).astype(jnp.bfloat16)
        field_f = field_now.astype(jnp.float32)
        y_real = jnp.einsum("cxzy,ky->kxcz", field_f, fwd_cos_y)
        y_imag = -jnp.einsum("cxzy,ky->kxcz", field_f, fwd_sin_y)
        packed = rounded(jnp.stack([y_real, y_imag], axis=2))
        with_cos = jnp.einsum("kxrcz,mx->kmrcz", packed, x_cos)
        with_sin = jnp.einsum("kxrcz,mx->kmrcz", packed, x_sin)
        spec_real = rounded(with_cos[:, :, 0] + with_sin[:, :, 1])
        spec_imag = rounded(with_cos[:, :, 1] - with_sin[:, :, 0])
        mix_real = mixing(weight_real, spec_real) - mixing(weight_imag, spec_imag)
        mix_imag = mixing(weight_real, spec_imag) + mixing(weight_imag, spec_real)
        keep = (jnp.arange(KY, dtype=jnp.int32) < keep_count).astype(jnp.float32)[:, None, None, None]
        mix_real = rounded(mix_real * keep)
        mix_imag = rounded(mix_imag * keep)
        back_real = rounded(jnp.einsum("kmoz,mx->kxoz", mix_real, x_cos) - jnp.einsum("kmoz,mx->kxoz", mix_imag, x_sin))
        back_imag = rounded(jnp.einsum("kmoz,mx->kxoz", mix_imag, x_cos) + jnp.einsum("kmoz,mx->kxoz", mix_real, x_sin))
        spectral = jnp.einsum("kxcz,ky->cxzy", back_real, inv_cos_y) - jnp.einsum("kxcz,ky->cxzy", back_imag, inv_sin_y)
        pointwise = jnp.einsum("oc,cxzy->oxzy", weight_f, field_f) + point_bias[:, None, None, None]
        layer = rounded(jax.nn.gelu(pointwise + spectral, approximate=True))
        return total + layer, None

    total, _ = lax.scan(member_step, jnp.zeros((C, NX, ZP, NY), jnp.float32), (levels, mode_count))
    return (total / MEMBERS).astype(jnp.bfloat16)
```

```python
import math

import jax
import jax.numpy as jnp
from jax import lax
from jax.sharding import PartitionSpec as P

TWO_PI = 2.0 * math.pi


def phases(frequency, positions, length):
    product = frequency[:, None] * positions[None, :] % length
    angles = product.astype(jnp.float32) * (TWO_PI / length)
    return (jnp.cos(angles), jnp.sin(angles))


def forward_x(pencil, cos_table, sin_table):
    row_total = pencil.shape[0]
    modes = cos_table.shape[0]
    with_cos = jnp.einsum(
        "kxf,mx->kmf", pencil, cos_table, preferred_element_type=jnp.float32
    ).reshape(row_total, modes, 2, -1)
    with_sin = jnp.einsum(
        "kxf,mx->kmf", pencil, sin_table, preferred_element_type=jnp.float32
    ).reshape(row_total, modes, 2, -1)
    real_part = with_cos[:, :, 0] + with_sin[:, :, 1]
    imag_part = with_cos[:, :, 1] - with_sin[:, :, 0]
    return jnp.stack([real_part, imag_part], axis=2).reshape(row_total, modes, -1)


def inverse_x(spectra, cos_table, sin_table):
    row_total = spectra.shape[0]
    points = cos_table.shape[1]
    with_cos = jnp.einsum(
        "kmf,mx->kxf", spectra, cos_table, preferred_element_type=jnp.float32
    ).reshape(row_total, points, 2, -1)
    with_sin = jnp.einsum(
        "kmf,mx->kxf", spectra, sin_table, preferred_element_type=jnp.float32
    ).reshape(row_total, points, 2, -1)
    real_part = with_cos[:, :, 0] - with_sin[:, :, 1]
    imag_part = with_cos[:, :, 1] + with_sin[:, :, 0]
    return jnp.stack([real_part, imag_part], axis=2).reshape(row_total, points, -1)


def mixing(weights, values):
    return jnp.einsum("kmoi,kmiz->kmoz", weights, values, preferred_element_type=jnp.float32)


def local(
    base_field,
    forcing,
    load,
    amplitudes,
    amp_index,
    mode_count,
    point_weight,
    point_bias,
    spectral_weight,
):
    channels, slab_rows, plane_count, length_y = base_field.shape
    slab_count = lax.axis_size("slab")
    local_modes = spectral_weight.shape[0]
    modes_y = local_modes * slab_count
    modes_x = spectral_weight.shape[1]
    length_x = slab_rows * slab_count
    packed_width = 2 * channels * plane_count
    slab_index = lax.axis_index("slab")
    level_ids = jnp.arange(amplitudes.shape[0], dtype=jnp.int32)
    amplitude = jnp.sum(jnp.where(level_ids == amp_index[0], amplitudes, 0.0))
    driven = base_field.astype(jnp.float32) + amplitude * load[:, None, None, None] * forcing[
        None
    ].astype(jnp.float32)
    field_now = (2.0 * jnp.tanh(0.5 * driven)).astype(jnp.bfloat16)
    y_cos, y_sin = phases(
        jnp.arange(modes_y, dtype=jnp.int32), jnp.arange(length_y, dtype=jnp.int32), length_y
    )
    y_real = jnp.einsum(
        "cxzy,ky->kxcz", field_now, y_cos.astype(jnp.bfloat16), preferred_element_type=jnp.float32
    )
    y_imag = -jnp.einsum(
        "cxzy,ky->kxcz", field_now, y_sin.astype(jnp.bfloat16), preferred_element_type=jnp.float32
    )
    packed = (
        jnp.stack([y_real, y_imag], axis=2)
        .astype(jnp.bfloat16)
        .reshape(modes_y, slab_rows, packed_width)
    )
    frequency_x = jnp.concatenate(
        [
            jnp.arange(modes_x // 2, dtype=jnp.int32),
            jnp.arange(length_x - modes_x // 2, length_x, dtype=jnp.int32),
        ]
    )
    full_cos, full_sin = phases(frequency_x, jnp.arange(length_x, dtype=jnp.int32), length_x)
    full_cos = full_cos.astype(jnp.bfloat16)
    full_sin = full_sin.astype(jnp.bfloat16)
    gathered = lax.all_to_all(packed, "slab", 0, 1, tiled=True)
    spectrum = forward_x(gathered, full_cos, full_sin)
    spectrum = spectrum.astype(jnp.bfloat16).reshape(local_modes, modes_x, 2, channels, plane_count)
    weight_real = spectral_weight[:, :, 0]
    weight_imag = spectral_weight[:, :, 1]
    spec_real = spectrum[:, :, 0]
    spec_imag = spectrum[:, :, 1]
    mix_real = mixing(weight_real, spec_real) - mixing(weight_imag, spec_imag)
    mix_imag = mixing(weight_real, spec_imag) + mixing(weight_imag, spec_real)
    global_modes = slab_index * local_modes + jnp.arange(local_modes, dtype=jnp.int32)
    keep = (global_modes < mode_count[0]).astype(jnp.float32)[:, None, None, None, None]
    mixed = (
        (jnp.stack([mix_real, mix_imag], axis=2) * keep)
        .astype(jnp.bfloat16)
        .reshape(local_modes, modes_x, packed_width)
    )
    returned = inverse_x(mixed, full_cos, full_sin).astype(jnp.bfloat16)
    returned = lax.all_to_all(returned, "slab", 1, 0, tiled=True)
    returned = returned.reshape(modes_y, slab_rows, 2, channels, plane_count)
    weights_y = jnp.where(jnp.arange(modes_y) == 0, 1.0, 2.0).astype(jnp.float32) / (
        length_x * length_y
    )
    back_cos = (weights_y[:, None] * y_cos).astype(jnp.bfloat16)
    back_sin = (weights_y[:, None] * y_sin).astype(jnp.bfloat16)
    spectral = jnp.einsum(
        "kxcz,ky->cxzy", returned[:, :, 0], back_cos, preferred_element_type=jnp.float32
    )
    spectral = spectral - jnp.einsum(
        "kxcz,ky->cxzy", returned[:, :, 1], back_sin, preferred_element_type=jnp.float32
    )
    pointwise = (
        jnp.einsum("oc,cxzy->oxzy", point_weight, field_now, preferred_element_type=jnp.float32)
        + point_bias[:, None, None, None]
    )
    layer = jax.nn.gelu(pointwise + spectral, approximate=True).astype(jnp.bfloat16)
    layer = lax.optimization_barrier(layer).astype(jnp.float32)
    total = lax.psum_scatter(
        layer.astype(jnp.bfloat16), "member", scatter_dimension=0, tiled=True
    ).astype(jnp.float32)
    return (total / lax.axis_size("member")).astype(jnp.bfloat16)


def solution(mesh):
    in_specs = (
        P(None, "slab", None, None),
        P("slab", None, None),
        P(),
        P(),
        P("member"),
        P("member"),
        P(),
        P(),
        P("slab", None, None, None, None),
    )
    out_specs = P("member", "slab", None, None)
    return jax.shard_map(local, mesh=mesh, in_specs=in_specs, out_specs=out_specs, check_vma=False)
```

```python
import functools
import math

import jax
import jax.numpy as jnp
from jax import lax
from jax.experimental import pallas as pl
from jax.experimental.pallas import tpu as pltpu
from jax.sharding import PartitionSpec as P

TWO_PI = 2.0 * math.pi


def phases(frequency, positions, length):
    product = frequency[:, None] * positions[None, :] % length
    angles = product.astype(jnp.float32) * (TWO_PI / length)
    return (jnp.cos(angles), jnp.sin(angles))


def forward_x(pencil, cos_table, sin_table):
    row_total = pencil.shape[0]
    modes = cos_table.shape[0]
    with_cos = jnp.einsum(
        "kxf,mx->kmf", pencil, cos_table, preferred_element_type=jnp.float32
    ).reshape(row_total, modes, 2, -1)
    with_sin = jnp.einsum(
        "kxf,mx->kmf", pencil, sin_table, preferred_element_type=jnp.float32
    ).reshape(row_total, modes, 2, -1)
    real_part = with_cos[:, :, 0] + with_sin[:, :, 1]
    imag_part = with_cos[:, :, 1] - with_sin[:, :, 0]
    return jnp.stack([real_part, imag_part], axis=2).reshape(row_total, modes, -1)


def inverse_x(spectra, cos_table, sin_table):
    row_total = spectra.shape[0]
    points = cos_table.shape[1]
    with_cos = jnp.einsum(
        "kmf,mx->kxf", spectra, cos_table, preferred_element_type=jnp.float32
    ).reshape(row_total, points, 2, -1)
    with_sin = jnp.einsum(
        "kmf,mx->kxf", spectra, sin_table, preferred_element_type=jnp.float32
    ).reshape(row_total, points, 2, -1)
    real_part = with_cos[:, :, 0] - with_sin[:, :, 1]
    imag_part = with_cos[:, :, 1] + with_sin[:, :, 0]
    return jnp.stack([real_part, imag_part], axis=2).reshape(row_total, points, -1)


def mixing(weights, values):
    return jnp.einsum("kmoi,kmiz->kmoz", weights, values, preferred_element_type=jnp.float32)


def member_sum_kernel(members, layer_ref, out_ref, landed, send_sems, recv_sems):
    me = lax.axis_index("member")
    slab = lax.axis_index("slab")
    barrier = pltpu.get_barrier_semaphore()
    for step in range(1, members):
        peer = lax.rem(me + step, members)
        pl.semaphore_signal(barrier, inc=1, device_id=(peer, slab), device_id_type=pl.DeviceIdType.MESH)
    pl.semaphore_wait(barrier, members - 1)
    copies = []
    for step in range(1, members):
        peer = lax.rem(me + step, members)
        copy = pltpu.make_async_remote_copy(
            src_ref=layer_ref.at[peer],
            dst_ref=landed.at[me],
            send_sem=send_sems.at[peer],
            recv_sem=recv_sems.at[me],
            device_id=(peer, slab),
            device_id_type=pl.DeviceIdType.MESH,
        )
        copy.start()
        copies.append(copy)
    total = layer_ref[me].astype(jnp.float32)
    for step in range(1, members):
        source = lax.rem(me + members - step, members)
        arrival = pltpu.make_async_remote_copy(
            src_ref=layer_ref.at[source],
            dst_ref=landed.at[source],
            send_sem=send_sems.at[source],
            recv_sem=recv_sems.at[source],
            device_id=(source, slab),
            device_id_type=pl.DeviceIdType.MESH,
        )
        arrival.wait_recv()
        total = total + landed[source].astype(jnp.float32)
    for copy in copies:
        copy.wait_send()
    out_ref[...] = (total / members).astype(out_ref.dtype)


def member_sum(layer, members):
    block_rows, width = layer.shape[1], layer.shape[2]
    return pl.pallas_call(
        functools.partial(member_sum_kernel, members),
        out_shape=jax.ShapeDtypeStruct((block_rows, width), jnp.bfloat16),
        in_specs=[pl.BlockSpec(memory_space=pltpu.VMEM)],
        out_specs=pl.BlockSpec(memory_space=pltpu.VMEM),
        scratch_shapes=[
            pltpu.VMEM((members, block_rows, width), jnp.bfloat16),
            pltpu.SemaphoreType.DMA((members,)),
            pltpu.SemaphoreType.DMA((members,)),
        ],
        compiler_params=pltpu.CompilerParams(collective_id=0, has_side_effects=True),
    )(layer)


def local(
    base_field,
    forcing,
    load,
    amplitudes,
    amp_index,
    mode_count,
    point_weight,
    point_bias,
    spectral_weight,
):
    channels, slab_rows, plane_count, length_y = base_field.shape
    slab_count = lax.axis_size("slab")
    local_modes = spectral_weight.shape[0]
    modes_y = local_modes * slab_count
    modes_x = spectral_weight.shape[1]
    length_x = slab_rows * slab_count
    packed_width = 2 * channels * plane_count
    slab_index = lax.axis_index("slab")
    level_ids = jnp.arange(amplitudes.shape[0], dtype=jnp.int32)
    amplitude = jnp.sum(jnp.where(level_ids == amp_index[0], amplitudes, 0.0))
    driven = base_field.astype(jnp.float32) + amplitude * load[:, None, None, None] * forcing[
        None
    ].astype(jnp.float32)
    field_now = (2.0 * jnp.tanh(0.5 * driven)).astype(jnp.bfloat16)
    y_cos, y_sin = phases(
        jnp.arange(modes_y, dtype=jnp.int32), jnp.arange(length_y, dtype=jnp.int32), length_y
    )
    y_real = jnp.einsum(
        "cxzy,ky->kxcz", field_now, y_cos.astype(jnp.bfloat16), preferred_element_type=jnp.float32
    )
    y_imag = -jnp.einsum(
        "cxzy,ky->kxcz", field_now, y_sin.astype(jnp.bfloat16), preferred_element_type=jnp.float32
    )
    packed = (
        jnp.stack([y_real, y_imag], axis=2)
        .astype(jnp.bfloat16)
        .reshape(modes_y, slab_rows, packed_width)
    )
    frequency_x = jnp.concatenate(
        [
            jnp.arange(modes_x // 2, dtype=jnp.int32),
            jnp.arange(length_x - modes_x // 2, length_x, dtype=jnp.int32),
        ]
    )
    full_cos, full_sin = phases(frequency_x, jnp.arange(length_x, dtype=jnp.int32), length_x)
    full_cos = full_cos.astype(jnp.bfloat16)
    full_sin = full_sin.astype(jnp.bfloat16)
    gathered = lax.all_to_all(packed, "slab", 0, 1, tiled=True)
    spectrum = forward_x(gathered, full_cos, full_sin)
    spectrum = spectrum.astype(jnp.bfloat16).reshape(local_modes, modes_x, 2, channels, plane_count)
    weight_real = spectral_weight[:, :, 0]
    weight_imag = spectral_weight[:, :, 1]
    spec_real = spectrum[:, :, 0]
    spec_imag = spectrum[:, :, 1]
    mix_real = mixing(weight_real, spec_real) - mixing(weight_imag, spec_imag)
    mix_imag = mixing(weight_real, spec_imag) + mixing(weight_imag, spec_real)
    global_modes = slab_index * local_modes + jnp.arange(local_modes, dtype=jnp.int32)
    keep = (global_modes < mode_count[0]).astype(jnp.float32)[:, None, None, None, None]
    mixed = (
        (jnp.stack([mix_real, mix_imag], axis=2) * keep)
        .astype(jnp.bfloat16)
        .reshape(local_modes, modes_x, packed_width)
    )
    returned = inverse_x(mixed, full_cos, full_sin).astype(jnp.bfloat16)
    returned = lax.all_to_all(returned, "slab", 1, 0, tiled=True)
    returned = returned.reshape(modes_y, slab_rows, 2, channels, plane_count)
    weights_y = jnp.where(jnp.arange(modes_y) == 0, 1.0, 2.0).astype(jnp.float32) / (
        length_x * length_y
    )
    back_cos = (weights_y[:, None] * y_cos).astype(jnp.bfloat16)
    back_sin = (weights_y[:, None] * y_sin).astype(jnp.bfloat16)
    spectral = jnp.einsum(
        "kxcz,ky->cxzy", returned[:, :, 0], back_cos, preferred_element_type=jnp.float32
    )
    spectral = spectral - jnp.einsum(
        "kxcz,ky->cxzy", returned[:, :, 1], back_sin, preferred_element_type=jnp.float32
    )
    pointwise = (
        jnp.einsum("oc,cxzy->oxzy", point_weight, field_now, preferred_element_type=jnp.float32)
        + point_bias[:, None, None, None]
    )
    layer = jax.nn.gelu(pointwise + spectral, approximate=True).astype(jnp.bfloat16)
    members = lax.axis_size("member")
    blocks = layer.reshape(members, -1, length_y)
    total = member_sum(blocks, members)
    return total.reshape(channels // members, slab_rows, plane_count, length_y)


def solution(mesh):
    in_specs = (
        P(None, "slab", None, None),
        P("slab", None, None),
        P(),
        P(),
        P("member"),
        P("member"),
        P(),
        P(),
        P("slab", None, None, None, None),
    )
    out_specs = P("member", "slab", None, None)
    return jax.shard_map(local, mesh=mesh, in_specs=in_specs, out_specs=out_specs, check_vma=False)
```

```python
import functools
import math

import jax
import jax.numpy as jnp
from jax import lax
from jax.experimental import pallas as pl
from jax.experimental.pallas import tpu as pltpu
from jax.sharding import PartitionSpec as P

TWO_PI = 2.0 * math.pi


def phases(frequency, positions, length):
    product = frequency[:, None] * positions[None, :] % length
    angles = product.astype(jnp.float32) * (TWO_PI / length)
    return (jnp.cos(angles), jnp.sin(angles))


def forward_x(pencil, cos_table, sin_table):
    row_total = pencil.shape[0]
    modes = cos_table.shape[0]
    with_cos = jnp.einsum(
        "kxf,mx->kmf", pencil, cos_table, preferred_element_type=jnp.float32
    ).reshape(row_total, modes, 2, -1)
    with_sin = jnp.einsum(
        "kxf,mx->kmf", pencil, sin_table, preferred_element_type=jnp.float32
    ).reshape(row_total, modes, 2, -1)
    real_part = with_cos[:, :, 0] + with_sin[:, :, 1]
    imag_part = with_cos[:, :, 1] - with_sin[:, :, 0]
    return jnp.stack([real_part, imag_part], axis=2).reshape(row_total, modes, -1)


def inverse_x(spectra, cos_table, sin_table):
    row_total = spectra.shape[0]
    points = cos_table.shape[1]
    with_cos = jnp.einsum(
        "kmf,mx->kxf", spectra, cos_table, preferred_element_type=jnp.float32
    ).reshape(row_total, points, 2, -1)
    with_sin = jnp.einsum(
        "kmf,mx->kxf", spectra, sin_table, preferred_element_type=jnp.float32
    ).reshape(row_total, points, 2, -1)
    real_part = with_cos[:, :, 0] - with_sin[:, :, 1]
    imag_part = with_cos[:, :, 1] + with_sin[:, :, 0]
    return jnp.stack([real_part, imag_part], axis=2).reshape(row_total, points, -1)


def mixing(weights, values):
    return jnp.einsum("kmoi,kmiz->kmoz", weights, values, preferred_element_type=jnp.float32)


def member_sum_kernel(members, layer_ref, out_ref, landed, send_sems, recv_sems):
    me = lax.axis_index("member")
    slab = lax.axis_index("slab")
    barrier = pltpu.get_barrier_semaphore()
    for step in range(1, members):
        peer = lax.rem(me + step, members)
        pl.semaphore_signal(barrier, inc=1, device_id=(peer, slab), device_id_type=pl.DeviceIdType.MESH)
    pl.semaphore_wait(barrier, members - 1)
    copies = []
    for step in range(1, members):
        peer = lax.rem(me + step, members)
        copy = pltpu.make_async_remote_copy(
            src_ref=layer_ref.at[peer],
            dst_ref=landed.at[me],
            send_sem=send_sems.at[peer],
            recv_sem=recv_sems.at[me],
            device_id=(peer, slab),
            device_id_type=pl.DeviceIdType.MESH,
        )
        copy.start()
        copies.append(copy)
    total = layer_ref[me].astype(jnp.float32)
    for step in range(1, members):
        source = lax.rem(me + members - step, members)
        arrival = pltpu.make_async_remote_copy(
            src_ref=layer_ref.at[source],
            dst_ref=landed.at[source],
            send_sem=send_sems.at[source],
            recv_sem=recv_sems.at[source],
            device_id=(source, slab),
            device_id_type=pl.DeviceIdType.MESH,
        )
        arrival.wait_recv()
        total = total + landed[source].astype(jnp.float32)
    for copy in copies:
        copy.wait_send()
    out_ref[...] = (total / members).astype(out_ref.dtype)


def member_sum(layer, members):
    block_rows, width = layer.shape[1], layer.shape[2]
    return pl.pallas_call(
        functools.partial(member_sum_kernel, members),
        out_shape=jax.ShapeDtypeStruct((block_rows, width), jnp.bfloat16),
        in_specs=[pl.BlockSpec(memory_space=pltpu.VMEM)],
        out_specs=pl.BlockSpec(memory_space=pltpu.VMEM),
        scratch_shapes=[
            pltpu.VMEM((members, block_rows, width), jnp.bfloat16),
            pltpu.SemaphoreType.DMA((members,)),
            pltpu.SemaphoreType.DMA((members,)),
        ],
        compiler_params=pltpu.CompilerParams(collective_id=0, has_side_effects=True),
    )(layer)


def slab_exchange_kernel(parts, blocks_ref, out_ref, landed, send_sems, recv_sems):
    me = lax.axis_index("slab")
    member = lax.axis_index("member")
    barrier = pltpu.get_barrier_semaphore()

    def greet(step, carry):
        peer = lax.rem(me + step, parts)
        pl.semaphore_signal(barrier, inc=1, device_id=(member, peer), device_id_type=pl.DeviceIdType.MESH)
        return carry

    lax.fori_loop(1, parts, greet, 0)
    pl.semaphore_wait(barrier, parts - 1)

    def send(step, carry):
        peer = lax.rem(me + step, parts)
        pltpu.make_async_remote_copy(
            src_ref=blocks_ref.at[peer],
            dst_ref=landed.at[me],
            send_sem=send_sems.at[peer],
            recv_sem=recv_sems.at[me],
            device_id=(member, peer),
            device_id_type=pl.DeviceIdType.MESH,
        ).start()
        return carry

    lax.fori_loop(1, parts, send, 0)
    landed[me] = blocks_ref[me]

    def receive(step, carry):
        source = lax.rem(me + parts - step, parts)
        pltpu.make_async_remote_copy(
            src_ref=blocks_ref.at[source],
            dst_ref=landed.at[source],
            send_sem=send_sems.at[source],
            recv_sem=recv_sems.at[source],
            device_id=(member, source),
            device_id_type=pl.DeviceIdType.MESH,
        ).wait_recv()
        return carry

    lax.fori_loop(1, parts, receive, 0)

    def sent(step, carry):
        peer = lax.rem(me + step, parts)
        pltpu.make_async_remote_copy(
            src_ref=blocks_ref.at[peer],
            dst_ref=landed.at[me],
            send_sem=send_sems.at[peer],
            recv_sem=recv_sems.at[me],
            device_id=(member, peer),
            device_id_type=pl.DeviceIdType.MESH,
        ).wait_send()
        return carry

    lax.fori_loop(1, parts, sent, 0)
    out_ref[...] = landed[...]


def slab_exchange(blocks, parts, exchange_id):
    return pl.pallas_call(
        functools.partial(slab_exchange_kernel, parts),
        out_shape=jax.ShapeDtypeStruct(blocks.shape, blocks.dtype),
        in_specs=[pl.BlockSpec(memory_space=pltpu.VMEM)],
        out_specs=pl.BlockSpec(memory_space=pltpu.VMEM),
        scratch_shapes=[
            pltpu.VMEM(blocks.shape, blocks.dtype),
            pltpu.SemaphoreType.DMA((parts,)),
            pltpu.SemaphoreType.DMA((parts,)),
        ],
        compiler_params=pltpu.CompilerParams(collective_id=exchange_id, has_side_effects=True),
    )(blocks)


def local(
    base_field,
    forcing,
    load,
    amplitudes,
    amp_index,
    mode_count,
    point_weight,
    point_bias,
    spectral_weight,
):
    channels, slab_rows, plane_count, length_y = base_field.shape
    slab_count = lax.axis_size("slab")
    local_modes = spectral_weight.shape[0]
    modes_y = local_modes * slab_count
    modes_x = spectral_weight.shape[1]
    length_x = slab_rows * slab_count
    packed_width = 2 * channels * plane_count
    slab_index = lax.axis_index("slab")
    level_ids = jnp.arange(amplitudes.shape[0], dtype=jnp.int32)
    amplitude = jnp.sum(jnp.where(level_ids == amp_index[0], amplitudes, 0.0))
    driven = base_field.astype(jnp.float32) + amplitude * load[:, None, None, None] * forcing[
        None
    ].astype(jnp.float32)
    field_now = (2.0 * jnp.tanh(0.5 * driven)).astype(jnp.bfloat16)
    y_cos, y_sin = phases(
        jnp.arange(modes_y, dtype=jnp.int32), jnp.arange(length_y, dtype=jnp.int32), length_y
    )
    y_real = jnp.einsum(
        "cxzy,ky->kxcz", field_now, y_cos.astype(jnp.bfloat16), preferred_element_type=jnp.float32
    )
    y_imag = -jnp.einsum(
        "cxzy,ky->kxcz", field_now, y_sin.astype(jnp.bfloat16), preferred_element_type=jnp.float32
    )
    packed = (
        jnp.stack([y_real, y_imag], axis=2)
        .astype(jnp.bfloat16)
        .reshape(modes_y, slab_rows, packed_width)
    )
    frequency_x = jnp.concatenate(
        [
            jnp.arange(modes_x // 2, dtype=jnp.int32),
            jnp.arange(length_x - modes_x // 2, length_x, dtype=jnp.int32),
        ]
    )
    full_cos, full_sin = phases(frequency_x, jnp.arange(length_x, dtype=jnp.int32), length_x)
    full_cos = full_cos.astype(jnp.bfloat16)
    full_sin = full_sin.astype(jnp.bfloat16)
    gathered = slab_exchange(packed, slab_count, 1).reshape(length_x, packed_width)[None]
    spectrum = forward_x(gathered, full_cos, full_sin)
    spectrum = spectrum.astype(jnp.bfloat16).reshape(local_modes, modes_x, 2, channels, plane_count)
    weight_real = spectral_weight[:, :, 0]
    weight_imag = spectral_weight[:, :, 1]
    spec_real = spectrum[:, :, 0]
    spec_imag = spectrum[:, :, 1]
    mix_real = mixing(weight_real, spec_real) - mixing(weight_imag, spec_imag)
    mix_imag = mixing(weight_real, spec_imag) + mixing(weight_imag, spec_real)
    global_modes = slab_index * local_modes + jnp.arange(local_modes, dtype=jnp.int32)
    keep = (global_modes < mode_count[0]).astype(jnp.float32)[:, None, None, None, None]
    mixed = (
        (jnp.stack([mix_real, mix_imag], axis=2) * keep)
        .astype(jnp.bfloat16)
        .reshape(local_modes, modes_x, packed_width)
    )
    returned = inverse_x(mixed, full_cos, full_sin).astype(jnp.bfloat16)
    returned = slab_exchange(returned.reshape(slab_count, slab_rows, packed_width), slab_count, 2)
    returned = returned.reshape(modes_y, slab_rows, 2, channels, plane_count)
    weights_y = jnp.where(jnp.arange(modes_y) == 0, 1.0, 2.0).astype(jnp.float32) / (
        length_x * length_y
    )
    back_cos = (weights_y[:, None] * y_cos).astype(jnp.bfloat16)
    back_sin = (weights_y[:, None] * y_sin).astype(jnp.bfloat16)
    spectral = jnp.einsum(
        "kxcz,ky->cxzy", returned[:, :, 0], back_cos, preferred_element_type=jnp.float32
    )
    spectral = spectral - jnp.einsum(
        "kxcz,ky->cxzy", returned[:, :, 1], back_sin, preferred_element_type=jnp.float32
    )
    pointwise = (
        jnp.einsum("oc,cxzy->oxzy", point_weight, field_now, preferred_element_type=jnp.float32)
        + point_bias[:, None, None, None]
    )
    layer = jax.nn.gelu(pointwise + spectral, approximate=True).astype(jnp.bfloat16)
    members = lax.axis_size("member")
    blocks = layer.reshape(members, -1, length_y)
    total = member_sum(blocks, members)
    return total.reshape(channels // members, slab_rows, plane_count, length_y)


def solution(mesh):
    in_specs = (
        P(None, "slab", None, None),
        P("slab", None, None),
        P(),
        P(),
        P("member"),
        P("member"),
        P(),
        P(),
        P("slab", None, None, None, None),
    )
    out_specs = P("member", "slab", None, None)
    return jax.shard_map(local, mesh=mesh, in_specs=in_specs, out_specs=out_specs, check_vma=False)
```

```python
import functools
import math

import jax
import jax.numpy as jnp
from jax import lax
from jax.experimental import pallas as pl
from jax.experimental.pallas import tpu as pltpu
from jax.sharding import PartitionSpec as P

TWO_PI = 2.0 * math.pi


def phases(frequency, positions, length):
    product = frequency[:, None] * positions[None, :] % length
    angles = product.astype(jnp.float32) * (TWO_PI / length)
    return (jnp.cos(angles), jnp.sin(angles))


def forward_x(pencil, cos_table, sin_table):
    row_total = pencil.shape[0]
    modes = cos_table.shape[0]
    with_cos = jnp.einsum(
        "kxf,mx->kmf", pencil, cos_table, preferred_element_type=jnp.float32
    ).reshape(row_total, modes, 2, -1)
    with_sin = jnp.einsum(
        "kxf,mx->kmf", pencil, sin_table, preferred_element_type=jnp.float32
    ).reshape(row_total, modes, 2, -1)
    real_part = with_cos[:, :, 0] + with_sin[:, :, 1]
    imag_part = with_cos[:, :, 1] - with_sin[:, :, 0]
    return jnp.stack([real_part, imag_part], axis=2).reshape(row_total, modes, -1)


def inverse_x(spectra, cos_table, sin_table):
    row_total = spectra.shape[0]
    points = cos_table.shape[1]
    with_cos = jnp.einsum(
        "kmf,mx->kxf", spectra, cos_table, preferred_element_type=jnp.float32
    ).reshape(row_total, points, 2, -1)
    with_sin = jnp.einsum(
        "kmf,mx->kxf", spectra, sin_table, preferred_element_type=jnp.float32
    ).reshape(row_total, points, 2, -1)
    real_part = with_cos[:, :, 0] - with_sin[:, :, 1]
    imag_part = with_cos[:, :, 1] + with_sin[:, :, 0]
    return jnp.stack([real_part, imag_part], axis=2).reshape(row_total, points, -1)


def mixing(weights, values):
    return jnp.einsum("kmoi,kmiz->kmoz", weights, values, preferred_element_type=jnp.float32)


def member_sum_kernel(members, layer_ref, out_ref, landed, send_sems, recv_sems):
    me = lax.axis_index("member")
    slab = lax.axis_index("slab")
    barrier = pltpu.get_barrier_semaphore()
    for step in range(1, members):
        peer = lax.rem(me + step, members)
        pl.semaphore_signal(barrier, inc=1, device_id=(peer, slab), device_id_type=pl.DeviceIdType.MESH)
    pl.semaphore_wait(barrier, members - 1)
    copies = []
    for step in range(1, members):
        peer = lax.rem(me + step, members)
        copy = pltpu.make_async_remote_copy(
            src_ref=layer_ref.at[peer],
            dst_ref=landed.at[me],
            send_sem=send_sems.at[peer],
            recv_sem=recv_sems.at[me],
            device_id=(peer, slab),
            device_id_type=pl.DeviceIdType.MESH,
        )
        copy.start()
        copies.append(copy)
    total = layer_ref[me].astype(jnp.float32)
    for step in range(1, members):
        source = lax.rem(me + members - step, members)
        arrival = pltpu.make_async_remote_copy(
            src_ref=layer_ref.at[source],
            dst_ref=landed.at[source],
            send_sem=send_sems.at[source],
            recv_sem=recv_sems.at[source],
            device_id=(source, slab),
            device_id_type=pl.DeviceIdType.MESH,
        )
        arrival.wait_recv()
        total = total + landed[source].astype(jnp.float32)
    for copy in copies:
        copy.wait_send()
    out_ref[...] = (total / members).astype(out_ref.dtype)


def member_sum(layer, members):
    block_rows, width = layer.shape[1], layer.shape[2]
    return pl.pallas_call(
        functools.partial(member_sum_kernel, members),
        out_shape=jax.ShapeDtypeStruct((block_rows, width), jnp.bfloat16),
        in_specs=[pl.BlockSpec(memory_space=pltpu.VMEM)],
        out_specs=pl.BlockSpec(memory_space=pltpu.VMEM),
        scratch_shapes=[
            pltpu.VMEM((members, block_rows, width), jnp.bfloat16),
            pltpu.SemaphoreType.DMA((members,)),
            pltpu.SemaphoreType.DMA((members,)),
        ],
        compiler_params=pltpu.CompilerParams(collective_id=0, has_side_effects=True),
    )(layer)


def slab_exchange_kernel(outer, inner, blocks_ref, out_ref, middle, landed, first_send, first_recv,
                         second_send, second_recv, own_sems):
    me = lax.axis_index("slab")
    member = lax.axis_index("member")
    row, col = me // inner, me % inner
    mesh_kind = pl.DeviceIdType.MESH
    barrier = pltpu.get_barrier_semaphore()
    for step in range(1, inner):
        peer = row * inner + lax.rem(col + step, inner)
        pl.semaphore_signal(barrier, inc=1, device_id=(member, peer), device_id_type=mesh_kind)
    for step in range(1, outer):
        peer = lax.rem(row + step, outer) * inner + col
        pl.semaphore_signal(barrier, inc=1, device_id=(member, peer), device_id_type=mesh_kind)
    pl.semaphore_wait(barrier, inner + outer - 2)

    def first_copy(other):
        return pltpu.make_async_remote_copy(
            src_ref=blocks_ref.at[:, other],
            dst_ref=middle.at[col],
            send_sem=first_send.at[other],
            recv_sem=first_recv.at[col],
            device_id=(member, row * inner + other),
            device_id_type=mesh_kind,
        )

    def first_arrival(other):
        return pltpu.make_async_remote_copy(
            src_ref=blocks_ref.at[:, col],
            dst_ref=middle.at[other],
            send_sem=first_send.at[other],
            recv_sem=first_recv.at[other],
            device_id=(member, row * inner + other),
            device_id_type=mesh_kind,
        )

    for step in range(1, inner):
        first_copy(lax.rem(col + step, inner)).start()
    own_first = pltpu.make_async_copy(blocks_ref.at[:, col], middle.at[col], own_sems.at[0])
    own_first.start()
    own_first.wait()
    for step in range(1, inner):
        first_arrival(lax.rem(col + inner - step, inner)).wait_recv()
    for step in range(1, inner):
        first_copy(lax.rem(col + step, inner)).wait_send()

    def second_copy(other):
        return pltpu.make_async_remote_copy(
            src_ref=middle.at[:, other],
            dst_ref=landed.at[row],
            send_sem=second_send.at[other],
            recv_sem=second_recv.at[row],
            device_id=(member, other * inner + col),
            device_id_type=mesh_kind,
        )

    def second_arrival(other):
        return pltpu.make_async_remote_copy(
            src_ref=middle.at[:, row],
            dst_ref=landed.at[other],
            send_sem=second_send.at[other],
            recv_sem=second_recv.at[other],
            device_id=(member, other * inner + col),
            device_id_type=mesh_kind,
        )

    for step in range(1, outer):
        second_copy(lax.rem(row + step, outer)).start()
    own_second = pltpu.make_async_copy(middle.at[:, row], landed.at[row], own_sems.at[1])
    own_second.start()
    own_second.wait()
    for step in range(1, outer):
        second_arrival(lax.rem(row + outer - step, outer)).wait_recv()
    for step in range(1, outer):
        second_copy(lax.rem(row + step, outer)).wait_send()
    out_ref[...] = landed[...]


def slab_exchange(blocks, parts, exchange_id):
    inner = 8 if parts % 8 == 0 else 1
    outer = parts // inner
    rows, width = blocks.shape[1], blocks.shape[2]
    grid_blocks = blocks.reshape(outer, inner, rows, width)
    result = pl.pallas_call(
        functools.partial(slab_exchange_kernel, outer, inner),
        out_shape=jax.ShapeDtypeStruct((outer, inner, rows, width), blocks.dtype),
        in_specs=[pl.BlockSpec(memory_space=pltpu.VMEM)],
        out_specs=pl.BlockSpec(memory_space=pltpu.VMEM),
        scratch_shapes=[
            pltpu.VMEM((inner, outer, rows, width), blocks.dtype),
            pltpu.VMEM((outer, inner, rows, width), blocks.dtype),
            pltpu.SemaphoreType.DMA((inner,)),
            pltpu.SemaphoreType.DMA((inner,)),
            pltpu.SemaphoreType.DMA((outer,)),
            pltpu.SemaphoreType.DMA((outer,)),
            pltpu.SemaphoreType.DMA((2,)),
        ],
        compiler_params=pltpu.CompilerParams(collective_id=exchange_id, has_side_effects=True),
    )(grid_blocks)
    return result.reshape(parts, rows, width)


def local(
    base_field,
    forcing,
    load,
    amplitudes,
    amp_index,
    mode_count,
    point_weight,
    point_bias,
    spectral_weight,
):
    channels, slab_rows, plane_count, length_y = base_field.shape
    slab_count = lax.axis_size("slab")
    local_modes = spectral_weight.shape[0]
    modes_y = local_modes * slab_count
    modes_x = spectral_weight.shape[1]
    length_x = slab_rows * slab_count
    packed_width = 2 * channels * plane_count
    slab_index = lax.axis_index("slab")
    level_ids = jnp.arange(amplitudes.shape[0], dtype=jnp.int32)
    amplitude = jnp.sum(jnp.where(level_ids == amp_index[0], amplitudes, 0.0))
    driven = base_field.astype(jnp.float32) + amplitude * load[:, None, None, None] * forcing[
        None
    ].astype(jnp.float32)
    field_now = (2.0 * jnp.tanh(0.5 * driven)).astype(jnp.bfloat16)
    y_cos, y_sin = phases(
        jnp.arange(modes_y, dtype=jnp.int32), jnp.arange(length_y, dtype=jnp.int32), length_y
    )
    y_real = jnp.einsum(
        "cxzy,ky->kxcz", field_now, y_cos.astype(jnp.bfloat16), preferred_element_type=jnp.float32
    )
    y_imag = -jnp.einsum(
        "cxzy,ky->kxcz", field_now, y_sin.astype(jnp.bfloat16), preferred_element_type=jnp.float32
    )
    packed = (
        jnp.stack([y_real, y_imag], axis=2)
        .astype(jnp.bfloat16)
        .reshape(modes_y, slab_rows, packed_width)
    )
    frequency_x = jnp.concatenate(
        [
            jnp.arange(modes_x // 2, dtype=jnp.int32),
            jnp.arange(length_x - modes_x // 2, length_x, dtype=jnp.int32),
        ]
    )
    full_cos, full_sin = phases(frequency_x, jnp.arange(length_x, dtype=jnp.int32), length_x)
    full_cos = full_cos.astype(jnp.bfloat16)
    full_sin = full_sin.astype(jnp.bfloat16)
    gathered = slab_exchange(packed, slab_count, 1).reshape(length_x, packed_width)[None]
    spectrum = forward_x(gathered, full_cos, full_sin)
    spectrum = spectrum.astype(jnp.bfloat16).reshape(local_modes, modes_x, 2, channels, plane_count)
    weight_real = spectral_weight[:, :, 0]
    weight_imag = spectral_weight[:, :, 1]
    spec_real = spectrum[:, :, 0]
    spec_imag = spectrum[:, :, 1]
    mix_real = mixing(weight_real, spec_real) - mixing(weight_imag, spec_imag)
    mix_imag = mixing(weight_real, spec_imag) + mixing(weight_imag, spec_real)
    global_modes = slab_index * local_modes + jnp.arange(local_modes, dtype=jnp.int32)
    keep = (global_modes < mode_count[0]).astype(jnp.float32)[:, None, None, None, None]
    mixed = (
        (jnp.stack([mix_real, mix_imag], axis=2) * keep)
        .astype(jnp.bfloat16)
        .reshape(local_modes, modes_x, packed_width)
    )
    returned = inverse_x(mixed, full_cos, full_sin).astype(jnp.bfloat16)
    returned = slab_exchange(returned.reshape(slab_count, slab_rows, packed_width), slab_count, 2)
    returned = returned.reshape(modes_y, slab_rows, 2, channels, plane_count)
    weights_y = jnp.where(jnp.arange(modes_y) == 0, 1.0, 2.0).astype(jnp.float32) / (
        length_x * length_y
    )
    back_cos = (weights_y[:, None] * y_cos).astype(jnp.bfloat16)
    back_sin = (weights_y[:, None] * y_sin).astype(jnp.bfloat16)
    spectral = jnp.einsum(
        "kxcz,ky->cxzy", returned[:, :, 0], back_cos, preferred_element_type=jnp.float32
    )
    spectral = spectral - jnp.einsum(
        "kxcz,ky->cxzy", returned[:, :, 1], back_sin, preferred_element_type=jnp.float32
    )
    pointwise = (
        jnp.einsum("oc,cxzy->oxzy", point_weight, field_now, preferred_element_type=jnp.float32)
        + point_bias[:, None, None, None]
    )
    layer = jax.nn.gelu(pointwise + spectral, approximate=True).astype(jnp.bfloat16)
    members = lax.axis_size("member")
    blocks = layer.reshape(members, -1, length_y)
    total = member_sum(blocks, members)
    return total.reshape(channels // members, slab_rows, plane_count, length_y)


def solution(mesh):
    in_specs = (
        P(None, "slab", None, None),
        P("slab", None, None),
        P(),
        P(),
        P("member"),
        P("member"),
        P(),
        P(),
        P("slab", None, None, None, None),
    )
    out_specs = P("member", "slab", None, None)
    return jax.shard_map(local, mesh=mesh, in_specs=in_specs, out_specs=out_specs, check_vma=False)
```

```python
import functools
import math

import jax
import jax.numpy as jnp
from jax import lax
from jax.experimental import pallas as pl
from jax.experimental.pallas import tpu as pltpu
from jax.sharding import PartitionSpec as P

TWO_PI = 2.0 * math.pi


def phases(frequency, positions, length):
    product = frequency[:, None] * positions[None, :] % length
    angles = product.astype(jnp.float32) * (TWO_PI / length)
    return (jnp.cos(angles), jnp.sin(angles))


def forward_x(pencil, cos_table, sin_table):
    row_total = pencil.shape[0]
    modes = cos_table.shape[0]
    with_cos = jnp.einsum(
        "kxf,mx->kmf", pencil, cos_table, preferred_element_type=jnp.float32
    ).reshape(row_total, modes, 2, -1)
    with_sin = jnp.einsum(
        "kxf,mx->kmf", pencil, sin_table, preferred_element_type=jnp.float32
    ).reshape(row_total, modes, 2, -1)
    real_part = with_cos[:, :, 0] + with_sin[:, :, 1]
    imag_part = with_cos[:, :, 1] - with_sin[:, :, 0]
    return jnp.stack([real_part, imag_part], axis=2).reshape(row_total, modes, -1)


def inverse_x(spectra, cos_table, sin_table):
    row_total = spectra.shape[0]
    points = cos_table.shape[1]
    with_cos = jnp.einsum(
        "kmf,mx->kxf", spectra, cos_table, preferred_element_type=jnp.float32
    ).reshape(row_total, points, 2, -1)
    with_sin = jnp.einsum(
        "kmf,mx->kxf", spectra, sin_table, preferred_element_type=jnp.float32
    ).reshape(row_total, points, 2, -1)
    real_part = with_cos[:, :, 0] - with_sin[:, :, 1]
    imag_part = with_cos[:, :, 1] + with_sin[:, :, 0]
    return jnp.stack([real_part, imag_part], axis=2).reshape(row_total, points, -1)


def mixing(weights, values):
    return jnp.einsum("kmoi,kmiz->kmoz", weights, values, preferred_element_type=jnp.float32)


def layer_sum_kernel(members, back_ref, table_ref, kron_ref, field_ref, bias_ref, out_ref, layer, landed,
                     send_sems, recv_sems):
    me = lax.axis_index("member")
    slab = lax.axis_index("slab")
    mesh_kind = pl.DeviceIdType.MESH
    barrier = pltpu.get_barrier_semaphore()
    for step in range(1, members):
        peer = lax.rem(me + step, members)
        pl.semaphore_signal(barrier, inc=1, device_id=(peer, slab), device_id_type=mesh_kind)
    spectral = jnp.dot(back_ref[...], table_ref[...], preferred_element_type=jnp.float32)
    pointwise = jnp.dot(kron_ref[...], field_ref[...], preferred_element_type=jnp.float32)
    value = jax.nn.gelu(pointwise + bias_ref[...] + spectral, approximate=True)
    layer[...] = value.astype(layer.dtype).reshape(layer.shape)
    pl.semaphore_wait(barrier, members - 1)

    def copy_of(source, target, peer):
        return pltpu.make_async_remote_copy(
            src_ref=layer.at[source],
            dst_ref=landed.at[target],
            send_sem=send_sems.at[source],
            recv_sem=recv_sems.at[target],
            device_id=(peer, slab),
            device_id_type=mesh_kind,
        )

    for step in range(1, members):
        peer = lax.rem(me + step, members)
        copy_of(peer, me, peer).start()
    total = layer[me].astype(jnp.float32)
    for step in range(1, members):
        source = lax.rem(me + members - step, members)
        copy_of(source, source, source).wait_recv()
        total = total + landed[source].astype(jnp.float32)
    for step in range(1, members):
        peer = lax.rem(me + step, members)
        copy_of(peer, me, peer).wait_send()
    out_ref[...] = (total / members).astype(out_ref.dtype)


def layer_sum(back, table, kron, field, bias, members):
    rows, width = field.shape
    block_rows = rows // members
    return pl.pallas_call(
        functools.partial(layer_sum_kernel, members),
        out_shape=jax.ShapeDtypeStruct((block_rows, width), jnp.bfloat16),
        in_specs=[pl.BlockSpec(memory_space=pltpu.VMEM)] * 5,
        out_specs=pl.BlockSpec(memory_space=pltpu.VMEM),
        scratch_shapes=[
            pltpu.VMEM((members, block_rows, width), jnp.bfloat16),
            pltpu.VMEM((members, block_rows, width), jnp.bfloat16),
            pltpu.SemaphoreType.DMA((members,)),
            pltpu.SemaphoreType.DMA((members,)),
        ],
        compiler_params=pltpu.CompilerParams(collective_id=0, has_side_effects=True),
    )(back, table, kron, field, bias)


def slab_exchange_kernel(parts, blocks_ref, out_ref, landed, send_sems, recv_sems):
    me = lax.axis_index("slab")
    member = lax.axis_index("member")
    barrier = pltpu.get_barrier_semaphore()

    def greet(step, carry):
        peer = lax.rem(me + step, parts)
        pl.semaphore_signal(barrier, inc=1, device_id=(member, peer), device_id_type=pl.DeviceIdType.MESH)
        return carry

    lax.fori_loop(1, parts, greet, 0)
    pl.semaphore_wait(barrier, parts - 1)

    def send(step, carry):
        peer = lax.rem(me + step, parts)
        pltpu.make_async_remote_copy(
            src_ref=blocks_ref.at[peer],
            dst_ref=landed.at[me],
            send_sem=send_sems.at[peer],
            recv_sem=recv_sems.at[me],
            device_id=(member, peer),
            device_id_type=pl.DeviceIdType.MESH,
        ).start()
        return carry

    lax.fori_loop(1, parts, send, 0)
    landed[me] = blocks_ref[me]

    def receive(step, carry):
        source = lax.rem(me + parts - step, parts)
        pltpu.make_async_remote_copy(
            src_ref=blocks_ref.at[source],
            dst_ref=landed.at[source],
            send_sem=send_sems.at[source],
            recv_sem=recv_sems.at[source],
            device_id=(member, source),
            device_id_type=pl.DeviceIdType.MESH,
        ).wait_recv()
        return carry

    lax.fori_loop(1, parts, receive, 0)

    def sent(step, carry):
        peer = lax.rem(me + step, parts)
        pltpu.make_async_remote_copy(
            src_ref=blocks_ref.at[peer],
            dst_ref=landed.at[me],
            send_sem=send_sems.at[peer],
            recv_sem=recv_sems.at[me],
            device_id=(member, peer),
            device_id_type=pl.DeviceIdType.MESH,
        ).wait_send()
        return carry

    lax.fori_loop(1, parts, sent, 0)
    out_ref[...] = landed[...]


def slab_exchange(blocks, parts, exchange_id):
    return pl.pallas_call(
        functools.partial(slab_exchange_kernel, parts),
        out_shape=jax.ShapeDtypeStruct(blocks.shape, blocks.dtype),
        in_specs=[pl.BlockSpec(memory_space=pltpu.VMEM)],
        out_specs=pl.BlockSpec(memory_space=pltpu.VMEM),
        scratch_shapes=[
            pltpu.VMEM(blocks.shape, blocks.dtype),
            pltpu.SemaphoreType.DMA((parts,)),
            pltpu.SemaphoreType.DMA((parts,)),
        ],
        compiler_params=pltpu.CompilerParams(collective_id=exchange_id, has_side_effects=True),
    )(blocks)


def local(
    base_field,
    forcing,
    load,
    amplitudes,
    amp_index,
    mode_count,
    point_weight,
    point_bias,
    spectral_weight,
):
    channels, slab_rows, plane_count, length_y = base_field.shape
    slab_count = lax.axis_size("slab")
    local_modes = spectral_weight.shape[0]
    modes_y = local_modes * slab_count
    modes_x = spectral_weight.shape[1]
    length_x = slab_rows * slab_count
    packed_width = 2 * channels * plane_count
    slab_index = lax.axis_index("slab")
    level_ids = jnp.arange(amplitudes.shape[0], dtype=jnp.int32)
    amplitude = jnp.sum(jnp.where(level_ids == amp_index[0], amplitudes, 0.0))
    driven = base_field.astype(jnp.float32) + amplitude * load[:, None, None, None] * forcing[
        None
    ].astype(jnp.float32)
    field_now = (2.0 * jnp.tanh(0.5 * driven)).astype(jnp.bfloat16)
    y_cos, y_sin = phases(
        jnp.arange(modes_y, dtype=jnp.int32), jnp.arange(length_y, dtype=jnp.int32), length_y
    )
    y_real = jnp.einsum(
        "cxzy,ky->kxcz", field_now, y_cos.astype(jnp.bfloat16), preferred_element_type=jnp.float32
    )
    y_imag = -jnp.einsum(
        "cxzy,ky->kxcz", field_now, y_sin.astype(jnp.bfloat16), preferred_element_type=jnp.float32
    )
    packed = (
        jnp.stack([y_real, y_imag], axis=2)
        .astype(jnp.bfloat16)
        .reshape(modes_y, slab_rows, packed_width)
    )
    frequency_x = jnp.concatenate(
        [
            jnp.arange(modes_x // 2, dtype=jnp.int32),
            jnp.arange(length_x - modes_x // 2, length_x, dtype=jnp.int32),
        ]
    )
    full_cos, full_sin = phases(frequency_x, jnp.arange(length_x, dtype=jnp.int32), length_x)
    full_cos = full_cos.astype(jnp.bfloat16)
    full_sin = full_sin.astype(jnp.bfloat16)
    gathered = slab_exchange(packed, slab_count, 1).reshape(length_x, packed_width)[None]
    spectrum = forward_x(gathered, full_cos, full_sin)
    spectrum = spectrum.astype(jnp.bfloat16).reshape(local_modes, modes_x, 2, channels, plane_count)
    weight_real = spectral_weight[:, :, 0]
    weight_imag = spectral_weight[:, :, 1]
    spec_real = spectrum[:, :, 0]
    spec_imag = spectrum[:, :, 1]
    mix_real = mixing(weight_real, spec_real) - mixing(weight_imag, spec_imag)
    mix_imag = mixing(weight_real, spec_imag) + mixing(weight_imag, spec_real)
    global_modes = slab_index * local_modes + jnp.arange(local_modes, dtype=jnp.int32)
    keep = (global_modes < mode_count[0]).astype(jnp.float32)[:, None, None, None, None]
    mixed = (
        (jnp.stack([mix_real, mix_imag], axis=2) * keep)
        .astype(jnp.bfloat16)
        .reshape(local_modes, modes_x, packed_width)
    )
    returned = inverse_x(mixed, full_cos, full_sin).astype(jnp.bfloat16)
    returned = slab_exchange(returned.reshape(slab_count, slab_rows, packed_width), slab_count, 2)
    returned = returned.reshape(modes_y, slab_rows, 2, channels, plane_count)
    weights_y = jnp.where(jnp.arange(modes_y) == 0, 1.0, 2.0).astype(jnp.float32) / (
        length_x * length_y
    )
    back_cos = (weights_y[:, None] * y_cos).astype(jnp.bfloat16)
    back_sin = (weights_y[:, None] * y_sin).astype(jnp.bfloat16)
    table = jnp.concatenate([back_cos, -back_sin], axis=0)
    rows = channels * slab_rows * plane_count
    back = returned.transpose(3, 1, 4, 2, 0).reshape(rows, 2 * modes_y)
    cells = slab_rows * plane_count
    kron = (
        point_weight[:, None, :, None] * jnp.eye(cells, dtype=point_weight.dtype)[None, :, None, :]
    ).reshape(rows, rows)
    bias = jnp.repeat(point_bias, cells).reshape(rows, 1)
    field_rows = field_now.reshape(rows, length_y)
    members = lax.axis_size("member")
    total = layer_sum(back, table, kron, field_rows, bias, members)
    return total.reshape(channels // members, slab_rows, plane_count, length_y)


def solution(mesh):
    in_specs = (
        P(None, "slab", None, None),
        P("slab", None, None),
        P(),
        P(),
        P("member"),
        P("member"),
        P(),
        P(),
        P("slab", None, None, None, None),
    )
    out_specs = P("member", "slab", None, None)
    return jax.shard_map(local, mesh=mesh, in_specs=in_specs, out_specs=out_specs, check_vma=False)
```

```python
import functools
import math

import jax
import jax.numpy as jnp
from jax import lax
from jax.experimental import pallas as pl
from jax.experimental.pallas import tpu as pltpu
from jax.sharding import PartitionSpec as P

TWO_PI = 2.0 * math.pi


def phases(frequency, positions, length):
    product = frequency[:, None] * positions[None, :] % length
    angles = product.astype(jnp.float32) * (TWO_PI / length)
    return (jnp.cos(angles), jnp.sin(angles))


def forward_x(pencil, cos_table, sin_table):
    row_total = pencil.shape[0]
    modes = cos_table.shape[0]
    with_cos = jnp.einsum(
        "kxf,mx->kmf", pencil, cos_table, preferred_element_type=jnp.float32
    ).reshape(row_total, modes, 2, -1)
    with_sin = jnp.einsum(
        "kxf,mx->kmf", pencil, sin_table, preferred_element_type=jnp.float32
    ).reshape(row_total, modes, 2, -1)
    real_part = with_cos[:, :, 0] + with_sin[:, :, 1]
    imag_part = with_cos[:, :, 1] - with_sin[:, :, 0]
    return jnp.stack([real_part, imag_part], axis=2).reshape(row_total, modes, -1)


def inverse_x(spectra, cos_table, sin_table):
    row_total = spectra.shape[0]
    points = cos_table.shape[1]
    with_cos = jnp.einsum(
        "kmf,mx->kxf", spectra, cos_table, preferred_element_type=jnp.float32
    ).reshape(row_total, points, 2, -1)
    with_sin = jnp.einsum(
        "kmf,mx->kxf", spectra, sin_table, preferred_element_type=jnp.float32
    ).reshape(row_total, points, 2, -1)
    real_part = with_cos[:, :, 0] - with_sin[:, :, 1]
    imag_part = with_cos[:, :, 1] + with_sin[:, :, 0]
    return jnp.stack([real_part, imag_part], axis=2).reshape(row_total, points, -1)


def mixing(weights, values):
    return jnp.einsum("kmoi,kmiz->kmoz", weights, values, preferred_element_type=jnp.float32)


def layer_sum_kernel(members, back_ref, table_ref, weight_ref, field_ref, bias_ref, out_ref, value, layer,
                     landed, send_sems, recv_sems):
    me = lax.axis_index("member")
    slab = lax.axis_index("slab")
    mesh_kind = pl.DeviceIdType.MESH
    barrier = pltpu.get_barrier_semaphore()
    for step in range(1, members):
        peer = lax.rem(me + step, members)
        pl.semaphore_signal(barrier, inc=1, device_id=(peer, slab), device_id_type=mesh_kind)
    cells = back_ref.shape[0]
    length = table_ref.shape[1]
    block_rows = layer.shape[1]
    for cell in range(cells):
        lanes = pl.ds(cell * length, length)
        spectral = jnp.dot(back_ref[cell], table_ref[...], preferred_element_type=jnp.float32)
        pointwise = jnp.dot(weight_ref[...], field_ref[:, lanes], preferred_element_type=jnp.float32)
        value[:, lanes] = jax.nn.gelu(pointwise + bias_ref[...] + spectral, approximate=True)
    for block in range(members):
        layer[block] = value[pl.ds(block * block_rows, block_rows), :].astype(layer.dtype)
    pl.semaphore_wait(barrier, members - 1)

    def copy_of(source, target, peer):
        return pltpu.make_async_remote_copy(
            src_ref=layer.at[source],
            dst_ref=landed.at[target],
            send_sem=send_sems.at[source],
            recv_sem=recv_sems.at[target],
            device_id=(peer, slab),
            device_id_type=mesh_kind,
        )

    for step in range(1, members):
        peer = lax.rem(me + step, members)
        copy_of(peer, me, peer).start()
    total = layer[me].astype(jnp.float32)
    for step in range(1, members):
        source = lax.rem(me + members - step, members)
        copy_of(source, source, source).wait_recv()
        total = total + landed[source].astype(jnp.float32)
    for step in range(1, members):
        peer = lax.rem(me + step, members)
        copy_of(peer, me, peer).wait_send()
    out_ref[...] = (total / members).astype(out_ref.dtype)


def layer_sum(back, table, weight, field, bias, members):
    channels, width = field.shape
    block_rows = channels // members
    return pl.pallas_call(
        functools.partial(layer_sum_kernel, members),
        out_shape=jax.ShapeDtypeStruct((block_rows, width), jnp.bfloat16),
        in_specs=[pl.BlockSpec(memory_space=pltpu.VMEM)] * 5,
        out_specs=pl.BlockSpec(memory_space=pltpu.VMEM),
        scratch_shapes=[
            pltpu.VMEM((channels, width), jnp.float32),
            pltpu.VMEM((members, block_rows, width), jnp.bfloat16),
            pltpu.VMEM((members, block_rows, width), jnp.bfloat16),
            pltpu.SemaphoreType.DMA((members,)),
            pltpu.SemaphoreType.DMA((members,)),
        ],
        compiler_params=pltpu.CompilerParams(collective_id=0, has_side_effects=True),
    )(back, table, weight, field, bias)


def slab_exchange_kernel(parts, blocks_ref, out_ref, landed, send_sems, recv_sems):
    me = lax.axis_index("slab")
    member = lax.axis_index("member")
    barrier = pltpu.get_barrier_semaphore()

    def greet(step, carry):
        peer = lax.rem(me + step, parts)
        pl.semaphore_signal(barrier, inc=1, device_id=(member, peer), device_id_type=pl.DeviceIdType.MESH)
        return carry

    lax.fori_loop(1, parts, greet, 0)
    pl.semaphore_wait(barrier, parts - 1)

    def send(step, carry):
        peer = lax.rem(me + step, parts)
        pltpu.make_async_remote_copy(
            src_ref=blocks_ref.at[peer],
            dst_ref=landed.at[me],
            send_sem=send_sems.at[peer],
            recv_sem=recv_sems.at[me],
            device_id=(member, peer),
            device_id_type=pl.DeviceIdType.MESH,
        ).start()
        return carry

    lax.fori_loop(1, parts, send, 0)
    landed[me] = blocks_ref[me]

    def receive(step, carry):
        source = lax.rem(me + parts - step, parts)
        pltpu.make_async_remote_copy(
            src_ref=blocks_ref.at[source],
            dst_ref=landed.at[source],
            send_sem=send_sems.at[source],
            recv_sem=recv_sems.at[source],
            device_id=(member, source),
            device_id_type=pl.DeviceIdType.MESH,
        ).wait_recv()
        return carry

    lax.fori_loop(1, parts, receive, 0)

    def sent(step, carry):
        peer = lax.rem(me + step, parts)
        pltpu.make_async_remote_copy(
            src_ref=blocks_ref.at[peer],
            dst_ref=landed.at[me],
            send_sem=send_sems.at[peer],
            recv_sem=recv_sems.at[me],
            device_id=(member, peer),
            device_id_type=pl.DeviceIdType.MESH,
        ).wait_send()
        return carry

    lax.fori_loop(1, parts, sent, 0)
    out_ref[...] = landed[...]


def slab_exchange(blocks, parts, exchange_id):
    return pl.pallas_call(
        functools.partial(slab_exchange_kernel, parts),
        out_shape=jax.ShapeDtypeStruct(blocks.shape, blocks.dtype),
        in_specs=[pl.BlockSpec(memory_space=pltpu.VMEM)],
        out_specs=pl.BlockSpec(memory_space=pltpu.VMEM),
        scratch_shapes=[
            pltpu.VMEM(blocks.shape, blocks.dtype),
            pltpu.SemaphoreType.DMA((parts,)),
            pltpu.SemaphoreType.DMA((parts,)),
        ],
        compiler_params=pltpu.CompilerParams(collective_id=exchange_id, has_side_effects=True),
    )(blocks)


def local(
    base_field,
    forcing,
    load,
    amplitudes,
    amp_index,
    mode_count,
    point_weight,
    point_bias,
    spectral_weight,
):
    channels, slab_rows, plane_count, length_y = base_field.shape
    slab_count = lax.axis_size("slab")
    local_modes = spectral_weight.shape[0]
    modes_y = local_modes * slab_count
    modes_x = spectral_weight.shape[1]
    length_x = slab_rows * slab_count
    packed_width = 2 * channels * plane_count
    slab_index = lax.axis_index("slab")
    level_ids = jnp.arange(amplitudes.shape[0], dtype=jnp.int32)
    amplitude = jnp.sum(jnp.where(level_ids == amp_index[0], amplitudes, 0.0))
    driven = base_field.astype(jnp.float32) + amplitude * load[:, None, None, None] * forcing[
        None
    ].astype(jnp.float32)
    field_now = (2.0 * jnp.tanh(0.5 * driven)).astype(jnp.bfloat16)
    y_cos, y_sin = phases(
        jnp.arange(modes_y, dtype=jnp.int32), jnp.arange(length_y, dtype=jnp.int32), length_y
    )
    y_real = jnp.einsum(
        "cxzy,ky->kxcz", field_now, y_cos.astype(jnp.bfloat16), preferred_element_type=jnp.float32
    )
    y_imag = -jnp.einsum(
        "cxzy,ky->kxcz", field_now, y_sin.astype(jnp.bfloat16), preferred_element_type=jnp.float32
    )
    packed = (
        jnp.stack([y_real, y_imag], axis=2)
        .astype(jnp.bfloat16)
        .reshape(modes_y, slab_rows, packed_width)
    )
    frequency_x = jnp.concatenate(
        [
            jnp.arange(modes_x // 2, dtype=jnp.int32),
            jnp.arange(length_x - modes_x // 2, length_x, dtype=jnp.int32),
        ]
    )
    full_cos, full_sin = phases(frequency_x, jnp.arange(length_x, dtype=jnp.int32), length_x)
    full_cos = full_cos.astype(jnp.bfloat16)
    full_sin = full_sin.astype(jnp.bfloat16)
    gathered = slab_exchange(packed, slab_count, 1).reshape(length_x, packed_width)[None]
    spectrum = forward_x(gathered, full_cos, full_sin)
    spectrum = spectrum.astype(jnp.bfloat16).reshape(local_modes, modes_x, 2, channels, plane_count)
    weight_real = spectral_weight[:, :, 0]
    weight_imag = spectral_weight[:, :, 1]
    spec_real = spectrum[:, :, 0]
    spec_imag = spectrum[:, :, 1]
    mix_real = mixing(weight_real, spec_real) - mixing(weight_imag, spec_imag)
    mix_imag = mixing(weight_real, spec_imag) + mixing(weight_imag, spec_real)
    global_modes = slab_index * local_modes + jnp.arange(local_modes, dtype=jnp.int32)
    keep = (global_modes < mode_count[0]).astype(jnp.float32)[:, None, None, None, None]
    mixed = (
        (jnp.stack([mix_real, mix_imag], axis=2) * keep)
        .astype(jnp.bfloat16)
        .reshape(local_modes, modes_x, packed_width)
    )
    returned = inverse_x(mixed, full_cos, full_sin).astype(jnp.bfloat16)
    returned = slab_exchange(returned.reshape(slab_count, slab_rows, packed_width), slab_count, 2)
    returned = returned.reshape(modes_y, slab_rows, 2, channels, plane_count)
    weights_y = jnp.where(jnp.arange(modes_y) == 0, 1.0, 2.0).astype(jnp.float32) / (
        length_x * length_y
    )
    back_cos = (weights_y[:, None] * y_cos).astype(jnp.bfloat16)
    back_sin = (weights_y[:, None] * y_sin).astype(jnp.bfloat16)
    table = jnp.concatenate([back_cos, -back_sin], axis=0)
    cells = slab_rows * plane_count
    back = returned.transpose(1, 4, 3, 2, 0).reshape(cells, channels, 2 * modes_y)
    bias = point_bias.reshape(channels, 1)
    field_rows = field_now.reshape(channels, cells * length_y)
    members = lax.axis_size("member")
    total = layer_sum(back, table, point_weight, field_rows, bias, members)
    return total.reshape(channels // members, slab_rows, plane_count, length_y)


def solution(mesh):
    in_specs = (
        P(None, "slab", None, None),
        P("slab", None, None),
        P(),
        P(),
        P("member"),
        P("member"),
        P(),
        P(),
        P("slab", None, None, None, None),
    )
    out_specs = P("member", "slab", None, None)
    return jax.shard_map(local, mesh=mesh, in_specs=in_specs, out_specs=out_specs, check_vma=False)
```

```python
import functools
import math

import jax
import jax.numpy as jnp
from jax import lax
from jax.experimental import pallas as pl
from jax.experimental.pallas import tpu as pltpu
from jax.sharding import PartitionSpec as P

TWO_PI = 2.0 * math.pi


def phases(frequency, positions, length):
    product = frequency[:, None] * positions[None, :] % length
    angles = product.astype(jnp.float32) * (TWO_PI / length)
    return (jnp.cos(angles), jnp.sin(angles))


def forward_x(pencil, cos_table, sin_table):
    row_total = pencil.shape[0]
    modes = cos_table.shape[0]
    with_cos = jnp.einsum(
        "kxf,mx->kmf", pencil, cos_table, preferred_element_type=jnp.float32
    ).reshape(row_total, modes, 2, -1)
    with_sin = jnp.einsum(
        "kxf,mx->kmf", pencil, sin_table, preferred_element_type=jnp.float32
    ).reshape(row_total, modes, 2, -1)
    real_part = with_cos[:, :, 0] + with_sin[:, :, 1]
    imag_part = with_cos[:, :, 1] - with_sin[:, :, 0]
    return jnp.stack([real_part, imag_part], axis=2).reshape(row_total, modes, -1)


def inverse_x(spectra, cos_table, sin_table):
    row_total = spectra.shape[0]
    points = cos_table.shape[1]
    with_cos = jnp.einsum(
        "kmf,mx->kxf", spectra, cos_table, preferred_element_type=jnp.float32
    ).reshape(row_total, points, 2, -1)
    with_sin = jnp.einsum(
        "kmf,mx->kxf", spectra, sin_table, preferred_element_type=jnp.float32
    ).reshape(row_total, points, 2, -1)
    real_part = with_cos[:, :, 0] - with_sin[:, :, 1]
    imag_part = with_cos[:, :, 1] + with_sin[:, :, 0]
    return jnp.stack([real_part, imag_part], axis=2).reshape(row_total, points, -1)


def mixing(weights, values):
    return jnp.einsum("kmoi,kmiz->kmoz", weights, values, preferred_element_type=jnp.float32)


def layer_sum_kernel(members, back_ref, table_ref, weight_ref, field_ref, bias_ref, out_ref, value, layer,
                     near, part, far, near_sems, far_send, far_recv):
    me = lax.axis_index("member")
    slab = lax.axis_index("slab")
    chips = members // 2
    chip, core = me // 2, me % 2
    sibling = chip * 2 + 1 - core
    mesh_kind = pl.DeviceIdType.MESH
    barrier = pltpu.get_barrier_semaphore()
    pl.semaphore_signal(barrier, inc=1, device_id=(sibling, slab), device_id_type=mesh_kind)
    for step in range(1, chips):
        peer = lax.rem(chip + step, chips) * 2 + core
        pl.semaphore_signal(barrier, inc=1, device_id=(peer, slab), device_id_type=mesh_kind)
    cells = back_ref.shape[0]
    length = table_ref.shape[1]
    block_rows = layer.shape[2]
    for cell in range(cells):
        lanes = pl.ds(cell * length, length)
        spectral = jnp.dot(back_ref[cell], table_ref[...], preferred_element_type=jnp.float32)
        pointwise = jnp.dot(weight_ref[...], field_ref[:, lanes], preferred_element_type=jnp.float32)
        value[:, lanes] = jax.nn.gelu(pointwise + bias_ref[...] + spectral, approximate=True)
    for block in range(members):
        rows = pl.ds(block * block_rows, block_rows)
        layer[block % 2, block // 2] = value[rows, :].astype(layer.dtype)
    pl.semaphore_wait(barrier, chips)

    on_chip = pltpu.make_async_remote_copy(
        src_ref=layer.at[1 - core],
        dst_ref=near,
        send_sem=near_sems.at[0],
        recv_sem=near_sems.at[1],
        device_id=(sibling, slab),
        device_id_type=mesh_kind,
    )
    on_chip.start()
    on_chip.wait_recv()
    for index in range(chips):
        pair = layer[core, index].astype(jnp.float32) + near[index].astype(jnp.float32)
        part[index] = pair.astype(part.dtype)
    on_chip.wait_send()

    def copy_of(source, target, peer_chip):
        return pltpu.make_async_remote_copy(
            src_ref=part.at[source],
            dst_ref=far.at[target],
            send_sem=far_send.at[source],
            recv_sem=far_recv.at[target],
            device_id=(peer_chip * 2 + core, slab),
            device_id_type=mesh_kind,
        )

    for step in range(1, chips):
        peer = lax.rem(chip + step, chips)
        copy_of(peer, chip, peer).start()
    total = part[chip].astype(jnp.float32)
    for step in range(1, chips):
        source = lax.rem(chip + chips - step, chips)
        copy_of(source, source, source).wait_recv()
        total = total + far[source].astype(jnp.float32)
    for step in range(1, chips):
        peer = lax.rem(chip + step, chips)
        copy_of(peer, chip, peer).wait_send()
    out_ref[...] = (total / members).astype(out_ref.dtype)


def layer_sum(back, table, weight, field, bias, members):
    channels, width = field.shape
    block_rows = channels // members
    chips = members // 2
    return pl.pallas_call(
        functools.partial(layer_sum_kernel, members),
        out_shape=jax.ShapeDtypeStruct((block_rows, width), jnp.bfloat16),
        in_specs=[pl.BlockSpec(memory_space=pltpu.VMEM)] * 5,
        out_specs=pl.BlockSpec(memory_space=pltpu.VMEM),
        scratch_shapes=[
            pltpu.VMEM((channels, width), jnp.float32),
            pltpu.VMEM((2, chips, block_rows, width), jnp.bfloat16),
            pltpu.VMEM((chips, block_rows, width), jnp.bfloat16),
            pltpu.VMEM((chips, block_rows, width), jnp.bfloat16),
            pltpu.VMEM((chips, block_rows, width), jnp.bfloat16),
            pltpu.SemaphoreType.DMA((2,)),
            pltpu.SemaphoreType.DMA((chips,)),
            pltpu.SemaphoreType.DMA((chips,)),
        ],
        compiler_params=pltpu.CompilerParams(collective_id=0, has_side_effects=True),
    )(back, table, weight, field, bias)


def slab_exchange_kernel(parts, blocks_ref, out_ref, landed, send_sems, recv_sems):
    me = lax.axis_index("slab")
    member = lax.axis_index("member")
    barrier = pltpu.get_barrier_semaphore()

    def greet(step, carry):
        peer = lax.rem(me + step, parts)
        pl.semaphore_signal(barrier, inc=1, device_id=(member, peer), device_id_type=pl.DeviceIdType.MESH)
        return carry

    lax.fori_loop(1, parts, greet, 0)
    pl.semaphore_wait(barrier, parts - 1)

    def send(step, carry):
        peer = lax.rem(me + step, parts)
        pltpu.make_async_remote_copy(
            src_ref=blocks_ref.at[peer],
            dst_ref=landed.at[me],
            send_sem=send_sems.at[peer],
            recv_sem=recv_sems.at[me],
            device_id=(member, peer),
            device_id_type=pl.DeviceIdType.MESH,
        ).start()
        return carry

    lax.fori_loop(1, parts, send, 0)
    landed[me] = blocks_ref[me]

    def receive(step, carry):
        source = lax.rem(me + parts - step, parts)
        pltpu.make_async_remote_copy(
            src_ref=blocks_ref.at[source],
            dst_ref=landed.at[source],
            send_sem=send_sems.at[source],
            recv_sem=recv_sems.at[source],
            device_id=(member, source),
            device_id_type=pl.DeviceIdType.MESH,
        ).wait_recv()
        return carry

    lax.fori_loop(1, parts, receive, 0)

    def sent(step, carry):
        peer = lax.rem(me + step, parts)
        pltpu.make_async_remote_copy(
            src_ref=blocks_ref.at[peer],
            dst_ref=landed.at[me],
            send_sem=send_sems.at[peer],
            recv_sem=recv_sems.at[me],
            device_id=(member, peer),
            device_id_type=pl.DeviceIdType.MESH,
        ).wait_send()
        return carry

    lax.fori_loop(1, parts, sent, 0)
    out_ref[...] = landed[...]


def slab_exchange(blocks, parts, exchange_id):
    return pl.pallas_call(
        functools.partial(slab_exchange_kernel, parts),
        out_shape=jax.ShapeDtypeStruct(blocks.shape, blocks.dtype),
        in_specs=[pl.BlockSpec(memory_space=pltpu.VMEM)],
        out_specs=pl.BlockSpec(memory_space=pltpu.VMEM),
        scratch_shapes=[
            pltpu.VMEM(blocks.shape, blocks.dtype),
            pltpu.SemaphoreType.DMA((parts,)),
            pltpu.SemaphoreType.DMA((parts,)),
        ],
        compiler_params=pltpu.CompilerParams(collective_id=exchange_id, has_side_effects=True),
    )(blocks)


def local(
    base_field,
    forcing,
    load,
    amplitudes,
    amp_index,
    mode_count,
    point_weight,
    point_bias,
    spectral_weight,
):
    channels, slab_rows, plane_count, length_y = base_field.shape
    slab_count = lax.axis_size("slab")
    local_modes = spectral_weight.shape[0]
    modes_y = local_modes * slab_count
    modes_x = spectral_weight.shape[1]
    length_x = slab_rows * slab_count
    packed_width = 2 * channels * plane_count
    slab_index = lax.axis_index("slab")
    level_ids = jnp.arange(amplitudes.shape[0], dtype=jnp.int32)
    amplitude = jnp.sum(jnp.where(level_ids == amp_index[0], amplitudes, 0.0))
    driven = base_field.astype(jnp.float32) + amplitude * load[:, None, None, None] * forcing[
        None
    ].astype(jnp.float32)
    field_now = (2.0 * jnp.tanh(0.5 * driven)).astype(jnp.bfloat16)
    y_cos, y_sin = phases(
        jnp.arange(modes_y, dtype=jnp.int32), jnp.arange(length_y, dtype=jnp.int32), length_y
    )
    y_real = jnp.einsum(
        "cxzy,ky->kxcz", field_now, y_cos.astype(jnp.bfloat16), preferred_element_type=jnp.float32
    )
    y_imag = -jnp.einsum(
        "cxzy,ky->kxcz", field_now, y_sin.astype(jnp.bfloat16), preferred_element_type=jnp.float32
    )
    packed = (
        jnp.stack([y_real, y_imag], axis=2)
        .astype(jnp.bfloat16)
        .reshape(modes_y, slab_rows, packed_width)
    )
    frequency_x = jnp.concatenate(
        [
            jnp.arange(modes_x // 2, dtype=jnp.int32),
            jnp.arange(length_x - modes_x // 2, length_x, dtype=jnp.int32),
        ]
    )
    full_cos, full_sin = phases(frequency_x, jnp.arange(length_x, dtype=jnp.int32), length_x)
    full_cos = full_cos.astype(jnp.bfloat16)
    full_sin = full_sin.astype(jnp.bfloat16)
    gathered = slab_exchange(packed, slab_count, 1).reshape(length_x, packed_width)[None]
    spectrum = forward_x(gathered, full_cos, full_sin)
    spectrum = spectrum.astype(jnp.bfloat16).reshape(local_modes, modes_x, 2, channels, plane_count)
    weight_real = spectral_weight[:, :, 0]
    weight_imag = spectral_weight[:, :, 1]
    spec_real = spectrum[:, :, 0]
    spec_imag = spectrum[:, :, 1]
    mix_real = mixing(weight_real, spec_real) - mixing(weight_imag, spec_imag)
    mix_imag = mixing(weight_real, spec_imag) + mixing(weight_imag, spec_real)
    global_modes = slab_index * local_modes + jnp.arange(local_modes, dtype=jnp.int32)
    keep = (global_modes < mode_count[0]).astype(jnp.float32)[:, None, None, None, None]
    mixed = (
        (jnp.stack([mix_real, mix_imag], axis=2) * keep)
        .astype(jnp.bfloat16)
        .reshape(local_modes, modes_x, packed_width)
    )
    returned = inverse_x(mixed, full_cos, full_sin).astype(jnp.bfloat16)
    returned = slab_exchange(returned.reshape(slab_count, slab_rows, packed_width), slab_count, 2)
    returned = returned.reshape(modes_y, slab_rows, 2, channels, plane_count)
    weights_y = jnp.where(jnp.arange(modes_y) == 0, 1.0, 2.0).astype(jnp.float32) / (
        length_x * length_y
    )
    back_cos = (weights_y[:, None] * y_cos).astype(jnp.bfloat16)
    back_sin = (weights_y[:, None] * y_sin).astype(jnp.bfloat16)
    table = jnp.concatenate([back_cos, -back_sin], axis=0)
    cells = slab_rows * plane_count
    back = returned.transpose(1, 4, 3, 2, 0).reshape(cells, channels, 2 * modes_y)
    bias = point_bias.reshape(channels, 1)
    field_rows = field_now.reshape(channels, cells * length_y)
    members = lax.axis_size("member")
    total = layer_sum(back, table, point_weight, field_rows, bias, members)
    return total.reshape(channels // members, slab_rows, plane_count, length_y)


def solution(mesh):
    in_specs = (
        P(None, "slab", None, None),
        P("slab", None, None),
        P(),
        P(),
        P("member"),
        P("member"),
        P(),
        P(),
        P("slab", None, None, None, None),
    )
    out_specs = P("member", "slab", None, None)
    return jax.shard_map(local, mesh=mesh, in_specs=in_specs, out_specs=out_specs, check_vma=False)
```

```python
import functools
import math

import jax
import jax.numpy as jnp
from jax import lax
from jax.experimental import pallas as pl
from jax.experimental.pallas import tpu as pltpu
from jax.sharding import PartitionSpec as P

TWO_PI = 2.0 * math.pi


def phases(frequency, positions, length):
    product = frequency[:, None] * positions[None, :] % length
    angles = product.astype(jnp.float32) * (TWO_PI / length)
    return (jnp.cos(angles), jnp.sin(angles))


def forward_x(pencil, cos_table, sin_table):
    row_total = pencil.shape[0]
    modes = cos_table.shape[0]
    with_cos = jnp.einsum(
        "kxf,mx->kmf", pencil, cos_table, preferred_element_type=jnp.float32
    ).reshape(row_total, modes, 2, -1)
    with_sin = jnp.einsum(
        "kxf,mx->kmf", pencil, sin_table, preferred_element_type=jnp.float32
    ).reshape(row_total, modes, 2, -1)
    real_part = with_cos[:, :, 0] + with_sin[:, :, 1]
    imag_part = with_cos[:, :, 1] - with_sin[:, :, 0]
    return jnp.stack([real_part, imag_part], axis=2).reshape(row_total, modes, -1)


def inverse_x(spectra, cos_table, sin_table):
    row_total = spectra.shape[0]
    points = cos_table.shape[1]
    with_cos = jnp.einsum(
        "kmf,mx->kxf", spectra, cos_table, preferred_element_type=jnp.float32
    ).reshape(row_total, points, 2, -1)
    with_sin = jnp.einsum(
        "kmf,mx->kxf", spectra, sin_table, preferred_element_type=jnp.float32
    ).reshape(row_total, points, 2, -1)
    real_part = with_cos[:, :, 0] - with_sin[:, :, 1]
    imag_part = with_cos[:, :, 1] + with_sin[:, :, 0]
    return jnp.stack([real_part, imag_part], axis=2).reshape(row_total, points, -1)


def mixing(weights, values):
    return jnp.einsum("kmoi,kmiz->kmoz", weights, values, preferred_element_type=jnp.float32)


def layer_sum_kernel(members, back_ref, table_ref, weight_ref, field_ref, bias_ref, out_ref, value, layer,
                     near, part, far, near_sems, far_send, far_recv):
    me = lax.axis_index("member")
    slab = lax.axis_index("slab")
    chips = members // 2
    chip, core = me // 2, me % 2
    sibling = chip * 2 + 1 - core
    mesh_kind = pl.DeviceIdType.MESH
    barrier = pltpu.get_barrier_semaphore()
    pl.semaphore_signal(barrier, inc=1, device_id=(sibling, slab), device_id_type=mesh_kind)
    for step in range(1, chips):
        peer = lax.rem(chip + step, chips) * 2 + core
        pl.semaphore_signal(barrier, inc=1, device_id=(peer, slab), device_id_type=mesh_kind)
    cells = back_ref.shape[0]
    length = table_ref.shape[1]
    block_rows = layer.shape[2]
    for cell in range(cells):
        lanes = pl.ds(cell * length, length)
        spectral = jnp.dot(back_ref[cell], table_ref[...], preferred_element_type=jnp.float32)
        pointwise = jnp.dot(weight_ref[...], field_ref[:, lanes], preferred_element_type=jnp.float32)
        value[:, lanes] = jax.nn.gelu(pointwise + bias_ref[...] + spectral, approximate=True)
    for block in range(members):
        rows = pl.ds(block * block_rows, block_rows)
        layer[block % 2, block // 2] = value[rows, :].astype(layer.dtype)
    pl.semaphore_wait(barrier, chips)

    on_chip = pltpu.make_async_remote_copy(
        src_ref=layer.at[1 - core],
        dst_ref=near,
        send_sem=near_sems.at[0],
        recv_sem=near_sems.at[1],
        device_id=(sibling, slab),
        device_id_type=mesh_kind,
    )
    on_chip.start()
    on_chip.wait_recv()
    for index in range(chips):
        pair = layer[core, index].astype(jnp.float32) + near[index].astype(jnp.float32)
        part[index] = pair.astype(part.dtype)
    on_chip.wait_send()

    def copy_of(source, target, peer_chip):
        return pltpu.make_async_remote_copy(
            src_ref=part.at[source],
            dst_ref=far.at[target],
            send_sem=far_send.at[source],
            recv_sem=far_recv.at[target],
            device_id=(peer_chip * 2 + core, slab),
            device_id_type=mesh_kind,
        )

    for step in range(1, chips):
        peer = lax.rem(chip + step, chips)
        copy_of(peer, chip, peer).start()
    total = part[chip].astype(jnp.float32)
    for step in range(1, chips):
        source = lax.rem(chip + chips - step, chips)
        copy_of(source, source, source).wait_recv()
        total = total + far[source].astype(jnp.float32)
    for step in range(1, chips):
        peer = lax.rem(chip + step, chips)
        copy_of(peer, chip, peer).wait_send()
    out_ref[...] = (total / members).astype(out_ref.dtype)


def layer_sum(back, table, weight, field, bias, members):
    channels, width = field.shape
    block_rows = channels // members
    chips = members // 2
    return pl.pallas_call(
        functools.partial(layer_sum_kernel, members),
        out_shape=jax.ShapeDtypeStruct((block_rows, width), jnp.bfloat16),
        in_specs=[pl.BlockSpec(memory_space=pltpu.VMEM)] * 5,
        out_specs=pl.BlockSpec(memory_space=pltpu.VMEM),
        scratch_shapes=[
            pltpu.VMEM((channels, width), jnp.float32),
            pltpu.VMEM((2, chips, block_rows, width), jnp.bfloat16),
            pltpu.VMEM((chips, block_rows, width), jnp.bfloat16),
            pltpu.VMEM((chips, block_rows, width), jnp.bfloat16),
            pltpu.VMEM((chips, block_rows, width), jnp.bfloat16),
            pltpu.SemaphoreType.DMA((2,)),
            pltpu.SemaphoreType.DMA((chips,)),
            pltpu.SemaphoreType.DMA((chips,)),
        ],
        compiler_params=pltpu.CompilerParams(collective_id=0, has_side_effects=True),
    )(back, table, weight, field, bias)


def slab_exchange_kernel(parts, blocks_ref, out_ref, landed, send_sems, recv_sems):
    me = lax.axis_index("slab")
    member = lax.axis_index("member")
    mesh_kind = pl.DeviceIdType.MESH
    barrier = pltpu.get_barrier_semaphore()
    for step in range(1, parts):
        peer = lax.rem(me + step, parts)
        pl.semaphore_signal(barrier, inc=1, device_id=(member, peer), device_id_type=mesh_kind)
    pl.semaphore_wait(barrier, parts - 1)

    def copy_of(source, target, peer):
        return pltpu.make_async_remote_copy(
            src_ref=blocks_ref.at[source],
            dst_ref=landed.at[target],
            send_sem=send_sems.at[source],
            recv_sem=recv_sems.at[target],
            device_id=(member, peer),
            device_id_type=mesh_kind,
        )

    for step in range(1, parts):
        peer = lax.rem(me + step, parts)
        copy_of(peer, me, peer).start()
    landed[me] = blocks_ref[me]
    for step in range(1, parts):
        source = lax.rem(me + parts - step, parts)
        copy_of(source, source, source).wait_recv()
    for step in range(1, parts):
        peer = lax.rem(me + step, parts)
        copy_of(peer, me, peer).wait_send()
    out_ref[...] = landed[...]


def slab_exchange(blocks, parts, exchange_id):
    return pl.pallas_call(
        functools.partial(slab_exchange_kernel, parts),
        out_shape=jax.ShapeDtypeStruct(blocks.shape, blocks.dtype),
        in_specs=[pl.BlockSpec(memory_space=pltpu.VMEM)],
        out_specs=pl.BlockSpec(memory_space=pltpu.VMEM),
        scratch_shapes=[
            pltpu.VMEM(blocks.shape, blocks.dtype),
            pltpu.SemaphoreType.DMA((parts,)),
            pltpu.SemaphoreType.DMA((parts,)),
        ],
        compiler_params=pltpu.CompilerParams(collective_id=exchange_id, has_side_effects=True),
    )(blocks)


def local(
    base_field,
    forcing,
    load,
    amplitudes,
    amp_index,
    mode_count,
    point_weight,
    point_bias,
    spectral_weight,
):
    channels, slab_rows, plane_count, length_y = base_field.shape
    slab_count = lax.axis_size("slab")
    local_modes = spectral_weight.shape[0]
    modes_y = local_modes * slab_count
    modes_x = spectral_weight.shape[1]
    length_x = slab_rows * slab_count
    packed_width = 2 * channels * plane_count
    slab_index = lax.axis_index("slab")
    level_ids = jnp.arange(amplitudes.shape[0], dtype=jnp.int32)
    amplitude = jnp.sum(jnp.where(level_ids == amp_index[0], amplitudes, 0.0))
    driven = base_field.astype(jnp.float32) + amplitude * load[:, None, None, None] * forcing[
        None
    ].astype(jnp.float32)
    field_now = (2.0 * jnp.tanh(0.5 * driven)).astype(jnp.bfloat16)
    y_cos, y_sin = phases(
        jnp.arange(modes_y, dtype=jnp.int32), jnp.arange(length_y, dtype=jnp.int32), length_y
    )
    y_real = jnp.einsum(
        "cxzy,ky->kxcz", field_now, y_cos.astype(jnp.bfloat16), preferred_element_type=jnp.float32
    )
    y_imag = -jnp.einsum(
        "cxzy,ky->kxcz", field_now, y_sin.astype(jnp.bfloat16), preferred_element_type=jnp.float32
    )
    packed = (
        jnp.stack([y_real, y_imag], axis=2)
        .astype(jnp.bfloat16)
        .reshape(modes_y, slab_rows, packed_width)
    )
    frequency_x = jnp.concatenate(
        [
            jnp.arange(modes_x // 2, dtype=jnp.int32),
            jnp.arange(length_x - modes_x // 2, length_x, dtype=jnp.int32),
        ]
    )
    full_cos, full_sin = phases(frequency_x, jnp.arange(length_x, dtype=jnp.int32), length_x)
    full_cos = full_cos.astype(jnp.bfloat16)
    full_sin = full_sin.astype(jnp.bfloat16)
    gathered = slab_exchange(packed, slab_count, 1).reshape(length_x, packed_width)[None]
    spectrum = forward_x(gathered, full_cos, full_sin)
    spectrum = spectrum.astype(jnp.bfloat16).reshape(local_modes, modes_x, 2, channels, plane_count)
    weight_real = spectral_weight[:, :, 0]
    weight_imag = spectral_weight[:, :, 1]
    spec_real = spectrum[:, :, 0]
    spec_imag = spectrum[:, :, 1]
    mix_real = mixing(weight_real, spec_real) - mixing(weight_imag, spec_imag)
    mix_imag = mixing(weight_real, spec_imag) + mixing(weight_imag, spec_real)
    global_modes = slab_index * local_modes + jnp.arange(local_modes, dtype=jnp.int32)
    keep = (global_modes < mode_count[0]).astype(jnp.float32)[:, None, None, None, None]
    mixed = (
        (jnp.stack([mix_real, mix_imag], axis=2) * keep)
        .astype(jnp.bfloat16)
        .reshape(local_modes, modes_x, packed_width)
    )
    returned = inverse_x(mixed, full_cos, full_sin).astype(jnp.bfloat16)
    returned = slab_exchange(returned.reshape(slab_count, slab_rows, packed_width), slab_count, 2)
    returned = returned.reshape(modes_y, slab_rows, 2, channels, plane_count)
    weights_y = jnp.where(jnp.arange(modes_y) == 0, 1.0, 2.0).astype(jnp.float32) / (
        length_x * length_y
    )
    back_cos = (weights_y[:, None] * y_cos).astype(jnp.bfloat16)
    back_sin = (weights_y[:, None] * y_sin).astype(jnp.bfloat16)
    table = jnp.concatenate([back_cos, -back_sin], axis=0)
    cells = slab_rows * plane_count
    back = returned.transpose(1, 4, 3, 2, 0).reshape(cells, channels, 2 * modes_y)
    bias = point_bias.reshape(channels, 1)
    field_rows = field_now.reshape(channels, cells * length_y)
    members = lax.axis_size("member")
    total = layer_sum(back, table, point_weight, field_rows, bias, members)
    return total.reshape(channels // members, slab_rows, plane_count, length_y)


def solution(mesh):
    in_specs = (
        P(None, "slab", None, None),
        P("slab", None, None),
        P(),
        P(),
        P("member"),
        P("member"),
        P(),
        P(),
        P("slab", None, None, None, None),
    )
    out_specs = P("member", "slab", None, None)
    return jax.shard_map(local, mesh=mesh, in_specs=in_specs, out_specs=out_specs, check_vma=False)
```

```python
import functools
import math

import jax
import jax.numpy as jnp
from jax import lax
from jax.experimental import pallas as pl
from jax.experimental.pallas import tpu as pltpu
from jax.sharding import PartitionSpec as P

TWO_PI = 2.0 * math.pi


def phases(frequency, positions, length):
    product = frequency[:, None] * positions[None, :] % length
    angles = product.astype(jnp.float32) * (TWO_PI / length)
    return (jnp.cos(angles), jnp.sin(angles))


def forward_x(pencil, cos_table, sin_table):
    row_total = pencil.shape[0]
    modes = cos_table.shape[0]
    with_cos = jnp.einsum(
        "kxf,mx->kmf", pencil, cos_table, preferred_element_type=jnp.float32
    ).reshape(row_total, modes, 2, -1)
    with_sin = jnp.einsum(
        "kxf,mx->kmf", pencil, sin_table, preferred_element_type=jnp.float32
    ).reshape(row_total, modes, 2, -1)
    real_part = with_cos[:, :, 0] + with_sin[:, :, 1]
    imag_part = with_cos[:, :, 1] - with_sin[:, :, 0]
    return jnp.stack([real_part, imag_part], axis=2).reshape(row_total, modes, -1)


def inverse_x(spectra, cos_table, sin_table):
    row_total = spectra.shape[0]
    points = cos_table.shape[1]
    with_cos = jnp.einsum(
        "kmf,mx->kxf", spectra, cos_table, preferred_element_type=jnp.float32
    ).reshape(row_total, points, 2, -1)
    with_sin = jnp.einsum(
        "kmf,mx->kxf", spectra, sin_table, preferred_element_type=jnp.float32
    ).reshape(row_total, points, 2, -1)
    real_part = with_cos[:, :, 0] - with_sin[:, :, 1]
    imag_part = with_cos[:, :, 1] + with_sin[:, :, 0]
    return jnp.stack([real_part, imag_part], axis=2).reshape(row_total, points, -1)


def mixing(weights, values):
    return jnp.einsum("kmoi,kmiz->kmoz", weights, values, preferred_element_type=jnp.float32)


def layer_sum_kernel(members, back_ref, table_ref, weight_ref, field_ref, bias_ref, out_ref, value, layer,
                     near, part, far, near_sems, far_send, far_recv):
    me = lax.axis_index("member")
    slab = lax.axis_index("slab")
    chips = members // 2
    chip, core = me // 2, me % 2
    sibling = chip * 2 + 1 - core
    mesh_kind = pl.DeviceIdType.MESH
    barrier = pltpu.get_barrier_semaphore()
    pl.semaphore_signal(barrier, inc=1, device_id=(sibling, slab), device_id_type=mesh_kind)
    for step in range(1, chips):
        peer = lax.rem(chip + step, chips) * 2 + core
        pl.semaphore_signal(barrier, inc=1, device_id=(peer, slab), device_id_type=mesh_kind)
    cells = back_ref.shape[0]
    length = table_ref.shape[1]
    block_rows = layer.shape[2]
    for cell in range(cells):
        lanes = pl.ds(cell * length, length)
        spectral = jnp.dot(back_ref[cell], table_ref[...], preferred_element_type=jnp.float32)
        pointwise = jnp.dot(weight_ref[...], field_ref[:, lanes], preferred_element_type=jnp.float32)
        value[:, lanes] = jax.nn.gelu(pointwise + bias_ref[...] + spectral, approximate=True)
    for block in range(members):
        rows = pl.ds(block * block_rows, block_rows)
        layer[block % 2, block // 2] = value[rows, :].astype(layer.dtype)
    pl.semaphore_wait(barrier, chips)

    on_chip = pltpu.make_async_remote_copy(
        src_ref=layer.at[1 - core],
        dst_ref=near,
        send_sem=near_sems.at[0],
        recv_sem=near_sems.at[1],
        device_id=(sibling, slab),
        device_id_type=mesh_kind,
    )
    on_chip.start()
    on_chip.wait_recv()
    for index in range(chips):
        pair = layer[core, index].astype(jnp.float32) + near[index].astype(jnp.float32)
        part[index] = pair.astype(part.dtype)
    on_chip.wait_send()

    def copy_of(source, target, peer_chip):
        return pltpu.make_async_remote_copy(
            src_ref=part.at[source],
            dst_ref=far.at[target],
            send_sem=far_send.at[source],
            recv_sem=far_recv.at[target],
            device_id=(peer_chip * 2 + core, slab),
            device_id_type=mesh_kind,
        )

    for step in range(1, chips):
        peer = lax.rem(chip + step, chips)
        copy_of(peer, chip, peer).start()
    total = part[chip].astype(jnp.float32)
    for step in range(1, chips):
        source = lax.rem(chip + chips - step, chips)
        copy_of(source, source, source).wait_recv()
        total = total + far[source].astype(jnp.float32)
    for step in range(1, chips):
        peer = lax.rem(chip + step, chips)
        copy_of(peer, chip, peer).wait_send()
    out_ref[...] = (total / members).astype(out_ref.dtype)


def layer_sum(back, table, weight, field, bias, members):
    channels, width = field.shape
    block_rows = channels // members
    chips = members // 2
    return pl.pallas_call(
        functools.partial(layer_sum_kernel, members),
        out_shape=jax.ShapeDtypeStruct((block_rows, width), jnp.bfloat16),
        in_specs=[pl.BlockSpec(memory_space=pltpu.VMEM)] * 5,
        out_specs=pl.BlockSpec(memory_space=pltpu.VMEM),
        scratch_shapes=[
            pltpu.VMEM((channels, width), jnp.float32),
            pltpu.VMEM((2, chips, block_rows, width), jnp.bfloat16),
            pltpu.VMEM((chips, block_rows, width), jnp.bfloat16),
            pltpu.VMEM((chips, block_rows, width), jnp.bfloat16),
            pltpu.VMEM((chips, block_rows, width), jnp.bfloat16),
            pltpu.SemaphoreType.DMA((2,)),
            pltpu.SemaphoreType.DMA((chips,)),
            pltpu.SemaphoreType.DMA((chips,)),
        ],
        compiler_params=pltpu.CompilerParams(collective_id=0, has_side_effects=True),
    )(back, table, weight, field, bias)


def greet_slab(parts):
    me = lax.axis_index("slab")
    member = lax.axis_index("member")
    barrier = pltpu.get_barrier_semaphore()
    for step in range(1, parts):
        peer = lax.rem(me + step, parts)
        pl.semaphore_signal(barrier, inc=1, device_id=(member, peer), device_id_type=pl.DeviceIdType.MESH)
    return barrier


def swap_blocks(parts, source_ref, out_ref, landed, send_sems, recv_sems):
    me = lax.axis_index("slab")
    member = lax.axis_index("member")

    def copy_of(source, target, peer):
        return pltpu.make_async_remote_copy(
            src_ref=source_ref.at[source],
            dst_ref=landed.at[target],
            send_sem=send_sems.at[source],
            recv_sem=recv_sems.at[target],
            device_id=(member, peer),
            device_id_type=pl.DeviceIdType.MESH,
        )

    for step in range(1, parts):
        peer = lax.rem(me + step, parts)
        copy_of(peer, me, peer).start()
    landed[me] = source_ref[me]
    for step in range(1, parts):
        source = lax.rem(me + parts - step, parts)
        copy_of(source, source, source).wait_recv()
    for step in range(1, parts):
        peer = lax.rem(me + step, parts)
        copy_of(peer, me, peer).wait_send()
    out_ref[...] = landed[...]


def slab_exchange_kernel(parts, blocks_ref, out_ref, landed, send_sems, recv_sems):
    barrier = greet_slab(parts)
    pl.semaphore_wait(barrier, parts - 1)
    swap_blocks(parts, blocks_ref, out_ref, landed, send_sems, recv_sems)


def mode_mix_kernel(parts, pencil_ref, xcos_ref, xsin_ref, xcos_t_ref, xsin_t_ref, swap_ref, weight_ref,
                    keep_ref, out_ref, expanded, blocks, landed, send_sems, recv_sems):
    barrier = greet_slab(parts)
    pencil = pencil_ref[...]
    swapped = jnp.dot(pencil, swap_ref[...], preferred_element_type=jnp.float32).astype(pencil.dtype)
    spec = jnp.dot(xcos_ref[...], pencil, preferred_element_type=jnp.float32)
    spec = spec + jnp.dot(xsin_ref[...], swapped, preferred_element_type=jnp.float32)
    spec = spec.astype(pencil.dtype).astype(jnp.float32)
    modes, width = spec.shape
    rows = lax.broadcasted_iota(jnp.int32, spec.shape, 0)
    for mode in range(modes):
        lanes = pl.ds(mode * width, width)
        expanded[:, lanes] = jnp.where(rows == mode, spec, 0.0).astype(expanded.dtype)
    mixed = jnp.dot(expanded[...], weight_ref[...], preferred_element_type=jnp.float32)
    mixed = (mixed * keep_ref[...]).astype(pencil.dtype)
    mixed_swapped = jnp.dot(mixed, swap_ref[...], preferred_element_type=jnp.float32).astype(pencil.dtype)
    back = jnp.dot(xcos_t_ref[...], mixed, preferred_element_type=jnp.float32)
    back = back - jnp.dot(xsin_t_ref[...], mixed_swapped, preferred_element_type=jnp.float32)
    blocks[...] = back.reshape(blocks.shape).astype(blocks.dtype)
    pl.semaphore_wait(barrier, parts - 1)
    swap_blocks(parts, blocks, out_ref, landed, send_sems, recv_sems)


def mode_mix_exchange(pencil, xcos, xsin, swap, weight, keep, parts):
    points, width = pencil.shape
    modes = xcos.shape[0]
    shape = (parts, points // parts, width)
    return pl.pallas_call(
        functools.partial(mode_mix_kernel, parts),
        out_shape=jax.ShapeDtypeStruct(shape, pencil.dtype),
        in_specs=[pl.BlockSpec(memory_space=pltpu.VMEM)] * 8,
        out_specs=pl.BlockSpec(memory_space=pltpu.VMEM),
        scratch_shapes=[
            pltpu.VMEM((modes, modes * width), pencil.dtype),
            pltpu.VMEM(shape, pencil.dtype),
            pltpu.VMEM(shape, pencil.dtype),
            pltpu.SemaphoreType.DMA((parts,)),
            pltpu.SemaphoreType.DMA((parts,)),
        ],
        compiler_params=pltpu.CompilerParams(collective_id=2, has_side_effects=True),
    )(pencil, xcos, xsin, xcos.T, xsin.T, swap, weight, keep)


def slab_exchange(blocks, parts, exchange_id):
    return pl.pallas_call(
        functools.partial(slab_exchange_kernel, parts),
        out_shape=jax.ShapeDtypeStruct(blocks.shape, blocks.dtype),
        in_specs=[pl.BlockSpec(memory_space=pltpu.VMEM)],
        out_specs=pl.BlockSpec(memory_space=pltpu.VMEM),
        scratch_shapes=[
            pltpu.VMEM(blocks.shape, blocks.dtype),
            pltpu.SemaphoreType.DMA((parts,)),
            pltpu.SemaphoreType.DMA((parts,)),
        ],
        compiler_params=pltpu.CompilerParams(collective_id=exchange_id, has_side_effects=True),
    )(blocks)


def local(
    base_field,
    forcing,
    load,
    amplitudes,
    amp_index,
    mode_count,
    point_weight,
    point_bias,
    spectral_weight,
):
    channels, slab_rows, plane_count, length_y = base_field.shape
    slab_count = lax.axis_size("slab")
    local_modes = spectral_weight.shape[0]
    modes_y = local_modes * slab_count
    modes_x = spectral_weight.shape[1]
    length_x = slab_rows * slab_count
    packed_width = 2 * channels * plane_count
    slab_index = lax.axis_index("slab")
    level_ids = jnp.arange(amplitudes.shape[0], dtype=jnp.int32)
    amplitude = jnp.sum(jnp.where(level_ids == amp_index[0], amplitudes, 0.0))
    driven = base_field.astype(jnp.float32) + amplitude * load[:, None, None, None] * forcing[
        None
    ].astype(jnp.float32)
    field_now = (2.0 * jnp.tanh(0.5 * driven)).astype(jnp.bfloat16)
    y_cos, y_sin = phases(
        jnp.arange(modes_y, dtype=jnp.int32), jnp.arange(length_y, dtype=jnp.int32), length_y
    )
    y_real = jnp.einsum(
        "cxzy,ky->kxcz", field_now, y_cos.astype(jnp.bfloat16), preferred_element_type=jnp.float32
    )
    y_imag = -jnp.einsum(
        "cxzy,ky->kxcz", field_now, y_sin.astype(jnp.bfloat16), preferred_element_type=jnp.float32
    )
    packed = (
        jnp.stack([y_real, y_imag], axis=2)
        .transpose(0, 1, 4, 2, 3)
        .astype(jnp.bfloat16)
        .reshape(modes_y, slab_rows, packed_width)
    )
    frequency_x = jnp.concatenate(
        [
            jnp.arange(modes_x // 2, dtype=jnp.int32),
            jnp.arange(length_x - modes_x // 2, length_x, dtype=jnp.int32),
        ]
    )
    full_cos, full_sin = phases(frequency_x, jnp.arange(length_x, dtype=jnp.int32), length_x)
    full_cos = full_cos.astype(jnp.bfloat16)
    full_sin = full_sin.astype(jnp.bfloat16)
    gathered = slab_exchange(packed, slab_count, 1).reshape(length_x, packed_width)
    lane = jnp.arange(packed_width, dtype=jnp.int32)
    real_lane = (lane // channels) % 2 == 0
    swap = jnp.where(
        real_lane[None, :],
        (lane[:, None] == lane[None, :] + channels).astype(jnp.float32),
        -(lane[:, None] == lane[None, :] - channels).astype(jnp.float32),
    ).astype(jnp.bfloat16)
    weight_t = spectral_weight[0].transpose(0, 1, 3, 2)
    block = jnp.concatenate(
        [
            jnp.concatenate([weight_t[:, 0], weight_t[:, 1]], axis=2),
            jnp.concatenate([-weight_t[:, 1], weight_t[:, 0]], axis=2),
        ],
        axis=1,
    )
    empty = jnp.zeros_like(block)
    weight = jnp.concatenate(
        [jnp.concatenate([block, empty], axis=2), jnp.concatenate([empty, block], axis=2)], axis=1
    ).reshape(modes_x * packed_width, packed_width)
    kept = (slab_index * local_modes < mode_count[0]).astype(jnp.float32)
    keep = jnp.full((1, packed_width), kept, jnp.float32)
    returned = mode_mix_exchange(gathered, full_cos, full_sin, swap, weight, keep, slab_count)
    returned = returned.reshape(modes_y, slab_rows, plane_count, 2, channels)
    weights_y = jnp.where(jnp.arange(modes_y) == 0, 1.0, 2.0).astype(jnp.float32) / (
        length_x * length_y
    )
    back_cos = (weights_y[:, None] * y_cos).astype(jnp.bfloat16)
    back_sin = (weights_y[:, None] * y_sin).astype(jnp.bfloat16)
    table = jnp.concatenate([back_cos, -back_sin], axis=0)
    cells = slab_rows * plane_count
    back = returned.transpose(1, 2, 4, 3, 0).reshape(cells, channels, 2 * modes_y)
    bias = point_bias.reshape(channels, 1)
    field_rows = field_now.reshape(channels, cells * length_y)
    members = lax.axis_size("member")
    total = layer_sum(back, table, point_weight, field_rows, bias, members)
    return total.reshape(channels // members, slab_rows, plane_count, length_y)


def solution(mesh):
    in_specs = (
        P(None, "slab", None, None),
        P("slab", None, None),
        P(),
        P(),
        P("member"),
        P("member"),
        P(),
        P(),
        P("slab", None, None, None, None),
    )
    out_specs = P("member", "slab", None, None)
    return jax.shard_map(local, mesh=mesh, in_specs=in_specs, out_specs=out_specs, check_vma=False)
```

```python
import functools
import math

import jax
import jax.numpy as jnp
from jax import lax
from jax.experimental import pallas as pl
from jax.experimental.pallas import tpu as pltpu
from jax.sharding import PartitionSpec as P

TWO_PI = 2.0 * math.pi


def phases(frequency, positions, length):
    product = frequency[:, None] * positions[None, :] % length
    angles = product.astype(jnp.float32) * (TWO_PI / length)
    return (jnp.cos(angles), jnp.sin(angles))


def forward_x(pencil, cos_table, sin_table):
    row_total = pencil.shape[0]
    modes = cos_table.shape[0]
    with_cos = jnp.einsum(
        "kxf,mx->kmf", pencil, cos_table, preferred_element_type=jnp.float32
    ).reshape(row_total, modes, 2, -1)
    with_sin = jnp.einsum(
        "kxf,mx->kmf", pencil, sin_table, preferred_element_type=jnp.float32
    ).reshape(row_total, modes, 2, -1)
    real_part = with_cos[:, :, 0] + with_sin[:, :, 1]
    imag_part = with_cos[:, :, 1] - with_sin[:, :, 0]
    return jnp.stack([real_part, imag_part], axis=2).reshape(row_total, modes, -1)


def inverse_x(spectra, cos_table, sin_table):
    row_total = spectra.shape[0]
    points = cos_table.shape[1]
    with_cos = jnp.einsum(
        "kmf,mx->kxf", spectra, cos_table, preferred_element_type=jnp.float32
    ).reshape(row_total, points, 2, -1)
    with_sin = jnp.einsum(
        "kmf,mx->kxf", spectra, sin_table, preferred_element_type=jnp.float32
    ).reshape(row_total, points, 2, -1)
    real_part = with_cos[:, :, 0] - with_sin[:, :, 1]
    imag_part = with_cos[:, :, 1] + with_sin[:, :, 0]
    return jnp.stack([real_part, imag_part], axis=2).reshape(row_total, points, -1)


def mixing(weights, values):
    return jnp.einsum("kmoi,kmiz->kmoz", weights, values, preferred_element_type=jnp.float32)


def layer_sum_kernel(members, back_ref, table_ref, weight_ref, field_ref, bias_ref, out_ref, value, layer,
                     near, part, far, near_sems, far_send, far_recv):
    me = lax.axis_index("member")
    slab = lax.axis_index("slab")
    chips = members // 2
    chip, core = me // 2, me % 2
    sibling = chip * 2 + 1 - core
    mesh_kind = pl.DeviceIdType.MESH
    barrier = pltpu.get_barrier_semaphore()
    pl.semaphore_signal(barrier, inc=1, device_id=(sibling, slab), device_id_type=mesh_kind)
    for step in range(1, chips):
        peer = lax.rem(chip + step, chips) * 2 + core
        pl.semaphore_signal(barrier, inc=1, device_id=(peer, slab), device_id_type=mesh_kind)
    cells = back_ref.shape[0]
    length = table_ref.shape[1]
    block_rows = layer.shape[2]
    for cell in range(cells):
        lanes = pl.ds(cell * length, length)
        spectral = jnp.dot(back_ref[cell], table_ref[...], preferred_element_type=jnp.float32)
        pointwise = jnp.dot(weight_ref[...], field_ref[:, lanes], preferred_element_type=jnp.float32)
        value[:, lanes] = jax.nn.gelu(pointwise + bias_ref[...] + spectral, approximate=True)
    for block in range(members):
        rows = pl.ds(block * block_rows, block_rows)
        layer[block % 2, block // 2] = value[rows, :].astype(layer.dtype)
    pl.semaphore_wait(barrier, chips)

    on_chip = pltpu.make_async_remote_copy(
        src_ref=layer.at[1 - core],
        dst_ref=near,
        send_sem=near_sems.at[0],
        recv_sem=near_sems.at[1],
        device_id=(sibling, slab),
        device_id_type=mesh_kind,
    )
    on_chip.start()
    on_chip.wait_recv()
    for index in range(chips):
        pair = layer[core, index].astype(jnp.float32) + near[index].astype(jnp.float32)
        part[index] = pair.astype(part.dtype)
    on_chip.wait_send()

    def copy_of(source, target, peer_chip):
        return pltpu.make_async_remote_copy(
            src_ref=part.at[source],
            dst_ref=far.at[target],
            send_sem=far_send.at[source],
            recv_sem=far_recv.at[target],
            device_id=(peer_chip * 2 + core, slab),
            device_id_type=mesh_kind,
        )

    for step in range(1, chips):
        peer = lax.rem(chip + step, chips)
        copy_of(peer, chip, peer).start()
    total = part[chip].astype(jnp.float32)
    for step in range(1, chips):
        source = lax.rem(chip + chips - step, chips)
        copy_of(source, source, source).wait_recv()
        total = total + far[source].astype(jnp.float32)
    for step in range(1, chips):
        peer = lax.rem(chip + step, chips)
        copy_of(peer, chip, peer).wait_send()
    out_ref[...] = (total / members).astype(out_ref.dtype)


def layer_sum(back, table, weight, field, bias, members):
    channels, width = field.shape
    block_rows = channels // members
    chips = members // 2
    return pl.pallas_call(
        functools.partial(layer_sum_kernel, members),
        out_shape=jax.ShapeDtypeStruct((block_rows, width), jnp.bfloat16),
        in_specs=[pl.BlockSpec(memory_space=pltpu.VMEM)] * 5,
        out_specs=pl.BlockSpec(memory_space=pltpu.VMEM),
        scratch_shapes=[
            pltpu.VMEM((channels, width), jnp.float32),
            pltpu.VMEM((2, chips, block_rows, width), jnp.bfloat16),
            pltpu.VMEM((chips, block_rows, width), jnp.bfloat16),
            pltpu.VMEM((chips, block_rows, width), jnp.bfloat16),
            pltpu.VMEM((chips, block_rows, width), jnp.bfloat16),
            pltpu.SemaphoreType.DMA((2,)),
            pltpu.SemaphoreType.DMA((chips,)),
            pltpu.SemaphoreType.DMA((chips,)),
        ],
        compiler_params=pltpu.CompilerParams(collective_id=0, has_side_effects=True),
    )(back, table, weight, field, bias)


def greet_slab(parts):
    me = lax.axis_index("slab")
    member = lax.axis_index("member")
    barrier = pltpu.get_barrier_semaphore()
    for step in range(1, parts):
        peer = lax.rem(me + step, parts)
        pl.semaphore_signal(barrier, inc=1, device_id=(member, peer), device_id_type=pl.DeviceIdType.MESH)
    return barrier


def swap_blocks(parts, source_ref, out_ref, landed, send_sems, recv_sems):
    me = lax.axis_index("slab")
    member = lax.axis_index("member")

    def copy_of(source, target, peer):
        return pltpu.make_async_remote_copy(
            src_ref=source_ref.at[source],
            dst_ref=landed.at[target],
            send_sem=send_sems.at[source],
            recv_sem=recv_sems.at[target],
            device_id=(member, peer),
            device_id_type=pl.DeviceIdType.MESH,
        )

    for step in range(1, parts):
        peer = lax.rem(me + step, parts)
        copy_of(peer, me, peer).start()
    landed[me] = source_ref[me]
    for step in range(1, parts):
        source = lax.rem(me + parts - step, parts)
        copy_of(source, source, source).wait_recv()
    for step in range(1, parts):
        peer = lax.rem(me + step, parts)
        copy_of(peer, me, peer).wait_send()
    out_ref[...] = landed[...]


def slab_exchange_kernel(parts, blocks_ref, out_ref, landed, send_sems, recv_sems):
    barrier = greet_slab(parts)
    pl.semaphore_wait(barrier, parts - 1)
    swap_blocks(parts, blocks_ref, out_ref, landed, send_sems, recv_sems)


def mode_mix_kernel(parts, pencil_ref, xcos_ref, xsin_ref, xcos_t_ref, xsin_t_ref, swap_ref, weight_ref,
                    keep_ref, out_ref, expanded, blocks, landed, send_sems, recv_sems):
    barrier = greet_slab(parts)
    pencil = pencil_ref[...]
    swapped = jnp.dot(pencil, swap_ref[...], preferred_element_type=jnp.float32).astype(pencil.dtype)
    spec = jnp.dot(xcos_ref[...], pencil, preferred_element_type=jnp.float32)
    spec = spec + jnp.dot(xsin_ref[...], swapped, preferred_element_type=jnp.float32)
    spec = spec.astype(pencil.dtype).astype(jnp.float32)
    modes, width = spec.shape
    rows = lax.broadcasted_iota(jnp.int32, spec.shape, 0)
    for mode in range(modes):
        lanes = pl.ds(mode * width, width)
        expanded[:, lanes] = jnp.where(rows == mode, spec, 0.0).astype(expanded.dtype)
    mixed = jnp.dot(expanded[...], weight_ref[...], preferred_element_type=jnp.float32)
    mixed = (mixed * keep_ref[...]).astype(pencil.dtype)
    mixed_swapped = jnp.dot(mixed, swap_ref[...], preferred_element_type=jnp.float32).astype(pencil.dtype)
    back = jnp.dot(xcos_t_ref[...], mixed, preferred_element_type=jnp.float32)
    back = back - jnp.dot(xsin_t_ref[...], mixed_swapped, preferred_element_type=jnp.float32)
    blocks[...] = back.reshape(blocks.shape).astype(blocks.dtype)
    pl.semaphore_wait(barrier, parts - 1)
    swap_blocks(parts, blocks, out_ref, landed, send_sems, recv_sems)


def mode_mix_exchange(pencil, xcos, xsin, swap, weight, keep, parts):
    points, width = pencil.shape
    modes = xcos.shape[0]
    shape = (parts, points // parts, width)
    return pl.pallas_call(
        functools.partial(mode_mix_kernel, parts),
        out_shape=jax.ShapeDtypeStruct(shape, pencil.dtype),
        in_specs=[pl.BlockSpec(memory_space=pltpu.VMEM)] * 8,
        out_specs=pl.BlockSpec(memory_space=pltpu.VMEM),
        scratch_shapes=[
            pltpu.VMEM((modes, modes * width), pencil.dtype),
            pltpu.VMEM(shape, pencil.dtype),
            pltpu.VMEM(shape, pencil.dtype),
            pltpu.SemaphoreType.DMA((parts,)),
            pltpu.SemaphoreType.DMA((parts,)),
        ],
        compiler_params=pltpu.CompilerParams(collective_id=2, has_side_effects=True),
    )(pencil, xcos, xsin, xcos.T, xsin.T, swap, weight, keep)


def slab_exchange(blocks, parts, exchange_id):
    return pl.pallas_call(
        functools.partial(slab_exchange_kernel, parts),
        out_shape=jax.ShapeDtypeStruct(blocks.shape, blocks.dtype),
        in_specs=[pl.BlockSpec(memory_space=pltpu.VMEM)],
        out_specs=pl.BlockSpec(memory_space=pltpu.VMEM),
        scratch_shapes=[
            pltpu.VMEM(blocks.shape, blocks.dtype),
            pltpu.SemaphoreType.DMA((parts,)),
            pltpu.SemaphoreType.DMA((parts,)),
        ],
        compiler_params=pltpu.CompilerParams(collective_id=exchange_id, has_side_effects=True),
    )(blocks)


def local(
    base_field,
    forcing,
    load,
    amplitudes,
    amp_index,
    mode_count,
    point_weight,
    point_bias,
    spectral_weight,
):
    channels, slab_rows, plane_count, length_y = base_field.shape
    slab_count = lax.axis_size("slab")
    local_modes = spectral_weight.shape[0]
    modes_y = local_modes * slab_count
    modes_x = spectral_weight.shape[1]
    length_x = slab_rows * slab_count
    packed_width = 2 * channels * plane_count
    slab_index = lax.axis_index("slab")
    level_ids = jnp.arange(amplitudes.shape[0], dtype=jnp.int32)
    amplitude = jnp.sum(jnp.where(level_ids == amp_index[0], amplitudes, 0.0))
    driven = base_field.astype(jnp.float32) + amplitude * load[:, None, None, None] * forcing[
        None
    ].astype(jnp.float32)
    field_now = (2.0 * jnp.tanh(0.5 * driven)).astype(jnp.bfloat16)
    y_cos, y_sin = phases(
        jnp.arange(modes_y, dtype=jnp.int32), jnp.arange(length_y, dtype=jnp.int32), length_y
    )
    y_real = jnp.einsum(
        "cxzy,ky->kxcz", field_now, y_cos.astype(jnp.bfloat16), preferred_element_type=jnp.float32
    )
    y_imag = -jnp.einsum(
        "cxzy,ky->kxcz", field_now, y_sin.astype(jnp.bfloat16), preferred_element_type=jnp.float32
    )
    packed = (
        jnp.stack([y_real, y_imag], axis=2)
        .transpose(0, 1, 4, 2, 3)
        .astype(jnp.bfloat16)
        .reshape(modes_y, slab_rows, packed_width)
    )
    frequency_x = jnp.concatenate(
        [
            jnp.arange(modes_x // 2, dtype=jnp.int32),
            jnp.arange(length_x - modes_x // 2, length_x, dtype=jnp.int32),
        ]
    )
    full_cos, full_sin = phases(frequency_x, jnp.arange(length_x, dtype=jnp.int32), length_x)
    full_cos = full_cos.astype(jnp.bfloat16)
    full_sin = full_sin.astype(jnp.bfloat16)
    gathered = slab_exchange(packed, slab_count, 1).reshape(length_x, packed_width)
    lane = jnp.arange(packed_width, dtype=jnp.int32)
    real_lane = (lane // channels) % 2 == 0
    swap = jnp.where(
        real_lane[None, :],
        (lane[:, None] == lane[None, :] + channels).astype(jnp.float32),
        -(lane[:, None] == lane[None, :] - channels).astype(jnp.float32),
    ).astype(jnp.bfloat16)
    signs = jnp.array(
        [[[1.0, 0.0], [0.0, 1.0]], [[0.0, 1.0], [-1.0, 0.0]]], dtype=jnp.bfloat16
    )
    planes = jnp.eye(plane_count, dtype=jnp.bfloat16)
    weight = jnp.einsum(
        "qwoi,wab,zy->qzaiybo", spectral_weight[0], signs, planes,
        preferred_element_type=jnp.float32,
    ).astype(jnp.bfloat16).reshape(modes_x * packed_width, packed_width)
    kept = (slab_index * local_modes < mode_count[0]).astype(jnp.float32)
    keep = jnp.full((1, packed_width), kept, jnp.float32)
    returned = mode_mix_exchange(gathered, full_cos, full_sin, swap, weight, keep, slab_count)
    returned = returned.reshape(modes_y, slab_rows, plane_count, 2, channels)
    weights_y = jnp.where(jnp.arange(modes_y) == 0, 1.0, 2.0).astype(jnp.float32) / (
        length_x * length_y
    )
    back_cos = (weights_y[:, None] * y_cos).astype(jnp.bfloat16)
    back_sin = (weights_y[:, None] * y_sin).astype(jnp.bfloat16)
    table = jnp.concatenate([back_cos, -back_sin], axis=0)
    cells = slab_rows * plane_count
    back = returned.transpose(1, 2, 4, 3, 0).reshape(cells, channels, 2 * modes_y)
    bias = point_bias.reshape(channels, 1)
    field_rows = field_now.reshape(channels, cells * length_y)
    members = lax.axis_size("member")
    total = layer_sum(back, table, point_weight, field_rows, bias, members)
    return total.reshape(channels // members, slab_rows, plane_count, length_y)


def solution(mesh):
    in_specs = (
        P(None, "slab", None, None),
        P("slab", None, None),
        P(),
        P(),
        P("member"),
        P("member"),
        P(),
        P(),
        P("slab", None, None, None, None),
    )
    out_specs = P("member", "slab", None, None)
    return jax.shard_map(local, mesh=mesh, in_specs=in_specs, out_specs=out_specs, check_vma=False)
```

```python
import functools
import math

import jax
import jax.numpy as jnp
from jax import lax
from jax.experimental import pallas as pl
from jax.experimental.pallas import tpu as pltpu
from jax.sharding import PartitionSpec as P

TWO_PI = 2.0 * math.pi


def phases(frequency, positions, length):
    product = frequency[:, None] * positions[None, :] % length
    angles = product.astype(jnp.float32) * (TWO_PI / length)
    return (jnp.cos(angles), jnp.sin(angles))


def forward_x(pencil, cos_table, sin_table):
    row_total = pencil.shape[0]
    modes = cos_table.shape[0]
    with_cos = jnp.einsum(
        "kxf,mx->kmf", pencil, cos_table, preferred_element_type=jnp.float32
    ).reshape(row_total, modes, 2, -1)
    with_sin = jnp.einsum(
        "kxf,mx->kmf", pencil, sin_table, preferred_element_type=jnp.float32
    ).reshape(row_total, modes, 2, -1)
    real_part = with_cos[:, :, 0] + with_sin[:, :, 1]
    imag_part = with_cos[:, :, 1] - with_sin[:, :, 0]
    return jnp.stack([real_part, imag_part], axis=2).reshape(row_total, modes, -1)


def inverse_x(spectra, cos_table, sin_table):
    row_total = spectra.shape[0]
    points = cos_table.shape[1]
    with_cos = jnp.einsum(
        "kmf,mx->kxf", spectra, cos_table, preferred_element_type=jnp.float32
    ).reshape(row_total, points, 2, -1)
    with_sin = jnp.einsum(
        "kmf,mx->kxf", spectra, sin_table, preferred_element_type=jnp.float32
    ).reshape(row_total, points, 2, -1)
    real_part = with_cos[:, :, 0] - with_sin[:, :, 1]
    imag_part = with_cos[:, :, 1] + with_sin[:, :, 0]
    return jnp.stack([real_part, imag_part], axis=2).reshape(row_total, points, -1)


def mixing(weights, values):
    return jnp.einsum("kmoi,kmiz->kmoz", weights, values, preferred_element_type=jnp.float32)


def layer_sum_kernel(members, back_ref, table_ref, weight_ref, field_ref, bias_ref, out_ref, value, layer,
                     near, part, far, near_sems, far_send, far_recv):
    me = lax.axis_index("member")
    slab = lax.axis_index("slab")
    chips = members // 2
    chip, core = me // 2, me % 2
    sibling = chip * 2 + 1 - core
    mesh_kind = pl.DeviceIdType.MESH
    barrier = pltpu.get_barrier_semaphore()
    pl.semaphore_signal(barrier, inc=1, device_id=(sibling, slab), device_id_type=mesh_kind)
    for step in range(1, chips):
        peer = lax.rem(chip + step, chips) * 2 + core
        pl.semaphore_signal(barrier, inc=1, device_id=(peer, slab), device_id_type=mesh_kind)
    cells = back_ref.shape[0]
    length = table_ref.shape[1]
    block_rows = layer.shape[2]
    for cell in range(cells):
        lanes = pl.ds(cell * length, length)
        spectral = jnp.dot(back_ref[cell], table_ref[...], preferred_element_type=jnp.float32)
        pointwise = jnp.dot(weight_ref[...], field_ref[:, lanes], preferred_element_type=jnp.float32)
        value[:, lanes] = jax.nn.gelu(pointwise + bias_ref[...] + spectral, approximate=True)
    for block in range(members):
        rows = pl.ds(block * block_rows, block_rows)
        layer[block % 2, block // 2] = value[rows, :].astype(layer.dtype)
    pl.semaphore_wait(barrier, chips)

    on_chip = pltpu.make_async_remote_copy(
        src_ref=layer.at[1 - core],
        dst_ref=near,
        send_sem=near_sems.at[0],
        recv_sem=near_sems.at[1],
        device_id=(sibling, slab),
        device_id_type=mesh_kind,
    )
    on_chip.start()
    on_chip.wait_recv()
    for index in range(chips):
        pair = layer[core, index].astype(jnp.float32) + near[index].astype(jnp.float32)
        part[index] = pair.astype(part.dtype)
    on_chip.wait_send()

    def copy_of(source, target, peer_chip):
        return pltpu.make_async_remote_copy(
            src_ref=part.at[source],
            dst_ref=far.at[target],
            send_sem=far_send.at[source],
            recv_sem=far_recv.at[target],
            device_id=(peer_chip * 2 + core, slab),
            device_id_type=mesh_kind,
        )

    for step in range(1, chips):
        peer = lax.rem(chip + step, chips)
        copy_of(peer, chip, peer).start()
    total = part[chip].astype(jnp.float32)
    for step in range(1, chips):
        source = lax.rem(chip + chips - step, chips)
        copy_of(source, source, source).wait_recv()
        total = total + far[source].astype(jnp.float32)
    for step in range(1, chips):
        peer = lax.rem(chip + step, chips)
        copy_of(peer, chip, peer).wait_send()
    out_ref[...] = (total / members).astype(out_ref.dtype)


def layer_sum(back, table, weight, field, bias, members):
    channels, width = field.shape
    block_rows = channels // members
    chips = members // 2
    return pl.pallas_call(
        functools.partial(layer_sum_kernel, members),
        out_shape=jax.ShapeDtypeStruct((block_rows, width), jnp.bfloat16),
        in_specs=[pl.BlockSpec(memory_space=pltpu.VMEM)] * 5,
        out_specs=pl.BlockSpec(memory_space=pltpu.VMEM),
        scratch_shapes=[
            pltpu.VMEM((channels, width), jnp.float32),
            pltpu.VMEM((2, chips, block_rows, width), jnp.bfloat16),
            pltpu.VMEM((chips, block_rows, width), jnp.bfloat16),
            pltpu.VMEM((chips, block_rows, width), jnp.bfloat16),
            pltpu.VMEM((chips, block_rows, width), jnp.bfloat16),
            pltpu.SemaphoreType.DMA((2,)),
            pltpu.SemaphoreType.DMA((chips,)),
            pltpu.SemaphoreType.DMA((chips,)),
        ],
        compiler_params=pltpu.CompilerParams(collective_id=0, has_side_effects=True),
    )(back, table, weight, field, bias)


def greet_slab(parts):
    me = lax.axis_index("slab")
    member = lax.axis_index("member")
    barrier = pltpu.get_barrier_semaphore()
    for step in range(1, parts):
        peer = lax.rem(me + step, parts)
        pl.semaphore_signal(barrier, inc=1, device_id=(member, peer), device_id_type=pl.DeviceIdType.MESH)
    return barrier


def swap_blocks(parts, source_ref, out_ref, landed, send_sems, recv_sems):
    me = lax.axis_index("slab")
    member = lax.axis_index("member")

    def copy_of(source, target, peer):
        return pltpu.make_async_remote_copy(
            src_ref=source_ref.at[source],
            dst_ref=landed.at[target],
            send_sem=send_sems.at[source],
            recv_sem=recv_sems.at[target],
            device_id=(member, peer),
            device_id_type=pl.DeviceIdType.MESH,
        )

    for step in range(1, parts):
        peer = lax.rem(me + step, parts)
        copy_of(peer, me, peer).start()
    landed[me] = source_ref[me]
    for step in range(1, parts):
        source = lax.rem(me + parts - step, parts)
        copy_of(source, source, source).wait_recv()
    for step in range(1, parts):
        peer = lax.rem(me + step, parts)
        copy_of(peer, me, peer).wait_send()
    out_ref[...] = landed[...]


def slab_exchange_kernel(parts, blocks_ref, out_ref, landed, send_sems, recv_sems):
    barrier = greet_slab(parts)
    pl.semaphore_wait(barrier, parts - 1)
    swap_blocks(parts, blocks_ref, out_ref, landed, send_sems, recv_sems)


def mode_mix_kernel(parts, pencil_t_ref, xcos_t_ref, xsin_t_ref, swap_t_ref, weight_ref, keep_ref, out_ref,
                    mixed_t, blocks, landed, send_sems, recv_sems):
    barrier = greet_slab(parts)
    pencil_t = pencil_t_ref[...]
    swap_t = swap_t_ref[...]
    swapped_t = jnp.dot(swap_t, pencil_t, preferred_element_type=jnp.float32).astype(pencil_t.dtype)
    spec_t = jnp.dot(pencil_t, xcos_t_ref[...], preferred_element_type=jnp.float32)
    spec_t = spec_t + jnp.dot(swapped_t, xsin_t_ref[...], preferred_element_type=jnp.float32)
    spec_t = spec_t.astype(pencil_t.dtype).astype(jnp.float32)
    outputs = weight_ref.shape[1]
    planes = spec_t.shape[0] // (2 * outputs)
    for plane in range(planes):
        base = plane * 2 * outputs
        real = spec_t[base:base + outputs, :]
        imag = spec_t[base + outputs:base + 2 * outputs, :]
        for out in range(outputs):
            weight_real = weight_ref[0, out].astype(jnp.float32)
            weight_imag = weight_ref[1, out].astype(jnp.float32)
            mixed_t[pl.ds(base + out, 1), :] = jnp.sum(
                weight_real * real - weight_imag * imag, axis=0, keepdims=True
            )
            mixed_t[pl.ds(base + outputs + out, 1), :] = jnp.sum(
                weight_imag * real + weight_real * imag, axis=0, keepdims=True
            )
    mixed = (mixed_t[...] * keep_ref[...]).astype(pencil_t.dtype)
    mixed_swapped = jnp.dot(swap_t, mixed, preferred_element_type=jnp.float32).astype(pencil_t.dtype)
    contract = (((1,), (1,)), ((), ()))
    back = lax.dot_general(xcos_t_ref[...], mixed, contract, preferred_element_type=jnp.float32)
    back = back - lax.dot_general(
        xsin_t_ref[...], mixed_swapped, contract, preferred_element_type=jnp.float32
    )
    blocks[...] = back.reshape(blocks.shape).astype(blocks.dtype)
    pl.semaphore_wait(barrier, parts - 1)
    swap_blocks(parts, blocks, out_ref, landed, send_sems, recv_sems)


def mode_mix_exchange(pencil, xcos, xsin, swap, weight, keep, parts):
    points, width = pencil.shape
    modes = xcos.shape[0]
    shape = (parts, points // parts, width)
    return pl.pallas_call(
        functools.partial(mode_mix_kernel, parts),
        out_shape=jax.ShapeDtypeStruct(shape, pencil.dtype),
        in_specs=[pl.BlockSpec(memory_space=pltpu.VMEM)] * 6,
        out_specs=pl.BlockSpec(memory_space=pltpu.VMEM),
        scratch_shapes=[
            pltpu.VMEM((width, modes), jnp.float32),
            pltpu.VMEM(shape, pencil.dtype),
            pltpu.VMEM(shape, pencil.dtype),
            pltpu.SemaphoreType.DMA((parts,)),
            pltpu.SemaphoreType.DMA((parts,)),
        ],
        compiler_params=pltpu.CompilerParams(collective_id=2, has_side_effects=True),
    )(pencil.T, xcos.T, xsin.T, swap.T, weight, keep)


def slab_exchange(blocks, parts, exchange_id):
    return pl.pallas_call(
        functools.partial(slab_exchange_kernel, parts),
        out_shape=jax.ShapeDtypeStruct(blocks.shape, blocks.dtype),
        in_specs=[pl.BlockSpec(memory_space=pltpu.VMEM)],
        out_specs=pl.BlockSpec(memory_space=pltpu.VMEM),
        scratch_shapes=[
            pltpu.VMEM(blocks.shape, blocks.dtype),
            pltpu.SemaphoreType.DMA((parts,)),
            pltpu.SemaphoreType.DMA((parts,)),
        ],
        compiler_params=pltpu.CompilerParams(collective_id=exchange_id, has_side_effects=True),
    )(blocks)


def local(
    base_field,
    forcing,
    load,
    amplitudes,
    amp_index,
    mode_count,
    point_weight,
    point_bias,
    spectral_weight,
):
    channels, slab_rows, plane_count, length_y = base_field.shape
    slab_count = lax.axis_size("slab")
    local_modes = spectral_weight.shape[0]
    modes_y = local_modes * slab_count
    modes_x = spectral_weight.shape[1]
    length_x = slab_rows * slab_count
    packed_width = 2 * channels * plane_count
    slab_index = lax.axis_index("slab")
    level_ids = jnp.arange(amplitudes.shape[0], dtype=jnp.int32)
    amplitude = jnp.sum(jnp.where(level_ids == amp_index[0], amplitudes, 0.0))
    driven = base_field.astype(jnp.float32) + amplitude * load[:, None, None, None] * forcing[
        None
    ].astype(jnp.float32)
    field_now = (2.0 * jnp.tanh(0.5 * driven)).astype(jnp.bfloat16)
    y_cos, y_sin = phases(
        jnp.arange(modes_y, dtype=jnp.int32), jnp.arange(length_y, dtype=jnp.int32), length_y
    )
    y_real = jnp.einsum(
        "cxzy,ky->kxcz", field_now, y_cos.astype(jnp.bfloat16), preferred_element_type=jnp.float32
    )
    y_imag = -jnp.einsum(
        "cxzy,ky->kxcz", field_now, y_sin.astype(jnp.bfloat16), preferred_element_type=jnp.float32
    )
    packed = (
        jnp.stack([y_real, y_imag], axis=2)
        .transpose(0, 1, 4, 2, 3)
        .astype(jnp.bfloat16)
        .reshape(modes_y, slab_rows, packed_width)
    )
    frequency_x = jnp.concatenate(
        [
            jnp.arange(modes_x // 2, dtype=jnp.int32),
            jnp.arange(length_x - modes_x // 2, length_x, dtype=jnp.int32),
        ]
    )
    full_cos, full_sin = phases(frequency_x, jnp.arange(length_x, dtype=jnp.int32), length_x)
    full_cos = full_cos.astype(jnp.bfloat16)
    full_sin = full_sin.astype(jnp.bfloat16)
    gathered = slab_exchange(packed, slab_count, 1).reshape(length_x, packed_width)
    lane = jnp.arange(packed_width, dtype=jnp.int32)
    real_lane = (lane // channels) % 2 == 0
    swap = jnp.where(
        real_lane[None, :],
        (lane[:, None] == lane[None, :] + channels).astype(jnp.float32),
        -(lane[:, None] == lane[None, :] - channels).astype(jnp.float32),
    ).astype(jnp.bfloat16)
    weight = spectral_weight[0].transpose(1, 2, 3, 0)
    kept = (slab_index * local_modes < mode_count[0]).astype(jnp.float32)
    keep = jnp.full((1, modes_x), kept, jnp.float32)
    returned = mode_mix_exchange(gathered, full_cos, full_sin, swap, weight, keep, slab_count)
    returned = returned.reshape(modes_y, slab_rows, plane_count, 2, channels)
    weights_y = jnp.where(jnp.arange(modes_y) == 0, 1.0, 2.0).astype(jnp.float32) / (
        length_x * length_y
    )
    back_cos = (weights_y[:, None] * y_cos).astype(jnp.bfloat16)
    back_sin = (weights_y[:, None] * y_sin).astype(jnp.bfloat16)
    table = jnp.concatenate([back_cos, -back_sin], axis=0)
    cells = slab_rows * plane_count
    back = returned.transpose(1, 2, 4, 3, 0).reshape(cells, channels, 2 * modes_y)
    bias = point_bias.reshape(channels, 1)
    field_rows = field_now.reshape(channels, cells * length_y)
    members = lax.axis_size("member")
    total = layer_sum(back, table, point_weight, field_rows, bias, members)
    return total.reshape(channels // members, slab_rows, plane_count, length_y)


def solution(mesh):
    in_specs = (
        P(None, "slab", None, None),
        P("slab", None, None),
        P(),
        P(),
        P("member"),
        P("member"),
        P(),
        P(),
        P("slab", None, None, None, None),
    )
    out_specs = P("member", "slab", None, None)
    return jax.shard_map(local, mesh=mesh, in_specs=in_specs, out_specs=out_specs, check_vma=False)
```

```python
import functools
import math

import jax
import ml_dtypes
import numpy as np
import jax.numpy as jnp
from jax import lax
from jax.experimental import pallas as pl
from jax.experimental.pallas import tpu as pltpu
from jax.sharding import PartitionSpec as P

TWO_PI = 2.0 * math.pi


def phase_tables(frequency, positions, length):
    product = np.outer(frequency, positions) % length
    angles = (product.astype(np.float32) * np.float32(TWO_PI / length)).astype(np.float64)
    return np.cos(angles).astype(np.float32), np.sin(angles).astype(np.float32)


def bf16_constant(values):
    return jnp.asarray(np.asarray(values, np.float32).astype(ml_dtypes.bfloat16))


def phases(frequency, positions, length):
    product = frequency[:, None] * positions[None, :] % length
    angles = product.astype(jnp.float32) * (TWO_PI / length)
    return (jnp.cos(angles), jnp.sin(angles))


def forward_x(pencil, cos_table, sin_table):
    row_total = pencil.shape[0]
    modes = cos_table.shape[0]
    with_cos = jnp.einsum(
        "kxf,mx->kmf", pencil, cos_table, preferred_element_type=jnp.float32
    ).reshape(row_total, modes, 2, -1)
    with_sin = jnp.einsum(
        "kxf,mx->kmf", pencil, sin_table, preferred_element_type=jnp.float32
    ).reshape(row_total, modes, 2, -1)
    real_part = with_cos[:, :, 0] + with_sin[:, :, 1]
    imag_part = with_cos[:, :, 1] - with_sin[:, :, 0]
    return jnp.stack([real_part, imag_part], axis=2).reshape(row_total, modes, -1)


def inverse_x(spectra, cos_table, sin_table):
    row_total = spectra.shape[0]
    points = cos_table.shape[1]
    with_cos = jnp.einsum(
        "kmf,mx->kxf", spectra, cos_table, preferred_element_type=jnp.float32
    ).reshape(row_total, points, 2, -1)
    with_sin = jnp.einsum(
        "kmf,mx->kxf", spectra, sin_table, preferred_element_type=jnp.float32
    ).reshape(row_total, points, 2, -1)
    real_part = with_cos[:, :, 0] - with_sin[:, :, 1]
    imag_part = with_cos[:, :, 1] + with_sin[:, :, 0]
    return jnp.stack([real_part, imag_part], axis=2).reshape(row_total, points, -1)


def mixing(weights, values):
    return jnp.einsum("kmoi,kmiz->kmoz", weights, values, preferred_element_type=jnp.float32)


def layer_sum_kernel(members, back_ref, table_ref, weight_ref, field_ref, bias_ref, out_ref, value, layer,
                     near, part, far, near_sems, far_send, far_recv):
    me = lax.axis_index("member")
    slab = lax.axis_index("slab")
    chips = members // 2
    chip, core = me // 2, me % 2
    sibling = chip * 2 + 1 - core
    mesh_kind = pl.DeviceIdType.MESH
    barrier = pltpu.get_barrier_semaphore()
    pl.semaphore_signal(barrier, inc=1, device_id=(sibling, slab), device_id_type=mesh_kind)
    for step in range(1, chips):
        peer = lax.rem(chip + step, chips) * 2 + core
        pl.semaphore_signal(barrier, inc=1, device_id=(peer, slab), device_id_type=mesh_kind)
    cells = back_ref.shape[0]
    length = table_ref.shape[1]
    block_rows = layer.shape[2]
    for cell in range(cells):
        lanes = pl.ds(cell * length, length)
        spectral = jnp.dot(back_ref[cell], table_ref[...], preferred_element_type=jnp.float32)
        pointwise = jnp.dot(weight_ref[...], field_ref[:, lanes], preferred_element_type=jnp.float32)
        value[:, lanes] = jax.nn.gelu(pointwise + bias_ref[...] + spectral, approximate=True)
    for block in range(members):
        rows = pl.ds(block * block_rows, block_rows)
        layer[block % 2, block // 2] = value[rows, :].astype(layer.dtype)
    pl.semaphore_wait(barrier, chips)

    on_chip = pltpu.make_async_remote_copy(
        src_ref=layer.at[1 - core],
        dst_ref=near,
        send_sem=near_sems.at[0],
        recv_sem=near_sems.at[1],
        device_id=(sibling, slab),
        device_id_type=mesh_kind,
    )
    on_chip.start()
    on_chip.wait_recv()
    for index in range(chips):
        pair = layer[core, index].astype(jnp.float32) + near[index].astype(jnp.float32)
        part[index] = pair.astype(part.dtype)
    on_chip.wait_send()

    def copy_of(source, target, peer_chip):
        return pltpu.make_async_remote_copy(
            src_ref=part.at[source],
            dst_ref=far.at[target],
            send_sem=far_send.at[source],
            recv_sem=far_recv.at[target],
            device_id=(peer_chip * 2 + core, slab),
            device_id_type=mesh_kind,
        )

    for step in range(1, chips):
        peer = lax.rem(chip + step, chips)
        copy_of(peer, chip, peer).start()
    total = part[chip].astype(jnp.float32)
    for step in range(1, chips):
        source = lax.rem(chip + chips - step, chips)
        copy_of(source, source, source).wait_recv()
        total = total + far[source].astype(jnp.float32)
    for step in range(1, chips):
        peer = lax.rem(chip + step, chips)
        copy_of(peer, chip, peer).wait_send()
    out_ref[...] = (total / members).astype(out_ref.dtype)


def layer_sum(back, table, weight, field, bias, members):
    channels, width = field.shape
    block_rows = channels // members
    chips = members // 2
    return pl.pallas_call(
        functools.partial(layer_sum_kernel, members),
        out_shape=jax.ShapeDtypeStruct((block_rows, width), jnp.bfloat16),
        in_specs=[pl.BlockSpec(memory_space=pltpu.VMEM)] * 5,
        out_specs=pl.BlockSpec(memory_space=pltpu.VMEM),
        scratch_shapes=[
            pltpu.VMEM((channels, width), jnp.float32),
            pltpu.VMEM((2, chips, block_rows, width), jnp.bfloat16),
            pltpu.VMEM((chips, block_rows, width), jnp.bfloat16),
            pltpu.VMEM((chips, block_rows, width), jnp.bfloat16),
            pltpu.VMEM((chips, block_rows, width), jnp.bfloat16),
            pltpu.SemaphoreType.DMA((2,)),
            pltpu.SemaphoreType.DMA((chips,)),
            pltpu.SemaphoreType.DMA((chips,)),
        ],
        compiler_params=pltpu.CompilerParams(collective_id=0, has_side_effects=True),
    )(back, table, weight, field, bias)


def greet_slab(parts):
    me = lax.axis_index("slab")
    member = lax.axis_index("member")
    barrier = pltpu.get_barrier_semaphore()
    for step in range(1, parts):
        peer = lax.rem(me + step, parts)
        pl.semaphore_signal(barrier, inc=1, device_id=(member, peer), device_id_type=pl.DeviceIdType.MESH)
    return barrier


def swap_blocks(parts, source_ref, out_ref, landed, send_sems, recv_sems):
    me = lax.axis_index("slab")
    member = lax.axis_index("member")

    def copy_of(source, target, peer):
        return pltpu.make_async_remote_copy(
            src_ref=source_ref.at[source],
            dst_ref=landed.at[target],
            send_sem=send_sems.at[source],
            recv_sem=recv_sems.at[target],
            device_id=(member, peer),
            device_id_type=pl.DeviceIdType.MESH,
        )

    for step in range(1, parts):
        peer = lax.rem(me + step, parts)
        copy_of(peer, me, peer).start()
    landed[me] = source_ref[me]
    for step in range(1, parts):
        source = lax.rem(me + parts - step, parts)
        copy_of(source, source, source).wait_recv()
    for step in range(1, parts):
        peer = lax.rem(me + step, parts)
        copy_of(peer, me, peer).wait_send()
    out_ref[...] = landed[...]


def slab_exchange_kernel(parts, blocks_ref, out_ref, landed, send_sems, recv_sems):
    barrier = greet_slab(parts)
    pl.semaphore_wait(barrier, parts - 1)
    swap_blocks(parts, blocks_ref, out_ref, landed, send_sems, recv_sems)


def mode_mix_kernel(parts, pencil_t_ref, xcos_t_ref, xsin_t_ref, swap_t_ref, weight_ref, keep_ref, out_ref,
                    mixed_t, blocks, landed, send_sems, recv_sems):
    barrier = greet_slab(parts)
    pencil_t = pencil_t_ref[...]
    swap_t = swap_t_ref[...]
    swapped_t = jnp.dot(swap_t, pencil_t, preferred_element_type=jnp.float32).astype(pencil_t.dtype)
    spec_t = jnp.dot(pencil_t, xcos_t_ref[...], preferred_element_type=jnp.float32)
    spec_t = spec_t + jnp.dot(swapped_t, xsin_t_ref[...], preferred_element_type=jnp.float32)
    spec_t = spec_t.astype(pencil_t.dtype).astype(jnp.float32)
    outputs = weight_ref.shape[1]
    planes = spec_t.shape[0] // (2 * outputs)
    for plane in range(planes):
        base = plane * 2 * outputs
        real = spec_t[base:base + outputs, :]
        imag = spec_t[base + outputs:base + 2 * outputs, :]
        for out in range(outputs):
            weight_real = weight_ref[0, out].astype(jnp.float32)
            weight_imag = weight_ref[1, out].astype(jnp.float32)
            mixed_t[pl.ds(base + out, 1), :] = jnp.sum(
                weight_real * real - weight_imag * imag, axis=0, keepdims=True
            )
            mixed_t[pl.ds(base + outputs + out, 1), :] = jnp.sum(
                weight_imag * real + weight_real * imag, axis=0, keepdims=True
            )
    mixed = (mixed_t[...] * keep_ref[...]).astype(pencil_t.dtype)
    mixed_swapped = jnp.dot(swap_t, mixed, preferred_element_type=jnp.float32).astype(pencil_t.dtype)
    contract = (((1,), (1,)), ((), ()))
    back = lax.dot_general(xcos_t_ref[...], mixed, contract, preferred_element_type=jnp.float32)
    back = back - lax.dot_general(
        xsin_t_ref[...], mixed_swapped, contract, preferred_element_type=jnp.float32
    )
    blocks[...] = back.reshape(blocks.shape).astype(blocks.dtype)
    pl.semaphore_wait(barrier, parts - 1)
    swap_blocks(parts, blocks, out_ref, landed, send_sems, recv_sems)


def mode_mix_exchange(pencil, xcos_t, xsin_t, swap_t, weight, keep, parts):
    points, width = pencil.shape
    modes = xcos_t.shape[1]
    shape = (parts, points // parts, width)
    return pl.pallas_call(
        functools.partial(mode_mix_kernel, parts),
        out_shape=jax.ShapeDtypeStruct(shape, pencil.dtype),
        in_specs=[pl.BlockSpec(memory_space=pltpu.VMEM)] * 6,
        out_specs=pl.BlockSpec(memory_space=pltpu.VMEM),
        scratch_shapes=[
            pltpu.VMEM((width, modes), jnp.float32),
            pltpu.VMEM(shape, pencil.dtype),
            pltpu.VMEM(shape, pencil.dtype),
            pltpu.SemaphoreType.DMA((parts,)),
            pltpu.SemaphoreType.DMA((parts,)),
        ],
        compiler_params=pltpu.CompilerParams(collective_id=2, has_side_effects=True),
    )(pencil.T, xcos_t, xsin_t, swap_t, weight, keep)


def slab_exchange(blocks, parts, exchange_id):
    return pl.pallas_call(
        functools.partial(slab_exchange_kernel, parts),
        out_shape=jax.ShapeDtypeStruct(blocks.shape, blocks.dtype),
        in_specs=[pl.BlockSpec(memory_space=pltpu.VMEM)],
        out_specs=pl.BlockSpec(memory_space=pltpu.VMEM),
        scratch_shapes=[
            pltpu.VMEM(blocks.shape, blocks.dtype),
            pltpu.SemaphoreType.DMA((parts,)),
            pltpu.SemaphoreType.DMA((parts,)),
        ],
        compiler_params=pltpu.CompilerParams(collective_id=exchange_id, has_side_effects=True),
    )(blocks)


def local(
    base_field,
    forcing,
    load,
    amplitudes,
    amp_index,
    mode_count,
    point_weight,
    point_bias,
    spectral_weight,
):
    channels, slab_rows, plane_count, length_y = base_field.shape
    slab_count = lax.axis_size("slab")
    local_modes = spectral_weight.shape[0]
    modes_y = local_modes * slab_count
    modes_x = spectral_weight.shape[1]
    length_x = slab_rows * slab_count
    packed_width = 2 * channels * plane_count
    slab_index = lax.axis_index("slab")
    level_ids = jnp.arange(amplitudes.shape[0], dtype=jnp.int32)
    amplitude = jnp.sum(jnp.where(level_ids == amp_index[0], amplitudes, 0.0))
    driven = base_field.astype(jnp.float32) + amplitude * load[:, None, None, None] * forcing[
        None
    ].astype(jnp.float32)
    field_now = (2.0 * jnp.tanh(0.5 * driven)).astype(jnp.bfloat16)
    y_cos, y_sin = phase_tables(np.arange(modes_y), np.arange(length_y), length_y)
    y_real = jnp.einsum(
        "cxzy,ky->kxcz", field_now, bf16_constant(y_cos), preferred_element_type=jnp.float32
    )
    y_imag = -jnp.einsum(
        "cxzy,ky->kxcz", field_now, bf16_constant(y_sin), preferred_element_type=jnp.float32
    )
    packed = (
        jnp.stack([y_real, y_imag], axis=2)
        .transpose(0, 1, 4, 2, 3)
        .astype(jnp.bfloat16)
        .reshape(modes_y, slab_rows, packed_width)
    )
    frequency_x = np.concatenate(
        [np.arange(modes_x // 2), np.arange(length_x - modes_x // 2, length_x)]
    )
    full_cos, full_sin = phase_tables(frequency_x, np.arange(length_x), length_x)
    gathered = slab_exchange(packed, slab_count, 1).reshape(length_x, packed_width)
    lane = np.arange(packed_width)
    real_lane = (lane // channels) % 2 == 0
    swap = np.where(
        real_lane[None, :],
        (lane[:, None] == lane[None, :] + channels).astype(np.float32),
        -(lane[:, None] == lane[None, :] - channels).astype(np.float32),
    )
    weight = spectral_weight[0].transpose(1, 2, 3, 0)
    kept = (slab_index * local_modes < mode_count[0]).astype(jnp.float32)
    keep = jnp.full((1, modes_x), kept, jnp.float32)
    returned = mode_mix_exchange(
        gathered, bf16_constant(full_cos.T), bf16_constant(full_sin.T), bf16_constant(swap.T), weight,
        keep, slab_count,
    )
    returned = returned.reshape(modes_y, slab_rows, plane_count, 2, channels)
    weights_y = np.where(np.arange(modes_y) == 0, 1.0, 2.0).astype(np.float32) / np.float32(
        length_x * length_y
    )
    table = bf16_constant(
        np.concatenate([weights_y[:, None] * y_cos, -(weights_y[:, None] * y_sin)], axis=0)
    )
    cells = slab_rows * plane_count
    back = returned.transpose(1, 2, 4, 3, 0).reshape(cells, channels, 2 * modes_y)
    bias = point_bias.reshape(channels, 1)
    field_rows = field_now.reshape(channels, cells * length_y)
    members = lax.axis_size("member")
    total = layer_sum(back, table, point_weight, field_rows, bias, members)
    return total.reshape(channels // members, slab_rows, plane_count, length_y)


def solution(mesh):
    in_specs = (
        P(None, "slab", None, None),
        P("slab", None, None),
        P(),
        P(),
        P("member"),
        P("member"),
        P(),
        P(),
        P("slab", None, None, None, None),
    )
    out_specs = P("member", "slab", None, None)
    return jax.shard_map(local, mesh=mesh, in_specs=in_specs, out_specs=out_specs, check_vma=False)
```

```python
import functools
import math

import jax
import ml_dtypes
import numpy as np
import jax.numpy as jnp
from jax import lax
from jax.experimental import pallas as pl
from jax.experimental.pallas import tpu as pltpu
from jax.sharding import PartitionSpec as P

TWO_PI = 2.0 * math.pi


def phase_tables(frequency, positions, length):
    product = np.outer(frequency, positions) % length
    angles = (product.astype(np.float32) * np.float32(TWO_PI / length)).astype(np.float64)
    return np.cos(angles).astype(np.float32), np.sin(angles).astype(np.float32)


def bf16_constant(values):
    return jnp.asarray(np.asarray(values, np.float32).astype(ml_dtypes.bfloat16))


def phases(frequency, positions, length):
    product = frequency[:, None] * positions[None, :] % length
    angles = product.astype(jnp.float32) * (TWO_PI / length)
    return (jnp.cos(angles), jnp.sin(angles))


def forward_x(pencil, cos_table, sin_table):
    row_total = pencil.shape[0]
    modes = cos_table.shape[0]
    with_cos = jnp.einsum(
        "kxf,mx->kmf", pencil, cos_table, preferred_element_type=jnp.float32
    ).reshape(row_total, modes, 2, -1)
    with_sin = jnp.einsum(
        "kxf,mx->kmf", pencil, sin_table, preferred_element_type=jnp.float32
    ).reshape(row_total, modes, 2, -1)
    real_part = with_cos[:, :, 0] + with_sin[:, :, 1]
    imag_part = with_cos[:, :, 1] - with_sin[:, :, 0]
    return jnp.stack([real_part, imag_part], axis=2).reshape(row_total, modes, -1)


def inverse_x(spectra, cos_table, sin_table):
    row_total = spectra.shape[0]
    points = cos_table.shape[1]
    with_cos = jnp.einsum(
        "kmf,mx->kxf", spectra, cos_table, preferred_element_type=jnp.float32
    ).reshape(row_total, points, 2, -1)
    with_sin = jnp.einsum(
        "kmf,mx->kxf", spectra, sin_table, preferred_element_type=jnp.float32
    ).reshape(row_total, points, 2, -1)
    real_part = with_cos[:, :, 0] - with_sin[:, :, 1]
    imag_part = with_cos[:, :, 1] + with_sin[:, :, 0]
    return jnp.stack([real_part, imag_part], axis=2).reshape(row_total, points, -1)


def mixing(weights, values):
    return jnp.einsum("kmoi,kmiz->kmoz", weights, values, preferred_element_type=jnp.float32)


def layer_sum_kernel(members, back_ref, table_ref, weight_ref, field_ref, bias_ref, out_ref, value, layer,
                     near, part, far, near_sems, far_send, far_recv):
    me = lax.axis_index("member")
    slab = lax.axis_index("slab")
    chips = members // 2
    chip, core = me // 2, me % 2
    sibling = chip * 2 + 1 - core
    mesh_kind = pl.DeviceIdType.MESH
    barrier = pltpu.get_barrier_semaphore()
    pl.semaphore_signal(barrier, inc=1, device_id=(sibling, slab), device_id_type=mesh_kind)
    for step in range(1, chips):
        peer = lax.rem(chip + step, chips) * 2 + core
        pl.semaphore_signal(barrier, inc=1, device_id=(peer, slab), device_id_type=mesh_kind)
    cells = back_ref.shape[0]
    length = table_ref.shape[1]
    block_rows = layer.shape[2]
    for cell in range(cells):
        lanes = pl.ds(cell * length, length)
        spectral = jnp.dot(back_ref[cell], table_ref[...], preferred_element_type=jnp.float32)
        pointwise = jnp.dot(weight_ref[...], field_ref[:, lanes], preferred_element_type=jnp.float32)
        value[:, lanes] = jax.nn.gelu(pointwise + bias_ref[...] + spectral, approximate=True)
    for block in range(members):
        rows = pl.ds(block * block_rows, block_rows)
        layer[block % 2, block // 2] = value[rows, :].astype(layer.dtype)
    pl.semaphore_wait(barrier, chips)

    on_chip = pltpu.make_async_remote_copy(
        src_ref=layer.at[1 - core],
        dst_ref=near,
        send_sem=near_sems.at[0],
        recv_sem=near_sems.at[1],
        device_id=(sibling, slab),
        device_id_type=mesh_kind,
    )
    on_chip.start()
    on_chip.wait_recv()
    for index in range(chips):
        pair = layer[core, index].astype(jnp.float32) + near[index].astype(jnp.float32)
        part[index] = pair.astype(part.dtype)
    on_chip.wait_send()

    def copy_of(source, target, peer_chip):
        return pltpu.make_async_remote_copy(
            src_ref=part.at[source],
            dst_ref=far.at[target],
            send_sem=far_send.at[source],
            recv_sem=far_recv.at[target],
            device_id=(peer_chip * 2 + core, slab),
            device_id_type=mesh_kind,
        )

    for step in range(1, chips):
        peer = lax.rem(chip + step, chips)
        copy_of(peer, chip, peer).start()
    total = part[chip].astype(jnp.float32)
    for step in range(1, chips):
        source = lax.rem(chip + chips - step, chips)
        copy_of(source, source, source).wait_recv()
        total = total + far[source].astype(jnp.float32)
    for step in range(1, chips):
        peer = lax.rem(chip + step, chips)
        copy_of(peer, chip, peer).wait_send()
    out_ref[...] = (total / members).astype(out_ref.dtype)


def layer_sum(back, table, weight, field, bias, members):
    channels, width = field.shape
    block_rows = channels // members
    chips = members // 2
    return pl.pallas_call(
        functools.partial(layer_sum_kernel, members),
        out_shape=jax.ShapeDtypeStruct((block_rows, width), jnp.bfloat16),
        in_specs=[pl.BlockSpec(memory_space=pltpu.VMEM)] * 5,
        out_specs=pl.BlockSpec(memory_space=pltpu.VMEM),
        scratch_shapes=[
            pltpu.VMEM((channels, width), jnp.float32),
            pltpu.VMEM((2, chips, block_rows, width), jnp.bfloat16),
            pltpu.VMEM((chips, block_rows, width), jnp.bfloat16),
            pltpu.VMEM((chips, block_rows, width), jnp.bfloat16),
            pltpu.VMEM((chips, block_rows, width), jnp.bfloat16),
            pltpu.SemaphoreType.DMA((2,)),
            pltpu.SemaphoreType.DMA((chips,)),
            pltpu.SemaphoreType.DMA((chips,)),
        ],
        compiler_params=pltpu.CompilerParams(collective_id=0, has_side_effects=True),
    )(back, table, weight, field, bias)


def greet_slab(parts):
    me = lax.axis_index("slab")
    member = lax.axis_index("member")
    barrier = pltpu.get_barrier_semaphore()
    for step in range(1, parts):
        peer = lax.rem(me + step, parts)
        pl.semaphore_signal(barrier, inc=1, device_id=(member, peer), device_id_type=pl.DeviceIdType.MESH)
    return barrier


def swap_blocks(parts, source_ref, out_ref, landed, send_sems, recv_sems):
    me = lax.axis_index("slab")
    member = lax.axis_index("member")

    def copy_of(source, target, peer):
        return pltpu.make_async_remote_copy(
            src_ref=source_ref.at[source],
            dst_ref=landed.at[target],
            send_sem=send_sems.at[source],
            recv_sem=recv_sems.at[target],
            device_id=(member, peer),
            device_id_type=pl.DeviceIdType.MESH,
        )

    for step in range(1, parts):
        peer = lax.rem(me + step, parts)
        copy_of(peer, me, peer).start()
    landed[me] = source_ref[me]
    for step in range(1, parts):
        source = lax.rem(me + parts - step, parts)
        copy_of(source, source, source).wait_recv()
    for step in range(1, parts):
        peer = lax.rem(me + step, parts)
        copy_of(peer, me, peer).wait_send()
    out_ref[...] = landed[...]


def slab_exchange_kernel(parts, blocks_ref, out_ref, landed, send_sems, recv_sems):
    barrier = greet_slab(parts)
    pl.semaphore_wait(barrier, parts - 1)
    swap_blocks(parts, blocks_ref, out_ref, landed, send_sems, recv_sems)


def mode_mix_kernel(parts, pencil_ref, xcos_t_ref, xsin_t_ref, swap_t_ref, weight_ref, count_ref, out_ref,
                    mixed_t, blocks, landed, send_sems, recv_sems):
    barrier = greet_slab(parts)
    pencil_t = pencil_ref[...].astype(jnp.float32).T.astype(pencil_ref.dtype)
    swap_t = swap_t_ref[...]
    swapped_t = jnp.dot(swap_t, pencil_t, preferred_element_type=jnp.float32).astype(pencil_t.dtype)
    spec_t = jnp.dot(pencil_t, xcos_t_ref[...], preferred_element_type=jnp.float32)
    spec_t = spec_t + jnp.dot(swapped_t, xsin_t_ref[...], preferred_element_type=jnp.float32)
    spec_t = spec_t.astype(pencil_t.dtype).astype(jnp.float32)
    outputs = weight_ref.shape[1]
    planes = spec_t.shape[0] // (2 * outputs)
    for plane in range(planes):
        base = plane * 2 * outputs
        real = spec_t[base:base + outputs, :]
        imag = spec_t[base + outputs:base + 2 * outputs, :]
        for out in range(outputs):
            weight_real = weight_ref[0, out].astype(jnp.float32)
            weight_imag = weight_ref[1, out].astype(jnp.float32)
            mixed_t[pl.ds(base + out, 1), :] = jnp.sum(
                weight_real * real - weight_imag * imag, axis=0, keepdims=True
            )
            mixed_t[pl.ds(base + outputs + out, 1), :] = jnp.sum(
                weight_imag * real + weight_real * imag, axis=0, keepdims=True
            )
    kept = (lax.axis_index("slab") < count_ref[0]).astype(jnp.float32)
    mixed = (mixed_t[...] * kept).astype(pencil_t.dtype)
    mixed_swapped = jnp.dot(swap_t, mixed, preferred_element_type=jnp.float32).astype(pencil_t.dtype)
    contract = (((1,), (1,)), ((), ()))
    back = lax.dot_general(xcos_t_ref[...], mixed, contract, preferred_element_type=jnp.float32)
    back = back - lax.dot_general(
        xsin_t_ref[...], mixed_swapped, contract, preferred_element_type=jnp.float32
    )
    blocks[...] = back.reshape(blocks.shape).astype(blocks.dtype)
    pl.semaphore_wait(barrier, parts - 1)
    swap_blocks(parts, blocks, out_ref, landed, send_sems, recv_sems)


def mode_mix_exchange(pencil, xcos_t, xsin_t, swap_t, weight, count, parts):
    points, width = pencil.shape
    modes = xcos_t.shape[1]
    shape = (parts, points // parts, width)
    return pl.pallas_call(
        functools.partial(mode_mix_kernel, parts),
        out_shape=jax.ShapeDtypeStruct(shape, pencil.dtype),
        in_specs=[pl.BlockSpec(memory_space=pltpu.VMEM)] * 5
        + [pl.BlockSpec(memory_space=pltpu.SMEM)],
        out_specs=pl.BlockSpec(memory_space=pltpu.VMEM),
        scratch_shapes=[
            pltpu.VMEM((width, modes), jnp.float32),
            pltpu.VMEM(shape, pencil.dtype),
            pltpu.VMEM(shape, pencil.dtype),
            pltpu.SemaphoreType.DMA((parts,)),
            pltpu.SemaphoreType.DMA((parts,)),
        ],
        compiler_params=pltpu.CompilerParams(collective_id=2, has_side_effects=True),
    )(pencil, xcos_t, xsin_t, swap_t, weight, count)


def slab_exchange(blocks, parts, exchange_id):
    return pl.pallas_call(
        functools.partial(slab_exchange_kernel, parts),
        out_shape=jax.ShapeDtypeStruct(blocks.shape, blocks.dtype),
        in_specs=[pl.BlockSpec(memory_space=pltpu.VMEM)],
        out_specs=pl.BlockSpec(memory_space=pltpu.VMEM),
        scratch_shapes=[
            pltpu.VMEM(blocks.shape, blocks.dtype),
            pltpu.SemaphoreType.DMA((parts,)),
            pltpu.SemaphoreType.DMA((parts,)),
        ],
        compiler_params=pltpu.CompilerParams(collective_id=exchange_id, has_side_effects=True),
    )(blocks)


def local(
    base_field,
    forcing,
    load,
    amplitudes,
    amp_index,
    mode_count,
    point_weight,
    point_bias,
    spectral_weight,
):
    channels, slab_rows, plane_count, length_y = base_field.shape
    slab_count = lax.axis_size("slab")
    local_modes = spectral_weight.shape[0]
    modes_y = local_modes * slab_count
    modes_x = spectral_weight.shape[1]
    length_x = slab_rows * slab_count
    packed_width = 2 * channels * plane_count
    slab_index = lax.axis_index("slab")
    level_ids = jnp.arange(amplitudes.shape[0], dtype=jnp.int32)
    amplitude = jnp.sum(jnp.where(level_ids == amp_index[0], amplitudes, 0.0))
    driven = base_field.astype(jnp.float32) + amplitude * load[:, None, None, None] * forcing[
        None
    ].astype(jnp.float32)
    field_now = (2.0 * jnp.tanh(0.5 * driven)).astype(jnp.bfloat16)
    y_cos, y_sin = phase_tables(np.arange(modes_y), np.arange(length_y), length_y)
    y_real = jnp.einsum(
        "cxzy,ky->kxcz", field_now, bf16_constant(y_cos), preferred_element_type=jnp.float32
    )
    y_imag = -jnp.einsum(
        "cxzy,ky->kxcz", field_now, bf16_constant(y_sin), preferred_element_type=jnp.float32
    )
    packed = (
        jnp.stack([y_real, y_imag], axis=2)
        .transpose(0, 1, 4, 2, 3)
        .astype(jnp.bfloat16)
        .reshape(modes_y, slab_rows, packed_width)
    )
    frequency_x = np.concatenate(
        [np.arange(modes_x // 2), np.arange(length_x - modes_x // 2, length_x)]
    )
    full_cos, full_sin = phase_tables(frequency_x, np.arange(length_x), length_x)
    gathered = slab_exchange(packed, slab_count, 1).reshape(length_x, packed_width)
    lane = np.arange(packed_width)
    real_lane = (lane // channels) % 2 == 0
    swap = np.where(
        real_lane[None, :],
        (lane[:, None] == lane[None, :] + channels).astype(np.float32),
        -(lane[:, None] == lane[None, :] - channels).astype(np.float32),
    )
    weight = spectral_weight[0].transpose(1, 2, 3, 0)
    returned = mode_mix_exchange(
        gathered, bf16_constant(full_cos.T), bf16_constant(full_sin.T), bf16_constant(swap.T), weight,
        mode_count, slab_count,
    )
    returned = returned.reshape(modes_y, slab_rows, plane_count, 2, channels)
    weights_y = np.where(np.arange(modes_y) == 0, 1.0, 2.0).astype(np.float32) / np.float32(
        length_x * length_y
    )
    table = bf16_constant(
        np.concatenate([weights_y[:, None] * y_cos, -(weights_y[:, None] * y_sin)], axis=0)
    )
    cells = slab_rows * plane_count
    back = returned.transpose(1, 2, 4, 3, 0).reshape(cells, channels, 2 * modes_y)
    bias = point_bias.reshape(channels, 1)
    field_rows = field_now.reshape(channels, cells * length_y)
    members = lax.axis_size("member")
    total = layer_sum(back, table, point_weight, field_rows, bias, members)
    return total.reshape(channels // members, slab_rows, plane_count, length_y)


def solution(mesh):
    in_specs = (
        P(None, "slab", None, None),
        P("slab", None, None),
        P(),
        P(),
        P("member"),
        P("member"),
        P(),
        P(),
        P("slab", None, None, None, None),
    )
    out_specs = P("member", "slab", None, None)
    return jax.shard_map(local, mesh=mesh, in_specs=in_specs, out_specs=out_specs, check_vma=False)
```

```python
import functools
import math

import jax
import ml_dtypes
import numpy as np
import jax.numpy as jnp
from jax import lax
from jax.experimental import pallas as pl
from jax.experimental.pallas import tpu as pltpu
from jax.sharding import PartitionSpec as P

TWO_PI = 2.0 * math.pi


def phase_tables(frequency, positions, length):
    product = np.outer(frequency, positions) % length
    angles = (product.astype(np.float32) * np.float32(TWO_PI / length)).astype(np.float64)
    return np.cos(angles).astype(np.float32), np.sin(angles).astype(np.float32)


def bf16_constant(values):
    return jnp.asarray(np.asarray(values, np.float32).astype(ml_dtypes.bfloat16))


def phases(frequency, positions, length):
    product = frequency[:, None] * positions[None, :] % length
    angles = product.astype(jnp.float32) * (TWO_PI / length)
    return (jnp.cos(angles), jnp.sin(angles))


def forward_x(pencil, cos_table, sin_table):
    row_total = pencil.shape[0]
    modes = cos_table.shape[0]
    with_cos = jnp.einsum(
        "kxf,mx->kmf", pencil, cos_table, preferred_element_type=jnp.float32
    ).reshape(row_total, modes, 2, -1)
    with_sin = jnp.einsum(
        "kxf,mx->kmf", pencil, sin_table, preferred_element_type=jnp.float32
    ).reshape(row_total, modes, 2, -1)
    real_part = with_cos[:, :, 0] + with_sin[:, :, 1]
    imag_part = with_cos[:, :, 1] - with_sin[:, :, 0]
    return jnp.stack([real_part, imag_part], axis=2).reshape(row_total, modes, -1)


def inverse_x(spectra, cos_table, sin_table):
    row_total = spectra.shape[0]
    points = cos_table.shape[1]
    with_cos = jnp.einsum(
        "kmf,mx->kxf", spectra, cos_table, preferred_element_type=jnp.float32
    ).reshape(row_total, points, 2, -1)
    with_sin = jnp.einsum(
        "kmf,mx->kxf", spectra, sin_table, preferred_element_type=jnp.float32
    ).reshape(row_total, points, 2, -1)
    real_part = with_cos[:, :, 0] - with_sin[:, :, 1]
    imag_part = with_cos[:, :, 1] + with_sin[:, :, 0]
    return jnp.stack([real_part, imag_part], axis=2).reshape(row_total, points, -1)


def mixing(weights, values):
    return jnp.einsum("kmoi,kmiz->kmoz", weights, values, preferred_element_type=jnp.float32)


def layer_sum_kernel(members, back_ref, table_ref, weight_ref, field_ref, bias_ref, out_ref, value, layer,
                     near, part, far, near_sems, far_send, far_recv):
    me = lax.axis_index("member")
    slab = lax.axis_index("slab")
    chips = members // 2
    chip, core = me // 2, me % 2
    sibling = chip * 2 + 1 - core
    mesh_kind = pl.DeviceIdType.MESH
    barrier = pltpu.get_barrier_semaphore()
    pl.semaphore_signal(barrier, inc=1, device_id=(sibling, slab), device_id_type=mesh_kind)
    for step in range(1, chips):
        peer = lax.rem(chip + step, chips) * 2 + core
        pl.semaphore_signal(barrier, inc=1, device_id=(peer, slab), device_id_type=mesh_kind)
    modes, slab_rows, width = back_ref.shape
    channels = weight_ref.shape[0]
    planes = width // (2 * channels)
    length = table_ref.shape[1]
    block_rows = layer.shape[2]
    table_real = table_ref[:modes, :]
    table_imag = table_ref[modes:, :]
    padding = jnp.zeros((width - modes, width), jnp.float32)
    for row in range(slab_rows):
        pencil = back_ref[:, row, :].astype(jnp.float32)
        pencil_t = jnp.concatenate([pencil, padding], axis=0).T[:, :modes].astype(back_ref.dtype)
        for plane in range(planes):
            cell = row * planes + plane
            base = plane * 2 * channels
            lanes = pl.ds(cell * length, length)
            spectral = jnp.dot(
                pencil_t[base:base + channels], table_real, preferred_element_type=jnp.float32
            )
            spectral = spectral + jnp.dot(
                pencil_t[base + channels:base + 2 * channels], table_imag,
                preferred_element_type=jnp.float32,
            )
            pointwise = jnp.dot(weight_ref[...], field_ref[:, lanes], preferred_element_type=jnp.float32)
            value[:, lanes] = jax.nn.gelu(pointwise + bias_ref[...] + spectral, approximate=True)
    for block in range(members):
        rows = pl.ds(block * block_rows, block_rows)
        layer[block % 2, block // 2] = value[rows, :].astype(layer.dtype)
    pl.semaphore_wait(barrier, chips)

    on_chip = pltpu.make_async_remote_copy(
        src_ref=layer.at[1 - core],
        dst_ref=near,
        send_sem=near_sems.at[0],
        recv_sem=near_sems.at[1],
        device_id=(sibling, slab),
        device_id_type=mesh_kind,
    )
    on_chip.start()
    on_chip.wait_recv()
    for index in range(chips):
        pair = layer[core, index].astype(jnp.float32) + near[index].astype(jnp.float32)
        part[index] = pair.astype(part.dtype)
    on_chip.wait_send()

    def copy_of(source, target, peer_chip):
        return pltpu.make_async_remote_copy(
            src_ref=part.at[source],
            dst_ref=far.at[target],
            send_sem=far_send.at[source],
            recv_sem=far_recv.at[target],
            device_id=(peer_chip * 2 + core, slab),
            device_id_type=mesh_kind,
        )

    for step in range(1, chips):
        peer = lax.rem(chip + step, chips)
        copy_of(peer, chip, peer).start()
    total = part[chip].astype(jnp.float32)
    for step in range(1, chips):
        source = lax.rem(chip + chips - step, chips)
        copy_of(source, source, source).wait_recv()
        total = total + far[source].astype(jnp.float32)
    for step in range(1, chips):
        peer = lax.rem(chip + step, chips)
        copy_of(peer, chip, peer).wait_send()
    out_ref[...] = (total / members).astype(out_ref.dtype)


def layer_sum(back, table, weight, field, bias, members):
    channels, width = field.shape
    block_rows = channels // members
    chips = members // 2
    return pl.pallas_call(
        functools.partial(layer_sum_kernel, members),
        out_shape=jax.ShapeDtypeStruct((block_rows, width), jnp.bfloat16),
        in_specs=[pl.BlockSpec(memory_space=pltpu.VMEM)] * 5,
        out_specs=pl.BlockSpec(memory_space=pltpu.VMEM),
        scratch_shapes=[
            pltpu.VMEM((channels, width), jnp.float32),
            pltpu.VMEM((2, chips, block_rows, width), jnp.bfloat16),
            pltpu.VMEM((chips, block_rows, width), jnp.bfloat16),
            pltpu.VMEM((chips, block_rows, width), jnp.bfloat16),
            pltpu.VMEM((chips, block_rows, width), jnp.bfloat16),
            pltpu.SemaphoreType.DMA((2,)),
            pltpu.SemaphoreType.DMA((chips,)),
            pltpu.SemaphoreType.DMA((chips,)),
        ],
        compiler_params=pltpu.CompilerParams(collective_id=0, has_side_effects=True),
    )(back, table, weight, field, bias)


def greet_slab(parts):
    me = lax.axis_index("slab")
    member = lax.axis_index("member")
    barrier = pltpu.get_barrier_semaphore()
    for step in range(1, parts):
        peer = lax.rem(me + step, parts)
        pl.semaphore_signal(barrier, inc=1, device_id=(member, peer), device_id_type=pl.DeviceIdType.MESH)
    return barrier


def swap_blocks(parts, source_ref, out_ref, landed, send_sems, recv_sems):
    me = lax.axis_index("slab")
    member = lax.axis_index("member")

    def copy_of(source, target, peer):
        return pltpu.make_async_remote_copy(
            src_ref=source_ref.at[source],
            dst_ref=landed.at[target],
            send_sem=send_sems.at[source],
            recv_sem=recv_sems.at[target],
            device_id=(member, peer),
            device_id_type=pl.DeviceIdType.MESH,
        )

    for step in range(1, parts):
        peer = lax.rem(me + step, parts)
        copy_of(peer, me, peer).start()
    landed[me] = source_ref[me]
    for step in range(1, parts):
        source = lax.rem(me + parts - step, parts)
        copy_of(source, source, source).wait_recv()
    for step in range(1, parts):
        peer = lax.rem(me + step, parts)
        copy_of(peer, me, peer).wait_send()
    out_ref[...] = landed[...]


def slab_exchange_kernel(parts, blocks_ref, out_ref, landed, send_sems, recv_sems):
    barrier = greet_slab(parts)
    pl.semaphore_wait(barrier, parts - 1)
    swap_blocks(parts, blocks_ref, out_ref, landed, send_sems, recv_sems)


def mode_mix_kernel(parts, pencil_ref, xcos_t_ref, xsin_t_ref, swap_t_ref, weight_ref, count_ref, out_ref,
                    mixed_t, blocks, landed, send_sems, recv_sems):
    barrier = greet_slab(parts)
    pencil_t = pencil_ref[...].astype(jnp.float32).T.astype(pencil_ref.dtype)
    swap_t = swap_t_ref[...]
    swapped_t = jnp.dot(swap_t, pencil_t, preferred_element_type=jnp.float32).astype(pencil_t.dtype)
    spec_t = jnp.dot(pencil_t, xcos_t_ref[...], preferred_element_type=jnp.float32)
    spec_t = spec_t + jnp.dot(swapped_t, xsin_t_ref[...], preferred_element_type=jnp.float32)
    spec_t = spec_t.astype(pencil_t.dtype).astype(jnp.float32)
    outputs = weight_ref.shape[1]
    planes = spec_t.shape[0] // (2 * outputs)
    for plane in range(planes):
        base = plane * 2 * outputs
        real = spec_t[base:base + outputs, :]
        imag = spec_t[base + outputs:base + 2 * outputs, :]
        for out in range(outputs):
            weight_real = weight_ref[0, out].astype(jnp.float32)
            weight_imag = weight_ref[1, out].astype(jnp.float32)
            mixed_t[pl.ds(base + out, 1), :] = jnp.sum(
                weight_real * real - weight_imag * imag, axis=0, keepdims=True
            )
            mixed_t[pl.ds(base + outputs + out, 1), :] = jnp.sum(
                weight_imag * real + weight_real * imag, axis=0, keepdims=True
            )
    kept = (lax.axis_index("slab") < count_ref[0]).astype(jnp.float32)
    mixed = (mixed_t[...] * kept).astype(pencil_t.dtype)
    mixed_swapped = jnp.dot(swap_t, mixed, preferred_element_type=jnp.float32).astype(pencil_t.dtype)
    contract = (((1,), (1,)), ((), ()))
    back = lax.dot_general(xcos_t_ref[...], mixed, contract, preferred_element_type=jnp.float32)
    back = back - lax.dot_general(
        xsin_t_ref[...], mixed_swapped, contract, preferred_element_type=jnp.float32
    )
    blocks[...] = back.reshape(blocks.shape).astype(blocks.dtype)
    pl.semaphore_wait(barrier, parts - 1)
    swap_blocks(parts, blocks, out_ref, landed, send_sems, recv_sems)


def mode_mix_exchange(pencil, xcos_t, xsin_t, swap_t, weight, count, parts):
    points, width = pencil.shape
    modes = xcos_t.shape[1]
    shape = (parts, points // parts, width)
    return pl.pallas_call(
        functools.partial(mode_mix_kernel, parts),
        out_shape=jax.ShapeDtypeStruct(shape, pencil.dtype),
        in_specs=[pl.BlockSpec(memory_space=pltpu.VMEM)] * 5
        + [pl.BlockSpec(memory_space=pltpu.SMEM)],
        out_specs=pl.BlockSpec(memory_space=pltpu.VMEM),
        scratch_shapes=[
            pltpu.VMEM((width, modes), jnp.float32),
            pltpu.VMEM(shape, pencil.dtype),
            pltpu.VMEM(shape, pencil.dtype),
            pltpu.SemaphoreType.DMA((parts,)),
            pltpu.SemaphoreType.DMA((parts,)),
        ],
        compiler_params=pltpu.CompilerParams(collective_id=2, has_side_effects=True),
    )(pencil, xcos_t, xsin_t, swap_t, weight, count)


def slab_exchange(blocks, parts, exchange_id):
    return pl.pallas_call(
        functools.partial(slab_exchange_kernel, parts),
        out_shape=jax.ShapeDtypeStruct(blocks.shape, blocks.dtype),
        in_specs=[pl.BlockSpec(memory_space=pltpu.VMEM)],
        out_specs=pl.BlockSpec(memory_space=pltpu.VMEM),
        scratch_shapes=[
            pltpu.VMEM(blocks.shape, blocks.dtype),
            pltpu.SemaphoreType.DMA((parts,)),
            pltpu.SemaphoreType.DMA((parts,)),
        ],
        compiler_params=pltpu.CompilerParams(collective_id=exchange_id, has_side_effects=True),
    )(blocks)


def local(
    base_field,
    forcing,
    load,
    amplitudes,
    amp_index,
    mode_count,
    point_weight,
    point_bias,
    spectral_weight,
):
    channels, slab_rows, plane_count, length_y = base_field.shape
    slab_count = lax.axis_size("slab")
    local_modes = spectral_weight.shape[0]
    modes_y = local_modes * slab_count
    modes_x = spectral_weight.shape[1]
    length_x = slab_rows * slab_count
    packed_width = 2 * channels * plane_count
    slab_index = lax.axis_index("slab")
    level_ids = jnp.arange(amplitudes.shape[0], dtype=jnp.int32)
    amplitude = jnp.sum(jnp.where(level_ids == amp_index[0], amplitudes, 0.0))
    driven = base_field.astype(jnp.float32) + amplitude * load[:, None, None, None] * forcing[
        None
    ].astype(jnp.float32)
    field_now = (2.0 * jnp.tanh(0.5 * driven)).astype(jnp.bfloat16)
    y_cos, y_sin = phase_tables(np.arange(modes_y), np.arange(length_y), length_y)
    y_real = jnp.einsum(
        "cxzy,ky->kxcz", field_now, bf16_constant(y_cos), preferred_element_type=jnp.float32
    )
    y_imag = -jnp.einsum(
        "cxzy,ky->kxcz", field_now, bf16_constant(y_sin), preferred_element_type=jnp.float32
    )
    packed = (
        jnp.stack([y_real, y_imag], axis=2)
        .transpose(0, 1, 4, 2, 3)
        .astype(jnp.bfloat16)
        .reshape(modes_y, slab_rows, packed_width)
    )
    frequency_x = np.concatenate(
        [np.arange(modes_x // 2), np.arange(length_x - modes_x // 2, length_x)]
    )
    full_cos, full_sin = phase_tables(frequency_x, np.arange(length_x), length_x)
    gathered = slab_exchange(packed, slab_count, 1).reshape(length_x, packed_width)
    lane = np.arange(packed_width)
    real_lane = (lane // channels) % 2 == 0
    swap = np.where(
        real_lane[None, :],
        (lane[:, None] == lane[None, :] + channels).astype(np.float32),
        -(lane[:, None] == lane[None, :] - channels).astype(np.float32),
    )
    weight = spectral_weight[0].transpose(1, 2, 3, 0)
    returned = mode_mix_exchange(
        gathered, bf16_constant(full_cos.T), bf16_constant(full_sin.T), bf16_constant(swap.T), weight,
        mode_count, slab_count,
    )
    weights_y = np.where(np.arange(modes_y) == 0, 1.0, 2.0).astype(np.float32) / np.float32(
        length_x * length_y
    )
    table = bf16_constant(
        np.concatenate([weights_y[:, None] * y_cos, -(weights_y[:, None] * y_sin)], axis=0)
    )
    cells = slab_rows * plane_count
    bias = point_bias.reshape(channels, 1)
    field_rows = field_now.reshape(channels, cells * length_y)
    members = lax.axis_size("member")
    total = layer_sum(returned, table, point_weight, field_rows, bias, members)
    return total.reshape(channels // members, slab_rows, plane_count, length_y)


def solution(mesh):
    in_specs = (
        P(None, "slab", None, None),
        P("slab", None, None),
        P(),
        P(),
        P("member"),
        P("member"),
        P(),
        P(),
        P("slab", None, None, None, None),
    )
    out_specs = P("member", "slab", None, None)
    return jax.shard_map(local, mesh=mesh, in_specs=in_specs, out_specs=out_specs, check_vma=False)
```

```python
import functools
import math

import jax
import ml_dtypes
import numpy as np
import jax.numpy as jnp
from jax import lax
from jax.experimental import pallas as pl
from jax.experimental.pallas import tpu as pltpu
from jax.sharding import PartitionSpec as P

TWO_PI = 2.0 * math.pi


def phase_tables(frequency, positions, length):
    product = np.outer(frequency, positions) % length
    angles = (product.astype(np.float32) * np.float32(TWO_PI / length)).astype(np.float64)
    return np.cos(angles).astype(np.float32), np.sin(angles).astype(np.float32)


def bf16_constant(values):
    return jnp.asarray(np.asarray(values, np.float32).astype(ml_dtypes.bfloat16))


def phases(frequency, positions, length):
    product = frequency[:, None] * positions[None, :] % length
    angles = product.astype(jnp.float32) * (TWO_PI / length)
    return (jnp.cos(angles), jnp.sin(angles))


def forward_x(pencil, cos_table, sin_table):
    row_total = pencil.shape[0]
    modes = cos_table.shape[0]
    with_cos = jnp.einsum(
        "kxf,mx->kmf", pencil, cos_table, preferred_element_type=jnp.float32
    ).reshape(row_total, modes, 2, -1)
    with_sin = jnp.einsum(
        "kxf,mx->kmf", pencil, sin_table, preferred_element_type=jnp.float32
    ).reshape(row_total, modes, 2, -1)
    real_part = with_cos[:, :, 0] + with_sin[:, :, 1]
    imag_part = with_cos[:, :, 1] - with_sin[:, :, 0]
    return jnp.stack([real_part, imag_part], axis=2).reshape(row_total, modes, -1)


def inverse_x(spectra, cos_table, sin_table):
    row_total = spectra.shape[0]
    points = cos_table.shape[1]
    with_cos = jnp.einsum(
        "kmf,mx->kxf", spectra, cos_table, preferred_element_type=jnp.float32
    ).reshape(row_total, points, 2, -1)
    with_sin = jnp.einsum(
        "kmf,mx->kxf", spectra, sin_table, preferred_element_type=jnp.float32
    ).reshape(row_total, points, 2, -1)
    real_part = with_cos[:, :, 0] - with_sin[:, :, 1]
    imag_part = with_cos[:, :, 1] + with_sin[:, :, 0]
    return jnp.stack([real_part, imag_part], axis=2).reshape(row_total, points, -1)


def mixing(weights, values):
    return jnp.einsum("kmoi,kmiz->kmoz", weights, values, preferred_element_type=jnp.float32)


def layer_sum_kernel(members, back_ref, table_ref, weight_ref, field_ref, bias_ref, out_ref, value, layer,
                     near, part, far, near_sems, far_send, far_recv):
    me = lax.axis_index("member")
    slab = lax.axis_index("slab")
    chips = members // 2
    chip, core = me // 2, me % 2
    sibling = chip * 2 + 1 - core
    mesh_kind = pl.DeviceIdType.MESH
    barrier = pltpu.get_barrier_semaphore()
    pl.semaphore_signal(barrier, inc=1, device_id=(sibling, slab), device_id_type=mesh_kind)
    for step in range(1, chips):
        peer = lax.rem(chip + step, chips) * 2 + core
        pl.semaphore_signal(barrier, inc=1, device_id=(peer, slab), device_id_type=mesh_kind)
    modes, slab_rows, width = back_ref.shape
    channels = weight_ref.shape[0]
    planes = width // (2 * channels)
    length = table_ref.shape[1]
    block_rows = layer.shape[2]
    table_real = table_ref[:modes, :]
    table_imag = table_ref[modes:, :]
    padding = jnp.zeros((width - modes, width), jnp.float32)
    for row in range(slab_rows):
        pencil = back_ref[:, row, :].astype(jnp.float32)
        pencil_t = jnp.concatenate([pencil, padding], axis=0).T[:, :modes].astype(back_ref.dtype)
        for plane in range(planes):
            cell = row * planes + plane
            base = plane * 2 * channels
            lanes = pl.ds(cell * length, length)
            spectral = jnp.dot(
                pencil_t[base:base + channels], table_real, preferred_element_type=jnp.float32
            )
            spectral = spectral + jnp.dot(
                pencil_t[base + channels:base + 2 * channels], table_imag,
                preferred_element_type=jnp.float32,
            )
            pointwise = jnp.dot(weight_ref[...], field_ref[:, lanes], preferred_element_type=jnp.float32)
            value[:, lanes] = jax.nn.gelu(pointwise + bias_ref[...] + spectral, approximate=True)
    for block in range(members):
        rows = pl.ds(block * block_rows, block_rows)
        layer[block % 2, block // 2] = value[rows, :].astype(layer.dtype)
    pl.semaphore_wait(barrier, chips)

    on_chip = pltpu.make_async_remote_copy(
        src_ref=layer.at[1 - core],
        dst_ref=near,
        send_sem=near_sems.at[0],
        recv_sem=near_sems.at[1],
        device_id=(sibling, slab),
        device_id_type=mesh_kind,
    )
    on_chip.start()
    on_chip.wait_recv()
    for index in range(chips):
        pair = layer[core, index].astype(jnp.float32) + near[index].astype(jnp.float32)
        part[index] = pair.astype(part.dtype)
    on_chip.wait_send()

    def copy_of(source, target, peer_chip):
        return pltpu.make_async_remote_copy(
            src_ref=part.at[source],
            dst_ref=far.at[target],
            send_sem=far_send.at[source],
            recv_sem=far_recv.at[target],
            device_id=(peer_chip * 2 + core, slab),
            device_id_type=mesh_kind,
        )

    for step in range(1, chips):
        peer = lax.rem(chip + step, chips)
        copy_of(peer, chip, peer).start()
    total = part[chip].astype(jnp.float32)
    for step in range(1, chips):
        source = lax.rem(chip + chips - step, chips)
        copy_of(source, source, source).wait_recv()
        total = total + far[source].astype(jnp.float32)
    for step in range(1, chips):
        peer = lax.rem(chip + step, chips)
        copy_of(peer, chip, peer).wait_send()
    out_ref[...] = (total / members).astype(out_ref.dtype)


def layer_sum(back, table, weight, field, bias, members):
    channels, width = field.shape
    block_rows = channels // members
    chips = members // 2
    return pl.pallas_call(
        functools.partial(layer_sum_kernel, members),
        out_shape=jax.ShapeDtypeStruct((block_rows, width), jnp.bfloat16),
        in_specs=[pl.BlockSpec(memory_space=pltpu.VMEM)] * 5,
        out_specs=pl.BlockSpec(memory_space=pltpu.VMEM),
        scratch_shapes=[
            pltpu.VMEM((channels, width), jnp.float32),
            pltpu.VMEM((2, chips, block_rows, width), jnp.bfloat16),
            pltpu.VMEM((chips, block_rows, width), jnp.bfloat16),
            pltpu.VMEM((chips, block_rows, width), jnp.bfloat16),
            pltpu.VMEM((chips, block_rows, width), jnp.bfloat16),
            pltpu.SemaphoreType.DMA((2,)),
            pltpu.SemaphoreType.DMA((chips,)),
            pltpu.SemaphoreType.DMA((chips,)),
        ],
        compiler_params=pltpu.CompilerParams(collective_id=0, has_side_effects=True),
    )(back, table, weight, field, bias)


def greet_slab(parts):
    me = lax.axis_index("slab")
    member = lax.axis_index("member")
    barrier = pltpu.get_barrier_semaphore()
    for step in range(1, parts):
        peer = lax.rem(me + step, parts)
        pl.semaphore_signal(barrier, inc=1, device_id=(member, peer), device_id_type=pl.DeviceIdType.MESH)
    return barrier


def swap_blocks(parts, source_ref, out_ref, landed, send_sems, recv_sems):
    me = lax.axis_index("slab")
    member = lax.axis_index("member")

    def copy_of(source, target, peer):
        return pltpu.make_async_remote_copy(
            src_ref=source_ref.at[source],
            dst_ref=landed.at[target],
            send_sem=send_sems.at[source],
            recv_sem=recv_sems.at[target],
            device_id=(member, peer),
            device_id_type=pl.DeviceIdType.MESH,
        )

    for step in range(1, parts):
        peer = lax.rem(me + step, parts)
        copy_of(peer, me, peer).start()
    landed[me] = source_ref[me]
    for step in range(1, parts):
        source = lax.rem(me + parts - step, parts)
        copy_of(source, source, source).wait_recv()
    for step in range(1, parts):
        peer = lax.rem(me + step, parts)
        copy_of(peer, me, peer).wait_send()
    out_ref[...] = landed[...]


def slab_exchange_kernel(parts, blocks_ref, out_ref, landed, send_sems, recv_sems):
    barrier = greet_slab(parts)
    pl.semaphore_wait(barrier, parts - 1)
    swap_blocks(parts, blocks_ref, out_ref, landed, send_sems, recv_sems)


def mode_mix_kernel(parts, pencil_ref, xcos_t_ref, xsin_t_ref, swap_t_ref, weight_ref, count_ref, out_ref,
                    mixed_t, blocks, landed, send_sems, recv_sems):
    barrier = greet_slab(parts)
    pencil_t = pencil_ref[...].astype(jnp.float32).T.astype(pencil_ref.dtype)
    swap_t = swap_t_ref[...]
    swapped_t = jnp.dot(swap_t, pencil_t, preferred_element_type=jnp.float32).astype(pencil_t.dtype)
    spec_t = jnp.dot(pencil_t, xcos_t_ref[...], preferred_element_type=jnp.float32)
    spec_t = spec_t + jnp.dot(swapped_t, xsin_t_ref[...], preferred_element_type=jnp.float32)
    spec_t = spec_t.astype(pencil_t.dtype).astype(jnp.float32)
    outputs = weight_ref.shape[1]
    planes = spec_t.shape[0] // (2 * outputs)
    for plane in range(planes):
        base = plane * 2 * outputs
        real = spec_t[base:base + outputs, :]
        imag = spec_t[base + outputs:base + 2 * outputs, :]
        for out in range(outputs):
            weight_real = weight_ref[0, out].astype(jnp.float32)
            weight_imag = weight_ref[1, out].astype(jnp.float32)
            mixed_t[pl.ds(base + out, 1), :] = jnp.sum(
                weight_real * real - weight_imag * imag, axis=0, keepdims=True
            )
            mixed_t[pl.ds(base + outputs + out, 1), :] = jnp.sum(
                weight_imag * real + weight_real * imag, axis=0, keepdims=True
            )
    kept = (lax.axis_index("slab") < count_ref[0]).astype(jnp.float32)
    mixed = (mixed_t[...] * kept).astype(pencil_t.dtype)
    mixed_swapped = jnp.dot(swap_t, mixed, preferred_element_type=jnp.float32).astype(pencil_t.dtype)
    contract = (((1,), (1,)), ((), ()))
    back = lax.dot_general(xcos_t_ref[...], mixed, contract, preferred_element_type=jnp.float32)
    back = back - lax.dot_general(
        xsin_t_ref[...], mixed_swapped, contract, preferred_element_type=jnp.float32
    )
    blocks[...] = back.reshape(blocks.shape).astype(blocks.dtype)
    pl.semaphore_wait(barrier, parts - 1)
    swap_blocks(parts, blocks, out_ref, landed, send_sems, recv_sems)


def mode_mix_exchange(pencil, xcos_t, xsin_t, swap_t, weight, count, parts):
    points, width = pencil.shape
    modes = xcos_t.shape[1]
    shape = (parts, points // parts, width)
    return pl.pallas_call(
        functools.partial(mode_mix_kernel, parts),
        out_shape=jax.ShapeDtypeStruct(shape, pencil.dtype),
        in_specs=[pl.BlockSpec(memory_space=pltpu.VMEM)] * 5
        + [pl.BlockSpec(memory_space=pltpu.SMEM)],
        out_specs=pl.BlockSpec(memory_space=pltpu.VMEM),
        scratch_shapes=[
            pltpu.VMEM((width, modes), jnp.float32),
            pltpu.VMEM(shape, pencil.dtype),
            pltpu.VMEM(shape, pencil.dtype),
            pltpu.SemaphoreType.DMA((parts,)),
            pltpu.SemaphoreType.DMA((parts,)),
        ],
        compiler_params=pltpu.CompilerParams(collective_id=2, has_side_effects=True),
    )(pencil, xcos_t, xsin_t, swap_t, weight, count)


def slab_exchange(blocks, parts, exchange_id):
    return pl.pallas_call(
        functools.partial(slab_exchange_kernel, parts),
        out_shape=jax.ShapeDtypeStruct(blocks.shape, blocks.dtype),
        in_specs=[pl.BlockSpec(memory_space=pltpu.VMEM)],
        out_specs=pl.BlockSpec(memory_space=pltpu.VMEM),
        scratch_shapes=[
            pltpu.VMEM(blocks.shape, blocks.dtype),
            pltpu.SemaphoreType.DMA((parts,)),
            pltpu.SemaphoreType.DMA((parts,)),
        ],
        compiler_params=pltpu.CompilerParams(collective_id=exchange_id, has_side_effects=True),
    )(blocks)


def local(
    base_field,
    forcing,
    load,
    amplitudes,
    amp_index,
    mode_count,
    point_weight,
    point_bias,
    spectral_weight,
):
    channels, slab_rows, plane_count, length_y = base_field.shape
    slab_count = lax.axis_size("slab")
    local_modes = spectral_weight.shape[0]
    modes_y = local_modes * slab_count
    modes_x = spectral_weight.shape[1]
    length_x = slab_rows * slab_count
    packed_width = 2 * channels * plane_count
    slab_index = lax.axis_index("slab")
    level_ids = jnp.arange(amplitudes.shape[0], dtype=jnp.int32)
    amplitude = jnp.sum(jnp.where(level_ids == amp_index[0], amplitudes, 0.0))
    cells = slab_rows * plane_count
    driven = base_field.reshape(channels, cells * length_y).astype(jnp.float32) + amplitude * load[
        :, None
    ] * forcing.reshape(1, cells * length_y).astype(jnp.float32)
    field_rows = (2.0 * jnp.tanh(0.5 * driven)).astype(jnp.bfloat16)
    field_now = field_rows.reshape(channels, slab_rows, plane_count, length_y)
    y_cos, y_sin = phase_tables(np.arange(modes_y), np.arange(length_y), length_y)
    y_real = jnp.einsum(
        "cxzy,ky->kxcz", field_now, bf16_constant(y_cos), preferred_element_type=jnp.float32
    )
    y_imag = -jnp.einsum(
        "cxzy,ky->kxcz", field_now, bf16_constant(y_sin), preferred_element_type=jnp.float32
    )
    packed = (
        jnp.stack([y_real, y_imag], axis=2)
        .transpose(0, 1, 4, 2, 3)
        .astype(jnp.bfloat16)
        .reshape(modes_y, slab_rows, packed_width)
    )
    frequency_x = np.concatenate(
        [np.arange(modes_x // 2), np.arange(length_x - modes_x // 2, length_x)]
    )
    full_cos, full_sin = phase_tables(frequency_x, np.arange(length_x), length_x)
    gathered = slab_exchange(packed, slab_count, 1).reshape(length_x, packed_width)
    lane = np.arange(packed_width)
    real_lane = (lane // channels) % 2 == 0
    swap = np.where(
        real_lane[None, :],
        (lane[:, None] == lane[None, :] + channels).astype(np.float32),
        -(lane[:, None] == lane[None, :] - channels).astype(np.float32),
    )
    weight = spectral_weight[0].transpose(1, 2, 3, 0)
    returned = mode_mix_exchange(
        gathered, bf16_constant(full_cos.T), bf16_constant(full_sin.T), bf16_constant(swap.T), weight,
        mode_count, slab_count,
    )
    weights_y = np.where(np.arange(modes_y) == 0, 1.0, 2.0).astype(np.float32) / np.float32(
        length_x * length_y
    )
    table = bf16_constant(
        np.concatenate([weights_y[:, None] * y_cos, -(weights_y[:, None] * y_sin)], axis=0)
    )
    bias = point_bias.reshape(channels, 1)
    members = lax.axis_size("member")
    total = layer_sum(returned, table, point_weight, field_rows, bias, members)
    return total.reshape(channels // members, slab_rows, plane_count, length_y)


def solution(mesh):
    in_specs = (
        P(None, "slab", None, None),
        P("slab", None, None),
        P(),
        P(),
        P("member"),
        P("member"),
        P(),
        P(),
        P("slab", None, None, None, None),
    )
    out_specs = P("member", "slab", None, None)
    return jax.shard_map(local, mesh=mesh, in_specs=in_specs, out_specs=out_specs, check_vma=False)
```

```python
import functools
import math

import jax
import ml_dtypes
import numpy as np
import jax.numpy as jnp
from jax import lax
from jax.experimental import pallas as pl
from jax.experimental.pallas import tpu as pltpu
from jax.sharding import PartitionSpec as P

TWO_PI = 2.0 * math.pi


def phase_tables(frequency, positions, length):
    product = np.outer(frequency, positions) % length
    angles = (product.astype(np.float32) * np.float32(TWO_PI / length)).astype(np.float64)
    return np.cos(angles).astype(np.float32), np.sin(angles).astype(np.float32)


def bf16_constant(values):
    return jnp.asarray(np.asarray(values, np.float32).astype(ml_dtypes.bfloat16))


def phases(frequency, positions, length):
    product = frequency[:, None] * positions[None, :] % length
    angles = product.astype(jnp.float32) * (TWO_PI / length)
    return (jnp.cos(angles), jnp.sin(angles))


def forward_x(pencil, cos_table, sin_table):
    row_total = pencil.shape[0]
    modes = cos_table.shape[0]
    with_cos = jnp.einsum(
        "kxf,mx->kmf", pencil, cos_table, preferred_element_type=jnp.float32
    ).reshape(row_total, modes, 2, -1)
    with_sin = jnp.einsum(
        "kxf,mx->kmf", pencil, sin_table, preferred_element_type=jnp.float32
    ).reshape(row_total, modes, 2, -1)
    real_part = with_cos[:, :, 0] + with_sin[:, :, 1]
    imag_part = with_cos[:, :, 1] - with_sin[:, :, 0]
    return jnp.stack([real_part, imag_part], axis=2).reshape(row_total, modes, -1)


def inverse_x(spectra, cos_table, sin_table):
    row_total = spectra.shape[0]
    points = cos_table.shape[1]
    with_cos = jnp.einsum(
        "kmf,mx->kxf", spectra, cos_table, preferred_element_type=jnp.float32
    ).reshape(row_total, points, 2, -1)
    with_sin = jnp.einsum(
        "kmf,mx->kxf", spectra, sin_table, preferred_element_type=jnp.float32
    ).reshape(row_total, points, 2, -1)
    real_part = with_cos[:, :, 0] - with_sin[:, :, 1]
    imag_part = with_cos[:, :, 1] + with_sin[:, :, 0]
    return jnp.stack([real_part, imag_part], axis=2).reshape(row_total, points, -1)


def mixing(weights, values):
    return jnp.einsum("kmoi,kmiz->kmoz", weights, values, preferred_element_type=jnp.float32)


def layer_sum_kernel(members, back_ref, table_ref, weight_ref, field_ref, bias_ref, out_ref, value, layer,
                     near, part, far, near_sems, far_send, far_recv):
    me = lax.axis_index("member")
    slab = lax.axis_index("slab")
    chips = members // 2
    chip, core = me // 2, me % 2
    sibling = chip * 2 + 1 - core
    mesh_kind = pl.DeviceIdType.MESH
    barrier = pltpu.get_barrier_semaphore()
    pl.semaphore_signal(barrier, inc=1, device_id=(sibling, slab), device_id_type=mesh_kind)
    for step in range(1, chips):
        peer = lax.rem(chip + step, chips) * 2 + core
        pl.semaphore_signal(barrier, inc=1, device_id=(peer, slab), device_id_type=mesh_kind)
    modes, slab_rows, width = back_ref.shape
    channels = weight_ref.shape[0]
    planes = width // (2 * channels)
    length = table_ref.shape[1]
    block_rows = layer.shape[2]
    table_real = table_ref[:modes, :]
    table_imag = table_ref[modes:, :]
    padding = jnp.zeros((width - modes, width), jnp.float32)
    for row in range(slab_rows):
        pencil = back_ref[:, row, :].astype(jnp.float32)
        pencil_t = jnp.concatenate([pencil, padding], axis=0).T[:, :modes].astype(back_ref.dtype)
        for plane in range(planes):
            cell = row * planes + plane
            base = plane * 2 * channels
            lanes = pl.ds(cell * length, length)
            spectral = jnp.dot(
                pencil_t[base:base + channels], table_real, preferred_element_type=jnp.float32
            )
            spectral = spectral + jnp.dot(
                pencil_t[base + channels:base + 2 * channels], table_imag,
                preferred_element_type=jnp.float32,
            )
            pointwise = jnp.dot(weight_ref[...], field_ref[:, lanes], preferred_element_type=jnp.float32)
            value[:, lanes] = jax.nn.gelu(pointwise + bias_ref[...] + spectral, approximate=True)
    for block in range(members):
        rows = pl.ds(block * block_rows, block_rows)
        layer[block % 2, block // 2] = value[rows, :].astype(layer.dtype)
    pl.semaphore_wait(barrier, chips)

    on_chip = pltpu.make_async_remote_copy(
        src_ref=layer.at[1 - core],
        dst_ref=near,
        send_sem=near_sems.at[0],
        recv_sem=near_sems.at[1],
        device_id=(sibling, slab),
        device_id_type=mesh_kind,
    )
    on_chip.start()
    on_chip.wait_recv()
    for index in range(chips):
        pair = layer[core, index].astype(jnp.float32) + near[index].astype(jnp.float32)
        part[index] = pair.astype(part.dtype)
    on_chip.wait_send()

    def copy_of(source, target, peer_chip):
        return pltpu.make_async_remote_copy(
            src_ref=part.at[source],
            dst_ref=far.at[target],
            send_sem=far_send.at[source],
            recv_sem=far_recv.at[target],
            device_id=(peer_chip * 2 + core, slab),
            device_id_type=mesh_kind,
        )

    for step in range(1, chips):
        peer = lax.rem(chip + step, chips)
        copy_of(peer, chip, peer).start()
    total = part[chip].astype(jnp.float32)
    for step in range(1, chips):
        source = lax.rem(chip + chips - step, chips)
        copy_of(source, source, source).wait_recv()
        total = total + far[source].astype(jnp.float32)
    for step in range(1, chips):
        peer = lax.rem(chip + step, chips)
        copy_of(peer, chip, peer).wait_send()
    out_ref[...] = (total / members).astype(out_ref.dtype)


def layer_sum(back, table, weight, field, bias, members):
    channels, width = field.shape
    block_rows = channels // members
    chips = members // 2
    return pl.pallas_call(
        functools.partial(layer_sum_kernel, members),
        out_shape=jax.ShapeDtypeStruct((block_rows, width), jnp.bfloat16),
        in_specs=[pl.BlockSpec(memory_space=pltpu.VMEM)] * 5,
        out_specs=pl.BlockSpec(memory_space=pltpu.VMEM),
        scratch_shapes=[
            pltpu.VMEM((channels, width), jnp.float32),
            pltpu.VMEM((2, chips, block_rows, width), jnp.bfloat16),
            pltpu.VMEM((chips, block_rows, width), jnp.bfloat16),
            pltpu.VMEM((chips, block_rows, width), jnp.bfloat16),
            pltpu.VMEM((chips, block_rows, width), jnp.bfloat16),
            pltpu.SemaphoreType.DMA((2,)),
            pltpu.SemaphoreType.DMA((chips,)),
            pltpu.SemaphoreType.DMA((chips,)),
        ],
        compiler_params=pltpu.CompilerParams(collective_id=0, has_side_effects=True),
    )(back, table, weight, field, bias)


def greet_slab(parts):
    me = lax.axis_index("slab")
    member = lax.axis_index("member")
    barrier = pltpu.get_barrier_semaphore()
    for step in range(1, parts):
        peer = lax.rem(me + step, parts)
        pl.semaphore_signal(barrier, inc=1, device_id=(member, peer), device_id_type=pl.DeviceIdType.MESH)
    return barrier


def swap_blocks(parts, source_ref, out_ref, landed, send_sems, recv_sems):
    me = lax.axis_index("slab")
    member = lax.axis_index("member")

    def copy_of(source, target, peer):
        return pltpu.make_async_remote_copy(
            src_ref=source_ref.at[source],
            dst_ref=landed.at[target],
            send_sem=send_sems.at[source],
            recv_sem=recv_sems.at[target],
            device_id=(member, peer),
            device_id_type=pl.DeviceIdType.MESH,
        )

    for step in range(1, parts):
        peer = lax.rem(me + step, parts)
        copy_of(peer, me, peer).start()
    landed[me] = source_ref[me]
    for step in range(1, parts):
        source = lax.rem(me + parts - step, parts)
        copy_of(source, source, source).wait_recv()
    for step in range(1, parts):
        peer = lax.rem(me + step, parts)
        copy_of(peer, me, peer).wait_send()
    out_ref[...] = landed[...]


def slab_exchange_kernel(parts, blocks_ref, out_ref, landed, send_sems, recv_sems):
    barrier = greet_slab(parts)
    pl.semaphore_wait(barrier, parts - 1)
    swap_blocks(parts, blocks_ref, out_ref, landed, send_sems, recv_sems)


def mode_mix_kernel(parts, pencil_ref, xcos_t_ref, xsin_t_ref, swap_t_ref, weight_ref, count_ref, out_ref,
                    mixed_t, blocks, landed, send_sems, recv_sems):
    barrier = greet_slab(parts)
    pencil_t = pencil_ref[...].astype(jnp.float32).T.astype(pencil_ref.dtype)
    swap_t = swap_t_ref[...]
    swapped_t = jnp.dot(swap_t, pencil_t, preferred_element_type=jnp.float32).astype(pencil_t.dtype)
    spec_t = jnp.dot(pencil_t, xcos_t_ref[...], preferred_element_type=jnp.float32)
    spec_t = spec_t + jnp.dot(swapped_t, xsin_t_ref[...], preferred_element_type=jnp.float32)
    spec_t = spec_t.astype(pencil_t.dtype).astype(jnp.float32)
    outputs = weight_ref.shape[1]
    planes = spec_t.shape[0] // (2 * outputs)
    for plane in range(planes):
        base = plane * 2 * outputs
        real = spec_t[base:base + outputs, :]
        imag = spec_t[base + outputs:base + 2 * outputs, :]
        for out in range(outputs):
            weight_real = weight_ref[0, out].astype(jnp.float32)
            weight_imag = weight_ref[1, out].astype(jnp.float32)
            mixed_t[pl.ds(base + out, 1), :] = jnp.sum(
                weight_real * real - weight_imag * imag, axis=0, keepdims=True
            )
            mixed_t[pl.ds(base + outputs + out, 1), :] = jnp.sum(
                weight_imag * real + weight_real * imag, axis=0, keepdims=True
            )
    kept = (lax.axis_index("slab") < count_ref[0]).astype(jnp.float32)
    mixed = (mixed_t[...] * kept).astype(pencil_t.dtype)
    mixed_swapped = jnp.dot(swap_t, mixed, preferred_element_type=jnp.float32).astype(pencil_t.dtype)
    contract = (((1,), (1,)), ((), ()))
    back = lax.dot_general(xcos_t_ref[...], mixed, contract, preferred_element_type=jnp.float32)
    back = back - lax.dot_general(
        xsin_t_ref[...], mixed_swapped, contract, preferred_element_type=jnp.float32
    )
    blocks[...] = back.reshape(blocks.shape).astype(blocks.dtype)
    pl.semaphore_wait(barrier, parts - 1)
    swap_blocks(parts, blocks, out_ref, landed, send_sems, recv_sems)


def mode_mix_exchange(pencil, xcos_t, xsin_t, swap_t, weight, count, parts):
    points, width = pencil.shape
    modes = xcos_t.shape[1]
    shape = (parts, points // parts, width)
    return pl.pallas_call(
        functools.partial(mode_mix_kernel, parts),
        out_shape=jax.ShapeDtypeStruct(shape, pencil.dtype),
        in_specs=[pl.BlockSpec(memory_space=pltpu.VMEM)] * 5
        + [pl.BlockSpec(memory_space=pltpu.SMEM)],
        out_specs=pl.BlockSpec(memory_space=pltpu.VMEM),
        scratch_shapes=[
            pltpu.VMEM((width, modes), jnp.float32),
            pltpu.VMEM(shape, pencil.dtype),
            pltpu.VMEM(shape, pencil.dtype),
            pltpu.SemaphoreType.DMA((parts,)),
            pltpu.SemaphoreType.DMA((parts,)),
        ],
        compiler_params=pltpu.CompilerParams(collective_id=2, has_side_effects=True),
    )(pencil, xcos_t, xsin_t, swap_t, weight, count)


def slab_exchange(blocks, parts, exchange_id):
    return pl.pallas_call(
        functools.partial(slab_exchange_kernel, parts),
        out_shape=jax.ShapeDtypeStruct(blocks.shape, blocks.dtype),
        in_specs=[pl.BlockSpec(memory_space=pltpu.VMEM)],
        out_specs=pl.BlockSpec(memory_space=pltpu.VMEM),
        scratch_shapes=[
            pltpu.VMEM(blocks.shape, blocks.dtype),
            pltpu.SemaphoreType.DMA((parts,)),
            pltpu.SemaphoreType.DMA((parts,)),
        ],
        compiler_params=pltpu.CompilerParams(collective_id=exchange_id, has_side_effects=True),
    )(blocks)


def local(
    base_field,
    forcing,
    load,
    amplitudes,
    amp_index,
    mode_count,
    point_weight,
    point_bias,
    spectral_weight,
):
    channels, slab_rows, plane_count, length_y = base_field.shape
    slab_count = lax.axis_size("slab")
    local_modes = spectral_weight.shape[0]
    modes_y = local_modes * slab_count
    modes_x = spectral_weight.shape[1]
    length_x = slab_rows * slab_count
    packed_width = 2 * channels * plane_count
    slab_index = lax.axis_index("slab")
    level_ids = jnp.arange(amplitudes.shape[0], dtype=jnp.int32)
    amplitude = jnp.sum(jnp.where(level_ids == amp_index[0], amplitudes, 0.0))
    cells = slab_rows * plane_count
    driven = base_field.reshape(channels, cells * length_y).astype(jnp.float32) + amplitude * load[
        :, None
    ] * forcing.reshape(1, cells * length_y).astype(jnp.float32)
    field_rows = (2.0 * jnp.tanh(0.5 * driven)).astype(jnp.bfloat16)
    field_now = field_rows.reshape(channels, slab_rows, plane_count, length_y)
    y_cos, y_sin = phase_tables(np.arange(modes_y), np.arange(length_y), length_y)
    forward_table = bf16_constant(np.stack([y_cos, -y_sin]))
    packed = (
        jnp.einsum("cxzy,rky->kxzrc", field_now, forward_table, preferred_element_type=jnp.float32)
        .astype(jnp.bfloat16)
        .reshape(modes_y, slab_rows, packed_width)
    )
    frequency_x = np.concatenate(
        [np.arange(modes_x // 2), np.arange(length_x - modes_x // 2, length_x)]
    )
    full_cos, full_sin = phase_tables(frequency_x, np.arange(length_x), length_x)
    gathered = slab_exchange(packed, slab_count, 1).reshape(length_x, packed_width)
    lane = np.arange(packed_width)
    real_lane = (lane // channels) % 2 == 0
    swap = np.where(
        real_lane[None, :],
        (lane[:, None] == lane[None, :] + channels).astype(np.float32),
        -(lane[:, None] == lane[None, :] - channels).astype(np.float32),
    )
    weight = spectral_weight[0].transpose(1, 2, 3, 0)
    returned = mode_mix_exchange(
        gathered, bf16_constant(full_cos.T), bf16_constant(full_sin.T), bf16_constant(swap.T), weight,
        mode_count, slab_count,
    )
    weights_y = np.where(np.arange(modes_y) == 0, 1.0, 2.0).astype(np.float32) / np.float32(
        length_x * length_y
    )
    table = bf16_constant(
        np.concatenate([weights_y[:, None] * y_cos, -(weights_y[:, None] * y_sin)], axis=0)
    )
    bias = point_bias.reshape(channels, 1)
    members = lax.axis_size("member")
    total = layer_sum(returned, table, point_weight, field_rows, bias, members)
    return total.reshape(channels // members, slab_rows, plane_count, length_y)


def solution(mesh):
    in_specs = (
        P(None, "slab", None, None),
        P("slab", None, None),
        P(),
        P(),
        P("member"),
        P("member"),
        P(),
        P(),
        P("slab", None, None, None, None),
    )
    out_specs = P("member", "slab", None, None)
    return jax.shard_map(local, mesh=mesh, in_specs=in_specs, out_specs=out_specs, check_vma=False)
```

```python
import functools
import math

import jax
import ml_dtypes
import numpy as np
import jax.numpy as jnp
from jax import lax
from jax.experimental import pallas as pl
from jax.experimental.pallas import tpu as pltpu
from jax.sharding import PartitionSpec as P

TWO_PI = 2.0 * math.pi


def phase_tables(frequency, positions, length):
    product = np.outer(frequency, positions) % length
    angles = (product.astype(np.float32) * np.float32(TWO_PI / length)).astype(np.float64)
    return np.cos(angles).astype(np.float32), np.sin(angles).astype(np.float32)


def bf16_constant(values):
    return jnp.asarray(np.asarray(values, np.float32).astype(ml_dtypes.bfloat16))


def phases(frequency, positions, length):
    product = frequency[:, None] * positions[None, :] % length
    angles = product.astype(jnp.float32) * (TWO_PI / length)
    return (jnp.cos(angles), jnp.sin(angles))


def forward_x(pencil, cos_table, sin_table):
    row_total = pencil.shape[0]
    modes = cos_table.shape[0]
    with_cos = jnp.einsum(
        "kxf,mx->kmf", pencil, cos_table, preferred_element_type=jnp.float32
    ).reshape(row_total, modes, 2, -1)
    with_sin = jnp.einsum(
        "kxf,mx->kmf", pencil, sin_table, preferred_element_type=jnp.float32
    ).reshape(row_total, modes, 2, -1)
    real_part = with_cos[:, :, 0] + with_sin[:, :, 1]
    imag_part = with_cos[:, :, 1] - with_sin[:, :, 0]
    return jnp.stack([real_part, imag_part], axis=2).reshape(row_total, modes, -1)


def inverse_x(spectra, cos_table, sin_table):
    row_total = spectra.shape[0]
    points = cos_table.shape[1]
    with_cos = jnp.einsum(
        "kmf,mx->kxf", spectra, cos_table, preferred_element_type=jnp.float32
    ).reshape(row_total, points, 2, -1)
    with_sin = jnp.einsum(
        "kmf,mx->kxf", spectra, sin_table, preferred_element_type=jnp.float32
    ).reshape(row_total, points, 2, -1)
    real_part = with_cos[:, :, 0] - with_sin[:, :, 1]
    imag_part = with_cos[:, :, 1] + with_sin[:, :, 0]
    return jnp.stack([real_part, imag_part], axis=2).reshape(row_total, points, -1)


def mixing(weights, values):
    return jnp.einsum("kmoi,kmiz->kmoz", weights, values, preferred_element_type=jnp.float32)


def layer_sum_kernel(members, back_ref, table_ref, weight_ref, field_ref, bias_ref, out_ref, value, layer,
                     near, part, far, near_sems, far_send, far_recv):
    me = lax.axis_index("member")
    slab = lax.axis_index("slab")
    chips = members // 2
    chip, core = me // 2, me % 2
    sibling = chip * 2 + 1 - core
    mesh_kind = pl.DeviceIdType.MESH
    barrier = pltpu.get_barrier_semaphore()
    pl.semaphore_signal(barrier, inc=1, device_id=(sibling, slab), device_id_type=mesh_kind)
    for step in range(1, chips):
        peer = lax.rem(chip + step, chips) * 2 + core
        pl.semaphore_signal(barrier, inc=1, device_id=(peer, slab), device_id_type=mesh_kind)
    modes, slab_rows, width = back_ref.shape
    channels = weight_ref.shape[0]
    planes = width // (2 * channels)
    length = table_ref.shape[1]
    block_rows = layer.shape[2]
    table_real = table_ref[:modes, :]
    table_imag = table_ref[modes:, :]
    padding = jnp.zeros((width - modes, width), jnp.float32)
    for row in range(slab_rows):
        pencil = back_ref[:, row, :].astype(jnp.float32)
        pencil_t = jnp.concatenate([pencil, padding], axis=0).T[:, :modes].astype(back_ref.dtype)
        for plane in range(planes):
            cell = row * planes + plane
            base = plane * 2 * channels
            lanes = pl.ds(cell * length, length)
            spectral = jnp.dot(
                pencil_t[base:base + channels], table_real, preferred_element_type=jnp.float32
            )
            spectral = spectral + jnp.dot(
                pencil_t[base + channels:base + 2 * channels], table_imag,
                preferred_element_type=jnp.float32,
            )
            pointwise = jnp.dot(weight_ref[...], field_ref[:, lanes], preferred_element_type=jnp.float32)
            value[:, lanes] = jax.nn.gelu(pointwise + bias_ref[...] + spectral, approximate=True)
    for block in range(members):
        rows = pl.ds(block * block_rows, block_rows)
        layer[block % 2, block // 2] = value[rows, :].astype(layer.dtype)
    pl.semaphore_wait(barrier, chips)

    on_chip = pltpu.make_async_remote_copy(
        src_ref=layer.at[1 - core],
        dst_ref=near,
        send_sem=near_sems.at[0],
        recv_sem=near_sems.at[1],
        device_id=(sibling, slab),
        device_id_type=mesh_kind,
    )
    on_chip.start()
    on_chip.wait_recv()
    for index in range(chips):
        pair = layer[core, index].astype(jnp.float32) + near[index].astype(jnp.float32)
        part[index] = pair.astype(part.dtype)
    on_chip.wait_send()

    def copy_of(source, target, peer_chip):
        return pltpu.make_async_remote_copy(
            src_ref=part.at[source],
            dst_ref=far.at[target],
            send_sem=far_send.at[source],
            recv_sem=far_recv.at[target],
            device_id=(peer_chip * 2 + core, slab),
            device_id_type=mesh_kind,
        )

    for step in range(1, chips):
        peer = lax.rem(chip + step, chips)
        copy_of(peer, chip, peer).start()
    total = part[chip].astype(jnp.float32)
    for step in range(1, chips):
        source = lax.rem(chip + chips - step, chips)
        copy_of(source, source, source).wait_recv()
        total = total + far[source].astype(jnp.float32)
    for step in range(1, chips):
        peer = lax.rem(chip + step, chips)
        copy_of(peer, chip, peer).wait_send()
    out_ref[...] = (total / members).astype(out_ref.dtype)


def layer_sum(back, table, weight, field, bias, members):
    channels, width = field.shape
    block_rows = channels // members
    chips = members // 2
    return pl.pallas_call(
        functools.partial(layer_sum_kernel, members),
        out_shape=jax.ShapeDtypeStruct((block_rows, width), jnp.bfloat16),
        in_specs=[pl.BlockSpec(memory_space=pltpu.VMEM)] * 5,
        out_specs=pl.BlockSpec(memory_space=pltpu.VMEM),
        scratch_shapes=[
            pltpu.VMEM((channels, width), jnp.float32),
            pltpu.VMEM((2, chips, block_rows, width), jnp.bfloat16),
            pltpu.VMEM((chips, block_rows, width), jnp.bfloat16),
            pltpu.VMEM((chips, block_rows, width), jnp.bfloat16),
            pltpu.VMEM((chips, block_rows, width), jnp.bfloat16),
            pltpu.SemaphoreType.DMA((2,)),
            pltpu.SemaphoreType.DMA((chips,)),
            pltpu.SemaphoreType.DMA((chips,)),
        ],
        compiler_params=pltpu.CompilerParams(collective_id=0, has_side_effects=True),
    )(back, table, weight, field, bias)


def greet_slab(parts):
    me = lax.axis_index("slab")
    member = lax.axis_index("member")
    barrier = pltpu.get_barrier_semaphore()
    for step in range(1, parts):
        peer = lax.rem(me + step, parts)
        pl.semaphore_signal(barrier, inc=1, device_id=(member, peer), device_id_type=pl.DeviceIdType.MESH)
    return barrier


def swap_blocks(parts, source_ref, out_ref, landed, send_sems, recv_sems):
    me = lax.axis_index("slab")
    member = lax.axis_index("member")

    def copy_of(source, target, peer):
        return pltpu.make_async_remote_copy(
            src_ref=source_ref.at[source],
            dst_ref=landed.at[target],
            send_sem=send_sems.at[source],
            recv_sem=recv_sems.at[target],
            device_id=(member, peer),
            device_id_type=pl.DeviceIdType.MESH,
        )

    for step in range(1, parts):
        peer = lax.rem(me + step, parts)
        copy_of(peer, me, peer).start()
    landed[me] = source_ref[me]
    for step in range(1, parts):
        source = lax.rem(me + parts - step, parts)
        copy_of(source, source, source).wait_recv()
    for step in range(1, parts):
        peer = lax.rem(me + step, parts)
        copy_of(peer, me, peer).wait_send()
    if out_ref is not None:
        out_ref[...] = landed[...]


def slab_exchange_kernel(parts, blocks_ref, out_ref, landed, send_sems, recv_sems):
    barrier = greet_slab(parts)
    pl.semaphore_wait(barrier, parts - 1)
    swap_blocks(parts, blocks_ref, out_ref, landed, send_sems, recv_sems)


def mode_mix_kernel(parts, modes_ref, xcos_t_ref, xsin_t_ref, swap_t_ref, weight_ref, count_ref, out_ref,
                    mixed_t, first, blocks, landed, first_send, first_recv, send_sems, recv_sems):
    barrier = greet_slab(parts)
    pl.semaphore_wait(barrier, parts - 1)
    swap_blocks(parts, modes_ref, None, first, first_send, first_recv)
    pencil = first[...].astype(jnp.float32)
    pencil = pencil.reshape(pencil.shape[0] * pencil.shape[1], pencil.shape[2])
    pencil_t = pencil.T.astype(modes_ref.dtype)
    swap_t = swap_t_ref[...]
    swapped_t = jnp.dot(swap_t, pencil_t, preferred_element_type=jnp.float32).astype(pencil_t.dtype)
    spec_t = jnp.dot(pencil_t, xcos_t_ref[...], preferred_element_type=jnp.float32)
    spec_t = spec_t + jnp.dot(swapped_t, xsin_t_ref[...], preferred_element_type=jnp.float32)
    spec_t = spec_t.astype(pencil_t.dtype).astype(jnp.float32)
    outputs = weight_ref.shape[1]
    planes = spec_t.shape[0] // (2 * outputs)
    for plane in range(planes):
        base = plane * 2 * outputs
        real = spec_t[base:base + outputs, :]
        imag = spec_t[base + outputs:base + 2 * outputs, :]
        for out in range(outputs):
            weight_real = weight_ref[0, out].astype(jnp.float32)
            weight_imag = weight_ref[1, out].astype(jnp.float32)
            mixed_t[pl.ds(base + out, 1), :] = jnp.sum(
                weight_real * real - weight_imag * imag, axis=0, keepdims=True
            )
            mixed_t[pl.ds(base + outputs + out, 1), :] = jnp.sum(
                weight_imag * real + weight_real * imag, axis=0, keepdims=True
            )
    kept = (lax.axis_index("slab") < count_ref[0]).astype(jnp.float32)
    mixed = (mixed_t[...] * kept).astype(pencil_t.dtype)
    mixed_swapped = jnp.dot(swap_t, mixed, preferred_element_type=jnp.float32).astype(pencil_t.dtype)
    contract = (((1,), (1,)), ((), ()))
    back = lax.dot_general(xcos_t_ref[...], mixed, contract, preferred_element_type=jnp.float32)
    back = back - lax.dot_general(
        xsin_t_ref[...], mixed_swapped, contract, preferred_element_type=jnp.float32
    )
    blocks[...] = back.reshape(blocks.shape).astype(blocks.dtype)
    swap_blocks(parts, blocks, out_ref, landed, send_sems, recv_sems)


def mode_mix_exchange(pencil, xcos_t, xsin_t, swap_t, weight, count, parts):
    shape = pencil.shape
    width = shape[2]
    modes = xcos_t.shape[1]
    return pl.pallas_call(
        functools.partial(mode_mix_kernel, parts),
        out_shape=jax.ShapeDtypeStruct(shape, pencil.dtype),
        in_specs=[pl.BlockSpec(memory_space=pltpu.VMEM)] * 5
        + [pl.BlockSpec(memory_space=pltpu.SMEM)],
        out_specs=pl.BlockSpec(memory_space=pltpu.VMEM),
        scratch_shapes=[
            pltpu.VMEM((width, modes), jnp.float32),
            pltpu.VMEM(shape, pencil.dtype),
            pltpu.VMEM(shape, pencil.dtype),
            pltpu.VMEM(shape, pencil.dtype),
            pltpu.SemaphoreType.DMA((parts,)),
            pltpu.SemaphoreType.DMA((parts,)),
            pltpu.SemaphoreType.DMA((parts,)),
            pltpu.SemaphoreType.DMA((parts,)),
        ],
        compiler_params=pltpu.CompilerParams(collective_id=2, has_side_effects=True),
    )(pencil, xcos_t, xsin_t, swap_t, weight, count)


def slab_exchange(blocks, parts, exchange_id):
    return pl.pallas_call(
        functools.partial(slab_exchange_kernel, parts),
        out_shape=jax.ShapeDtypeStruct(blocks.shape, blocks.dtype),
        in_specs=[pl.BlockSpec(memory_space=pltpu.VMEM)],
        out_specs=pl.BlockSpec(memory_space=pltpu.VMEM),
        scratch_shapes=[
            pltpu.VMEM(blocks.shape, blocks.dtype),
            pltpu.SemaphoreType.DMA((parts,)),
            pltpu.SemaphoreType.DMA((parts,)),
        ],
        compiler_params=pltpu.CompilerParams(collective_id=exchange_id, has_side_effects=True),
    )(blocks)


def local(
    base_field,
    forcing,
    load,
    amplitudes,
    amp_index,
    mode_count,
    point_weight,
    point_bias,
    spectral_weight,
):
    channels, slab_rows, plane_count, length_y = base_field.shape
    slab_count = lax.axis_size("slab")
    local_modes = spectral_weight.shape[0]
    modes_y = local_modes * slab_count
    modes_x = spectral_weight.shape[1]
    length_x = slab_rows * slab_count
    packed_width = 2 * channels * plane_count
    slab_index = lax.axis_index("slab")
    level_ids = jnp.arange(amplitudes.shape[0], dtype=jnp.int32)
    amplitude = jnp.sum(jnp.where(level_ids == amp_index[0], amplitudes, 0.0))
    cells = slab_rows * plane_count
    driven = base_field.reshape(channels, cells * length_y).astype(jnp.float32) + amplitude * load[
        :, None
    ] * forcing.reshape(1, cells * length_y).astype(jnp.float32)
    field_rows = (2.0 * jnp.tanh(0.5 * driven)).astype(jnp.bfloat16)
    field_now = field_rows.reshape(channels, slab_rows, plane_count, length_y)
    y_cos, y_sin = phase_tables(np.arange(modes_y), np.arange(length_y), length_y)
    forward_table = bf16_constant(np.stack([y_cos, -y_sin]))
    packed = (
        jnp.einsum("cxzy,rky->kxzrc", field_now, forward_table, preferred_element_type=jnp.float32)
        .astype(jnp.bfloat16)
        .reshape(modes_y, slab_rows, packed_width)
    )
    frequency_x = np.concatenate(
        [np.arange(modes_x // 2), np.arange(length_x - modes_x // 2, length_x)]
    )
    full_cos, full_sin = phase_tables(frequency_x, np.arange(length_x), length_x)
    lane = np.arange(packed_width)
    real_lane = (lane // channels) % 2 == 0
    swap = np.where(
        real_lane[None, :],
        (lane[:, None] == lane[None, :] + channels).astype(np.float32),
        -(lane[:, None] == lane[None, :] - channels).astype(np.float32),
    )
    weight = spectral_weight[0].transpose(1, 2, 3, 0)
    returned = mode_mix_exchange(
        packed, bf16_constant(full_cos.T), bf16_constant(full_sin.T), bf16_constant(swap.T), weight,
        mode_count, slab_count,
    )
    weights_y = np.where(np.arange(modes_y) == 0, 1.0, 2.0).astype(np.float32) / np.float32(
        length_x * length_y
    )
    table = bf16_constant(
        np.concatenate([weights_y[:, None] * y_cos, -(weights_y[:, None] * y_sin)], axis=0)
    )
    bias = point_bias.reshape(channels, 1)
    members = lax.axis_size("member")
    total = layer_sum(returned, table, point_weight, field_rows, bias, members)
    return total.reshape(channels // members, slab_rows, plane_count, length_y)


def solution(mesh):
    in_specs = (
        P(None, "slab", None, None),
        P("slab", None, None),
        P(),
        P(),
        P("member"),
        P("member"),
        P(),
        P(),
        P("slab", None, None, None, None),
    )
    out_specs = P("member", "slab", None, None)
    return jax.shard_map(local, mesh=mesh, in_specs=in_specs, out_specs=out_specs, check_vma=False)
```

```python
import functools
import math

import jax
import ml_dtypes
import numpy as np
import jax.numpy as jnp
from jax import lax
from jax.experimental import pallas as pl
from jax.experimental.pallas import tpu as pltpu
from jax.sharding import PartitionSpec as P

TWO_PI = 2.0 * math.pi


def phase_tables(frequency, positions, length):
    product = np.outer(frequency, positions) % length
    angles = (product.astype(np.float32) * np.float32(TWO_PI / length)).astype(np.float64)
    return np.cos(angles).astype(np.float32), np.sin(angles).astype(np.float32)


def bf16_constant(values):
    return jnp.asarray(np.asarray(values, np.float32).astype(ml_dtypes.bfloat16))


def phases(frequency, positions, length):
    product = frequency[:, None] * positions[None, :] % length
    angles = product.astype(jnp.float32) * (TWO_PI / length)
    return (jnp.cos(angles), jnp.sin(angles))


def forward_x(pencil, cos_table, sin_table):
    row_total = pencil.shape[0]
    modes = cos_table.shape[0]
    with_cos = jnp.einsum(
        "kxf,mx->kmf", pencil, cos_table, preferred_element_type=jnp.float32
    ).reshape(row_total, modes, 2, -1)
    with_sin = jnp.einsum(
        "kxf,mx->kmf", pencil, sin_table, preferred_element_type=jnp.float32
    ).reshape(row_total, modes, 2, -1)
    real_part = with_cos[:, :, 0] + with_sin[:, :, 1]
    imag_part = with_cos[:, :, 1] - with_sin[:, :, 0]
    return jnp.stack([real_part, imag_part], axis=2).reshape(row_total, modes, -1)


def inverse_x(spectra, cos_table, sin_table):
    row_total = spectra.shape[0]
    points = cos_table.shape[1]
    with_cos = jnp.einsum(
        "kmf,mx->kxf", spectra, cos_table, preferred_element_type=jnp.float32
    ).reshape(row_total, points, 2, -1)
    with_sin = jnp.einsum(
        "kmf,mx->kxf", spectra, sin_table, preferred_element_type=jnp.float32
    ).reshape(row_total, points, 2, -1)
    real_part = with_cos[:, :, 0] - with_sin[:, :, 1]
    imag_part = with_cos[:, :, 1] + with_sin[:, :, 0]
    return jnp.stack([real_part, imag_part], axis=2).reshape(row_total, points, -1)


def mixing(weights, values):
    return jnp.einsum("kmoi,kmiz->kmoz", weights, values, preferred_element_type=jnp.float32)


def layer_sum_kernel(members, back_ref, table_ref, weight_ref, field_ref, bias_ref, out_ref, value, layer,
                     near, part, far, near_sems, far_send, far_recv):
    me = lax.axis_index("member")
    slab = lax.axis_index("slab")
    chips = members // 2
    chip, core = me // 2, me % 2
    sibling = chip * 2 + 1 - core
    mesh_kind = pl.DeviceIdType.MESH
    barrier = pltpu.get_barrier_semaphore()
    pl.semaphore_signal(barrier, inc=1, device_id=(sibling, slab), device_id_type=mesh_kind)
    for step in range(1, chips):
        peer = lax.rem(chip + step, chips) * 2 + core
        pl.semaphore_signal(barrier, inc=1, device_id=(peer, slab), device_id_type=mesh_kind)
    modes, slab_rows, width = back_ref.shape
    channels = weight_ref.shape[0]
    planes = width // (2 * channels)
    length = table_ref.shape[1]
    block_rows = layer.shape[2]
    table_real = table_ref[:modes, :]
    table_imag = table_ref[modes:, :]
    padding = jnp.zeros((width - modes, width), jnp.float32)
    for row in range(slab_rows):
        pencil = back_ref[:, row, :].astype(jnp.float32)
        pencil_t = jnp.concatenate([pencil, padding], axis=0).T[:, :modes].astype(back_ref.dtype)
        for plane in range(planes):
            cell = row * planes + plane
            base = plane * 2 * channels
            lanes = pl.ds(cell * length, length)
            spectral = jnp.dot(
                pencil_t[base:base + channels], table_real, preferred_element_type=jnp.float32
            )
            spectral = spectral + jnp.dot(
                pencil_t[base + channels:base + 2 * channels], table_imag,
                preferred_element_type=jnp.float32,
            )
            pointwise = jnp.dot(weight_ref[...], field_ref[:, lanes], preferred_element_type=jnp.float32)
            value[:, lanes] = jax.nn.gelu(pointwise + bias_ref[...] + spectral, approximate=True)
    for block in range(members):
        rows = pl.ds(block * block_rows, block_rows)
        layer[block % 2, block // 2] = value[rows, :].astype(layer.dtype)
    pl.semaphore_wait(barrier, chips)

    on_chip = pltpu.make_async_remote_copy(
        src_ref=layer.at[1 - core],
        dst_ref=near,
        send_sem=near_sems.at[0],
        recv_sem=near_sems.at[1],
        device_id=(sibling, slab),
        device_id_type=mesh_kind,
    )
    on_chip.start()
    on_chip.wait_recv()
    for index in range(chips):
        pair = layer[core, index].astype(jnp.float32) + near[index].astype(jnp.float32)
        part[index] = pair.astype(part.dtype)
    on_chip.wait_send()

    def copy_of(source, target, peer_chip):
        return pltpu.make_async_remote_copy(
            src_ref=part.at[source],
            dst_ref=far.at[target],
            send_sem=far_send.at[source],
            recv_sem=far_recv.at[target],
            device_id=(peer_chip * 2 + core, slab),
            device_id_type=mesh_kind,
        )

    for step in range(1, chips):
        peer = lax.rem(chip + step, chips)
        copy_of(peer, chip, peer).start()
    total = part[chip].astype(jnp.float32)
    for step in range(1, chips):
        source = lax.rem(chip + chips - step, chips)
        copy_of(source, source, source).wait_recv()
        total = total + far[source].astype(jnp.float32)
    for step in range(1, chips):
        peer = lax.rem(chip + step, chips)
        copy_of(peer, chip, peer).wait_send()
    out_ref[...] = (total / members).astype(out_ref.dtype)


def layer_sum(back, table, weight, field, bias, members):
    channels, width = field.shape
    block_rows = channels // members
    chips = members // 2
    return pl.pallas_call(
        functools.partial(layer_sum_kernel, members),
        out_shape=jax.ShapeDtypeStruct((block_rows, width), jnp.bfloat16),
        in_specs=[pl.BlockSpec(memory_space=pltpu.VMEM)] * 5,
        out_specs=pl.BlockSpec(memory_space=pltpu.VMEM),
        scratch_shapes=[
            pltpu.VMEM((channels, width), jnp.float32),
            pltpu.VMEM((2, chips, block_rows, width), jnp.bfloat16),
            pltpu.VMEM((chips, block_rows, width), jnp.bfloat16),
            pltpu.VMEM((chips, block_rows, width), jnp.bfloat16),
            pltpu.VMEM((chips, block_rows, width), jnp.bfloat16),
            pltpu.SemaphoreType.DMA((2,)),
            pltpu.SemaphoreType.DMA((chips,)),
            pltpu.SemaphoreType.DMA((chips,)),
        ],
        compiler_params=pltpu.CompilerParams(collective_id=0, has_side_effects=True),
    )(back, table, weight, field, bias)


def greet_slab(parts):
    me = lax.axis_index("slab")
    member = lax.axis_index("member")
    barrier = pltpu.get_barrier_semaphore()
    for step in range(1, parts):
        peer = lax.rem(me + step, parts)
        pl.semaphore_signal(barrier, inc=1, device_id=(member, peer), device_id_type=pl.DeviceIdType.MESH)
    return barrier


def swap_blocks(parts, source_ref, out_ref, landed, send_sems, recv_sems):
    me = lax.axis_index("slab")
    member = lax.axis_index("member")

    def copy_of(source, target, peer):
        return pltpu.make_async_remote_copy(
            src_ref=source_ref.at[source],
            dst_ref=landed.at[target],
            send_sem=send_sems.at[source],
            recv_sem=recv_sems.at[target],
            device_id=(member, peer),
            device_id_type=pl.DeviceIdType.MESH,
        )

    for step in range(1, parts):
        peer = lax.rem(me + step, parts)
        copy_of(peer, me, peer).start()
    landed[me] = source_ref[me]
    for step in range(1, parts):
        source = lax.rem(me + parts - step, parts)
        copy_of(source, source, source).wait_recv()
    for step in range(1, parts):
        peer = lax.rem(me + step, parts)
        copy_of(peer, me, peer).wait_send()
    if out_ref is not None:
        out_ref[...] = landed[...]


def slab_exchange_kernel(parts, blocks_ref, out_ref, landed, send_sems, recv_sems):
    barrier = greet_slab(parts)
    pl.semaphore_wait(barrier, parts - 1)
    swap_blocks(parts, blocks_ref, out_ref, landed, send_sems, recv_sems)


def mode_mix_kernel(parts, field_ref, table_ref, xcos_t_ref, xsin_t_ref, swap_t_ref, weight_ref, count_ref,
                    out_ref, mixed_t, modes_out, first, blocks, landed, first_send, first_recv, send_sems,
                    recv_sems):
    barrier = greet_slab(parts)
    modes, slab_rows, width = modes_out.shape
    channels = field_ref.shape[0]
    planes = width // (2 * channels)
    length = table_ref.shape[2]
    lane = lax.broadcasted_iota(jnp.int32, (modes, width), 1)
    real_lanes = (lane // channels) % 2 == 0
    contract_last = (((1,), (1,)), ((), ()))
    for row in range(slab_rows):
        pieces = []
        for plane in range(planes):
            cell = row * planes + plane
            values = field_ref[:, pl.ds(cell * length, length)]
            pieces += [values, values]
        stack = jnp.concatenate(pieces, axis=0)
        real = lax.dot_general(table_ref[0], stack, contract_last, preferred_element_type=jnp.float32)
        imag = lax.dot_general(table_ref[1], stack, contract_last, preferred_element_type=jnp.float32)
        modes_out[:, row, :] = jnp.where(real_lanes, real, imag).astype(modes_out.dtype)
    pl.semaphore_wait(barrier, parts - 1)
    swap_blocks(parts, modes_out, None, first, first_send, first_recv)
    pencil = first[...].astype(jnp.float32)
    pencil = pencil.reshape(pencil.shape[0] * pencil.shape[1], pencil.shape[2])
    pencil_t = pencil.T.astype(modes_out.dtype)
    swap_t = swap_t_ref[...]
    swapped_t = jnp.dot(swap_t, pencil_t, preferred_element_type=jnp.float32).astype(pencil_t.dtype)
    spec_t = jnp.dot(pencil_t, xcos_t_ref[...], preferred_element_type=jnp.float32)
    spec_t = spec_t + jnp.dot(swapped_t, xsin_t_ref[...], preferred_element_type=jnp.float32)
    spec_t = spec_t.astype(pencil_t.dtype).astype(jnp.float32)
    outputs = weight_ref.shape[1]
    planes = spec_t.shape[0] // (2 * outputs)
    for plane in range(planes):
        base = plane * 2 * outputs
        real = spec_t[base:base + outputs, :]
        imag = spec_t[base + outputs:base + 2 * outputs, :]
        for out in range(outputs):
            weight_real = weight_ref[0, out].astype(jnp.float32)
            weight_imag = weight_ref[1, out].astype(jnp.float32)
            mixed_t[pl.ds(base + out, 1), :] = jnp.sum(
                weight_real * real - weight_imag * imag, axis=0, keepdims=True
            )
            mixed_t[pl.ds(base + outputs + out, 1), :] = jnp.sum(
                weight_imag * real + weight_real * imag, axis=0, keepdims=True
            )
    kept = (lax.axis_index("slab") < count_ref[0]).astype(jnp.float32)
    mixed = (mixed_t[...] * kept).astype(pencil_t.dtype)
    mixed_swapped = jnp.dot(swap_t, mixed, preferred_element_type=jnp.float32).astype(pencil_t.dtype)
    contract = (((1,), (1,)), ((), ()))
    back = lax.dot_general(xcos_t_ref[...], mixed, contract, preferred_element_type=jnp.float32)
    back = back - lax.dot_general(
        xsin_t_ref[...], mixed_swapped, contract, preferred_element_type=jnp.float32
    )
    blocks[...] = back.reshape(blocks.shape).astype(blocks.dtype)
    swap_blocks(parts, blocks, out_ref, landed, send_sems, recv_sems)


def mode_mix_exchange(field, table, xcos_t, xsin_t, swap_t, weight, count, parts):
    channels = field.shape[0]
    modes, length = table.shape[1], table.shape[2]
    width = swap_t.shape[0]
    planes = width // (2 * channels)
    shape = (modes, field.shape[1] // (planes * length), width)
    pencil = field
    return pl.pallas_call(
        functools.partial(mode_mix_kernel, parts),
        out_shape=jax.ShapeDtypeStruct(shape, pencil.dtype),
        in_specs=[pl.BlockSpec(memory_space=pltpu.VMEM)] * 6
        + [pl.BlockSpec(memory_space=pltpu.SMEM)],
        out_specs=pl.BlockSpec(memory_space=pltpu.VMEM),
        scratch_shapes=[
            pltpu.VMEM((width, modes), jnp.float32),
            pltpu.VMEM(shape, pencil.dtype),
            pltpu.VMEM(shape, pencil.dtype),
            pltpu.VMEM(shape, pencil.dtype),
            pltpu.VMEM(shape, pencil.dtype),
            pltpu.SemaphoreType.DMA((parts,)),
            pltpu.SemaphoreType.DMA((parts,)),
            pltpu.SemaphoreType.DMA((parts,)),
            pltpu.SemaphoreType.DMA((parts,)),
        ],
        compiler_params=pltpu.CompilerParams(collective_id=2, has_side_effects=True),
    )(field, table, xcos_t, xsin_t, swap_t, weight, count)


def slab_exchange(blocks, parts, exchange_id):
    return pl.pallas_call(
        functools.partial(slab_exchange_kernel, parts),
        out_shape=jax.ShapeDtypeStruct(blocks.shape, blocks.dtype),
        in_specs=[pl.BlockSpec(memory_space=pltpu.VMEM)],
        out_specs=pl.BlockSpec(memory_space=pltpu.VMEM),
        scratch_shapes=[
            pltpu.VMEM(blocks.shape, blocks.dtype),
            pltpu.SemaphoreType.DMA((parts,)),
            pltpu.SemaphoreType.DMA((parts,)),
        ],
        compiler_params=pltpu.CompilerParams(collective_id=exchange_id, has_side_effects=True),
    )(blocks)


def local(
    base_field,
    forcing,
    load,
    amplitudes,
    amp_index,
    mode_count,
    point_weight,
    point_bias,
    spectral_weight,
):
    channels, slab_rows, plane_count, length_y = base_field.shape
    slab_count = lax.axis_size("slab")
    local_modes = spectral_weight.shape[0]
    modes_y = local_modes * slab_count
    modes_x = spectral_weight.shape[1]
    length_x = slab_rows * slab_count
    packed_width = 2 * channels * plane_count
    slab_index = lax.axis_index("slab")
    level_ids = jnp.arange(amplitudes.shape[0], dtype=jnp.int32)
    amplitude = jnp.sum(jnp.where(level_ids == amp_index[0], amplitudes, 0.0))
    cells = slab_rows * plane_count
    driven = base_field.reshape(channels, cells * length_y).astype(jnp.float32) + amplitude * load[
        :, None
    ] * forcing.reshape(1, cells * length_y).astype(jnp.float32)
    field_rows = (2.0 * jnp.tanh(0.5 * driven)).astype(jnp.bfloat16)
    field_now = field_rows.reshape(channels, slab_rows, plane_count, length_y)
    y_cos, y_sin = phase_tables(np.arange(modes_y), np.arange(length_y), length_y)
    forward_table = bf16_constant(np.stack([y_cos, -y_sin]))
    frequency_x = np.concatenate(
        [np.arange(modes_x // 2), np.arange(length_x - modes_x // 2, length_x)]
    )
    full_cos, full_sin = phase_tables(frequency_x, np.arange(length_x), length_x)
    lane = np.arange(packed_width)
    real_lane = (lane // channels) % 2 == 0
    swap = np.where(
        real_lane[None, :],
        (lane[:, None] == lane[None, :] + channels).astype(np.float32),
        -(lane[:, None] == lane[None, :] - channels).astype(np.float32),
    )
    weight = spectral_weight[0].transpose(1, 2, 3, 0)
    returned = mode_mix_exchange(
        field_rows, forward_table, bf16_constant(full_cos.T), bf16_constant(full_sin.T), bf16_constant(swap.T), weight,
        mode_count, slab_count,
    )
    weights_y = np.where(np.arange(modes_y) == 0, 1.0, 2.0).astype(np.float32) / np.float32(
        length_x * length_y
    )
    table = bf16_constant(
        np.concatenate([weights_y[:, None] * y_cos, -(weights_y[:, None] * y_sin)], axis=0)
    )
    bias = point_bias.reshape(channels, 1)
    members = lax.axis_size("member")
    total = layer_sum(returned, table, point_weight, field_rows, bias, members)
    return total.reshape(channels // members, slab_rows, plane_count, length_y)


def solution(mesh):
    in_specs = (
        P(None, "slab", None, None),
        P("slab", None, None),
        P(),
        P(),
        P("member"),
        P("member"),
        P(),
        P(),
        P("slab", None, None, None, None),
    )
    out_specs = P("member", "slab", None, None)
    return jax.shard_map(local, mesh=mesh, in_specs=in_specs, out_specs=out_specs, check_vma=False)
```

```python
import functools
import math

import jax
import ml_dtypes
import numpy as np
import jax.numpy as jnp
from jax import lax
from jax.experimental import pallas as pl
from jax.experimental.pallas import tpu as pltpu
from jax.sharding import PartitionSpec as P

TWO_PI = 2.0 * math.pi


def phase_tables(frequency, positions, length):
    product = np.outer(frequency, positions) % length
    angles = (product.astype(np.float32) * np.float32(TWO_PI / length)).astype(np.float64)
    return np.cos(angles).astype(np.float32), np.sin(angles).astype(np.float32)


def bf16_constant(values):
    return jnp.asarray(np.asarray(values, np.float32).astype(ml_dtypes.bfloat16))


def phases(frequency, positions, length):
    product = frequency[:, None] * positions[None, :] % length
    angles = product.astype(jnp.float32) * (TWO_PI / length)
    return (jnp.cos(angles), jnp.sin(angles))


def forward_x(pencil, cos_table, sin_table):
    row_total = pencil.shape[0]
    modes = cos_table.shape[0]
    with_cos = jnp.einsum(
        "kxf,mx->kmf", pencil, cos_table, preferred_element_type=jnp.float32
    ).reshape(row_total, modes, 2, -1)
    with_sin = jnp.einsum(
        "kxf,mx->kmf", pencil, sin_table, preferred_element_type=jnp.float32
    ).reshape(row_total, modes, 2, -1)
    real_part = with_cos[:, :, 0] + with_sin[:, :, 1]
    imag_part = with_cos[:, :, 1] - with_sin[:, :, 0]
    return jnp.stack([real_part, imag_part], axis=2).reshape(row_total, modes, -1)


def inverse_x(spectra, cos_table, sin_table):
    row_total = spectra.shape[0]
    points = cos_table.shape[1]
    with_cos = jnp.einsum(
        "kmf,mx->kxf", spectra, cos_table, preferred_element_type=jnp.float32
    ).reshape(row_total, points, 2, -1)
    with_sin = jnp.einsum(
        "kmf,mx->kxf", spectra, sin_table, preferred_element_type=jnp.float32
    ).reshape(row_total, points, 2, -1)
    real_part = with_cos[:, :, 0] - with_sin[:, :, 1]
    imag_part = with_cos[:, :, 1] + with_sin[:, :, 0]
    return jnp.stack([real_part, imag_part], axis=2).reshape(row_total, points, -1)


def mixing(weights, values):
    return jnp.einsum("kmoi,kmiz->kmoz", weights, values, preferred_element_type=jnp.float32)


def greet_members(members):
    me = lax.axis_index("member")
    slab = lax.axis_index("slab")
    chips = members // 2
    chip, core = me // 2, me % 2
    mesh_kind = pl.DeviceIdType.MESH
    barrier = pltpu.get_barrier_semaphore()
    pl.semaphore_signal(barrier, inc=1, device_id=(chip * 2 + 1 - core, slab), device_id_type=mesh_kind)
    for step in range(1, chips):
        peer = lax.rem(chip + step, chips) * 2 + core
        pl.semaphore_signal(barrier, inc=1, device_id=(peer, slab), device_id_type=mesh_kind)
    return barrier


def layer_values(members, back_ref, table_ref, weight_ref, field_ref, bias_ref, value, layer):
    modes, slab_rows, width = back_ref.shape
    channels = weight_ref.shape[0]
    planes = width // (2 * channels)
    length = table_ref.shape[1]
    block_rows = layer.shape[2]
    table_real = table_ref[:modes, :]
    table_imag = table_ref[modes:, :]
    padding = jnp.zeros((width - modes, width), jnp.float32)
    for row in range(slab_rows):
        pencil = back_ref[:, row, :].astype(jnp.float32)
        pencil_t = jnp.concatenate([pencil, padding], axis=0).T[:, :modes].astype(back_ref.dtype)
        for plane in range(planes):
            cell = row * planes + plane
            base = plane * 2 * channels
            lanes = pl.ds(cell * length, length)
            spectral = jnp.dot(
                pencil_t[base:base + channels], table_real, preferred_element_type=jnp.float32
            )
            spectral = spectral + jnp.dot(
                pencil_t[base + channels:base + 2 * channels], table_imag,
                preferred_element_type=jnp.float32,
            )
            pointwise = jnp.dot(weight_ref[...], field_ref[:, lanes], preferred_element_type=jnp.float32)
            value[:, lanes] = jax.nn.gelu(pointwise + bias_ref[...] + spectral, approximate=True)
    for block in range(members):
        rows = pl.ds(block * block_rows, block_rows)
        layer[block % 2, block // 2] = value[rows, :].astype(layer.dtype)


def member_total(members, out_ref, layer, near, part, far, near_sems, far_send, far_recv):
    me = lax.axis_index("member")
    slab = lax.axis_index("slab")
    chips = members // 2
    chip, core = me // 2, me % 2
    sibling = chip * 2 + 1 - core
    mesh_kind = pl.DeviceIdType.MESH
    on_chip = pltpu.make_async_remote_copy(
        src_ref=layer.at[1 - core],
        dst_ref=near,
        send_sem=near_sems.at[0],
        recv_sem=near_sems.at[1],
        device_id=(sibling, slab),
        device_id_type=mesh_kind,
    )
    on_chip.start()
    on_chip.wait_recv()
    for index in range(chips):
        pair = layer[core, index].astype(jnp.float32) + near[index].astype(jnp.float32)
        part[index] = pair.astype(part.dtype)
    on_chip.wait_send()

    def copy_of(source, target, peer_chip):
        return pltpu.make_async_remote_copy(
            src_ref=part.at[source],
            dst_ref=far.at[target],
            send_sem=far_send.at[source],
            recv_sem=far_recv.at[target],
            device_id=(peer_chip * 2 + core, slab),
            device_id_type=mesh_kind,
        )

    for step in range(1, chips):
        peer = lax.rem(chip + step, chips)
        copy_of(peer, chip, peer).start()
    total = part[chip].astype(jnp.float32)
    for step in range(1, chips):
        source = lax.rem(chip + chips - step, chips)
        copy_of(source, source, source).wait_recv()
        total = total + far[source].astype(jnp.float32)
    for step in range(1, chips):
        peer = lax.rem(chip + step, chips)
        copy_of(peer, chip, peer).wait_send()
    out_ref[...] = (total / members).astype(out_ref.dtype)


def layer_sum_kernel(members, back_ref, table_ref, weight_ref, field_ref, bias_ref, out_ref, value, layer,
                     near, part, far, near_sems, far_send, far_recv):
    barrier = greet_members(members)
    layer_values(members, back_ref, table_ref, weight_ref, field_ref, bias_ref, value, layer)
    pl.semaphore_wait(barrier, members // 2)
    member_total(members, out_ref, layer, near, part, far, near_sems, far_send, far_recv)


def layer_sum(back, table, weight, field, bias, members):
    channels, width = field.shape
    block_rows = channels // members
    chips = members // 2
    return pl.pallas_call(
        functools.partial(layer_sum_kernel, members),
        out_shape=jax.ShapeDtypeStruct((block_rows, width), jnp.bfloat16),
        in_specs=[pl.BlockSpec(memory_space=pltpu.VMEM)] * 5,
        out_specs=pl.BlockSpec(memory_space=pltpu.VMEM),
        scratch_shapes=[
            pltpu.VMEM((channels, width), jnp.float32),
            pltpu.VMEM((2, chips, block_rows, width), jnp.bfloat16),
            pltpu.VMEM((chips, block_rows, width), jnp.bfloat16),
            pltpu.VMEM((chips, block_rows, width), jnp.bfloat16),
            pltpu.VMEM((chips, block_rows, width), jnp.bfloat16),
            pltpu.SemaphoreType.DMA((2,)),
            pltpu.SemaphoreType.DMA((chips,)),
            pltpu.SemaphoreType.DMA((chips,)),
        ],
        compiler_params=pltpu.CompilerParams(collective_id=0, has_side_effects=True),
    )(back, table, weight, field, bias)


def greet_slab(parts):
    me = lax.axis_index("slab")
    member = lax.axis_index("member")
    barrier = pltpu.get_barrier_semaphore()
    for step in range(1, parts):
        peer = lax.rem(me + step, parts)
        pl.semaphore_signal(barrier, inc=1, device_id=(member, peer), device_id_type=pl.DeviceIdType.MESH)
    return barrier


def swap_blocks(parts, source_ref, out_ref, landed, send_sems, recv_sems):
    me = lax.axis_index("slab")
    member = lax.axis_index("member")

    def copy_of(source, target, peer):
        return pltpu.make_async_remote_copy(
            src_ref=source_ref.at[source],
            dst_ref=landed.at[target],
            send_sem=send_sems.at[source],
            recv_sem=recv_sems.at[target],
            device_id=(member, peer),
            device_id_type=pl.DeviceIdType.MESH,
        )

    for step in range(1, parts):
        peer = lax.rem(me + step, parts)
        copy_of(peer, me, peer).start()
    landed[me] = source_ref[me]
    for step in range(1, parts):
        source = lax.rem(me + parts - step, parts)
        copy_of(source, source, source).wait_recv()
    for step in range(1, parts):
        peer = lax.rem(me + step, parts)
        copy_of(peer, me, peer).wait_send()
    if out_ref is not None:
        out_ref[...] = landed[...]


def slab_exchange_kernel(parts, blocks_ref, out_ref, landed, send_sems, recv_sems):
    barrier = greet_slab(parts)
    pl.semaphore_wait(barrier, parts - 1)
    swap_blocks(parts, blocks_ref, out_ref, landed, send_sems, recv_sems)


def mode_mix_kernel(parts, members, field_ref, table_ref, xcos_t_ref, xsin_t_ref, swap_t_ref, weight_ref,
                    count_ref, back_table_ref, point_weight_ref, bias_ref, out_ref, mixed_t, modes_out, first,
                    blocks, landed, first_send, first_recv, send_sems, recv_sems, value, layer, near, part,
                    far, near_sems, far_send, far_recv):
    barrier = greet_slab(parts)
    greet_members(members)
    modes, slab_rows, width = modes_out.shape
    channels = field_ref.shape[0]
    planes = width // (2 * channels)
    length = table_ref.shape[2]
    lane = lax.broadcasted_iota(jnp.int32, (modes, width), 1)
    real_lanes = (lane // channels) % 2 == 0
    contract_last = (((1,), (1,)), ((), ()))
    for row in range(slab_rows):
        pieces = []
        for plane in range(planes):
            cell = row * planes + plane
            values = field_ref[:, pl.ds(cell * length, length)]
            pieces += [values, values]
        stack = jnp.concatenate(pieces, axis=0)
        real = lax.dot_general(table_ref[0], stack, contract_last, preferred_element_type=jnp.float32)
        imag = lax.dot_general(table_ref[1], stack, contract_last, preferred_element_type=jnp.float32)
        modes_out[:, row, :] = jnp.where(real_lanes, real, imag).astype(modes_out.dtype)
    pl.semaphore_wait(barrier, parts - 1 + members // 2)
    swap_blocks(parts, modes_out, None, first, first_send, first_recv)
    pencil = first[...].astype(jnp.float32)
    pencil = pencil.reshape(pencil.shape[0] * pencil.shape[1], pencil.shape[2])
    pencil_t = pencil.T.astype(modes_out.dtype)
    swap_t = swap_t_ref[...]
    swapped_t = jnp.dot(swap_t, pencil_t, preferred_element_type=jnp.float32).astype(pencil_t.dtype)
    spec_t = jnp.dot(pencil_t, xcos_t_ref[...], preferred_element_type=jnp.float32)
    spec_t = spec_t + jnp.dot(swapped_t, xsin_t_ref[...], preferred_element_type=jnp.float32)
    spec_t = spec_t.astype(pencil_t.dtype).astype(jnp.float32)
    outputs = weight_ref.shape[1]
    planes = spec_t.shape[0] // (2 * outputs)
    for plane in range(planes):
        base = plane * 2 * outputs
        real = spec_t[base:base + outputs, :]
        imag = spec_t[base + outputs:base + 2 * outputs, :]
        for out in range(outputs):
            weight_real = weight_ref[0, out].astype(jnp.float32)
            weight_imag = weight_ref[1, out].astype(jnp.float32)
            mixed_t[pl.ds(base + out, 1), :] = jnp.sum(
                weight_real * real - weight_imag * imag, axis=0, keepdims=True
            )
            mixed_t[pl.ds(base + outputs + out, 1), :] = jnp.sum(
                weight_imag * real + weight_real * imag, axis=0, keepdims=True
            )
    kept = (lax.axis_index("slab") < count_ref[0]).astype(jnp.float32)
    mixed = (mixed_t[...] * kept).astype(pencil_t.dtype)
    mixed_swapped = jnp.dot(swap_t, mixed, preferred_element_type=jnp.float32).astype(pencil_t.dtype)
    contract = (((1,), (1,)), ((), ()))
    back = lax.dot_general(xcos_t_ref[...], mixed, contract, preferred_element_type=jnp.float32)
    back = back - lax.dot_general(
        xsin_t_ref[...], mixed_swapped, contract, preferred_element_type=jnp.float32
    )
    blocks[...] = back.reshape(blocks.shape).astype(blocks.dtype)
    swap_blocks(parts, blocks, None, landed, send_sems, recv_sems)
    layer_values(members, landed, back_table_ref, point_weight_ref, field_ref, bias_ref, value, layer)
    member_total(members, out_ref, layer, near, part, far, near_sems, far_send, far_recv)


def mode_mix_exchange(field, table, xcos_t, xsin_t, swap_t, weight, count, back_table, point_weight, bias,
                      parts, members):
    channels, cells_width = field.shape
    modes, length = table.shape[1], table.shape[2]
    width = swap_t.shape[0]
    planes = width // (2 * channels)
    shape = (modes, cells_width // (planes * length), width)
    block_rows = channels // members
    chips = members // 2
    return pl.pallas_call(
        functools.partial(mode_mix_kernel, parts, members),
        out_shape=jax.ShapeDtypeStruct((block_rows, cells_width), jnp.bfloat16),
        in_specs=[pl.BlockSpec(memory_space=pltpu.VMEM)] * 6
        + [pl.BlockSpec(memory_space=pltpu.SMEM)]
        + [pl.BlockSpec(memory_space=pltpu.VMEM)] * 3,
        out_specs=pl.BlockSpec(memory_space=pltpu.VMEM),
        scratch_shapes=[
            pltpu.VMEM((width, modes), jnp.float32),
            pltpu.VMEM(shape, field.dtype),
            pltpu.VMEM(shape, field.dtype),
            pltpu.VMEM(shape, field.dtype),
            pltpu.VMEM(shape, field.dtype),
            pltpu.SemaphoreType.DMA((parts,)),
            pltpu.SemaphoreType.DMA((parts,)),
            pltpu.SemaphoreType.DMA((parts,)),
            pltpu.SemaphoreType.DMA((parts,)),
            pltpu.VMEM((channels, cells_width), jnp.float32),
            pltpu.VMEM((2, chips, block_rows, cells_width), jnp.bfloat16),
            pltpu.VMEM((chips, block_rows, cells_width), jnp.bfloat16),
            pltpu.VMEM((chips, block_rows, cells_width), jnp.bfloat16),
            pltpu.VMEM((chips, block_rows, cells_width), jnp.bfloat16),
            pltpu.SemaphoreType.DMA((2,)),
            pltpu.SemaphoreType.DMA((chips,)),
            pltpu.SemaphoreType.DMA((chips,)),
        ],
        compiler_params=pltpu.CompilerParams(collective_id=2, has_side_effects=True),
    )(field, table, xcos_t, xsin_t, swap_t, weight, count, back_table, point_weight, bias)


def slab_exchange(blocks, parts, exchange_id):
    return pl.pallas_call(
        functools.partial(slab_exchange_kernel, parts),
        out_shape=jax.ShapeDtypeStruct(blocks.shape, blocks.dtype),
        in_specs=[pl.BlockSpec(memory_space=pltpu.VMEM)],
        out_specs=pl.BlockSpec(memory_space=pltpu.VMEM),
        scratch_shapes=[
            pltpu.VMEM(blocks.shape, blocks.dtype),
            pltpu.SemaphoreType.DMA((parts,)),
            pltpu.SemaphoreType.DMA((parts,)),
        ],
        compiler_params=pltpu.CompilerParams(collective_id=exchange_id, has_side_effects=True),
    )(blocks)


def local(
    base_field,
    forcing,
    load,
    amplitudes,
    amp_index,
    mode_count,
    point_weight,
    point_bias,
    spectral_weight,
):
    channels, slab_rows, plane_count, length_y = base_field.shape
    slab_count = lax.axis_size("slab")
    local_modes = spectral_weight.shape[0]
    modes_y = local_modes * slab_count
    modes_x = spectral_weight.shape[1]
    length_x = slab_rows * slab_count
    packed_width = 2 * channels * plane_count
    slab_index = lax.axis_index("slab")
    level_ids = jnp.arange(amplitudes.shape[0], dtype=jnp.int32)
    amplitude = jnp.sum(jnp.where(level_ids == amp_index[0], amplitudes, 0.0))
    cells = slab_rows * plane_count
    driven = base_field.reshape(channels, cells * length_y).astype(jnp.float32) + amplitude * load[
        :, None
    ] * forcing.reshape(1, cells * length_y).astype(jnp.float32)
    field_rows = (2.0 * jnp.tanh(0.5 * driven)).astype(jnp.bfloat16)
    field_now = field_rows.reshape(channels, slab_rows, plane_count, length_y)
    y_cos, y_sin = phase_tables(np.arange(modes_y), np.arange(length_y), length_y)
    forward_table = bf16_constant(np.stack([y_cos, -y_sin]))
    frequency_x = np.concatenate(
        [np.arange(modes_x // 2), np.arange(length_x - modes_x // 2, length_x)]
    )
    full_cos, full_sin = phase_tables(frequency_x, np.arange(length_x), length_x)
    lane = np.arange(packed_width)
    real_lane = (lane // channels) % 2 == 0
    swap = np.where(
        real_lane[None, :],
        (lane[:, None] == lane[None, :] + channels).astype(np.float32),
        -(lane[:, None] == lane[None, :] - channels).astype(np.float32),
    )
    weight = spectral_weight[0].transpose(1, 2, 3, 0)
    weights_y = np.where(np.arange(modes_y) == 0, 1.0, 2.0).astype(np.float32) / np.float32(
        length_x * length_y
    )
    table = bf16_constant(
        np.concatenate([weights_y[:, None] * y_cos, -(weights_y[:, None] * y_sin)], axis=0)
    )
    bias = point_bias.reshape(channels, 1)
    members = lax.axis_size("member")
    total = mode_mix_exchange(
        field_rows, forward_table, bf16_constant(full_cos.T), bf16_constant(full_sin.T),
        bf16_constant(swap.T), weight, mode_count, table, point_weight, bias, slab_count, members,
    )
    return total.reshape(channels // members, slab_rows, plane_count, length_y)


def solution(mesh):
    in_specs = (
        P(None, "slab", None, None),
        P("slab", None, None),
        P(),
        P(),
        P("member"),
        P("member"),
        P(),
        P(),
        P("slab", None, None, None, None),
    )
    out_specs = P("member", "slab", None, None)
    return jax.shard_map(local, mesh=mesh, in_specs=in_specs, out_specs=out_specs, check_vma=False)
```

```python
import functools
import math

import jax
import ml_dtypes
import numpy as np
import jax.numpy as jnp
from jax import lax
from jax.experimental import pallas as pl
from jax.experimental.pallas import tpu as pltpu
from jax.sharding import PartitionSpec as P

TWO_PI = 2.0 * math.pi


def phase_tables(frequency, positions, length):
    product = np.outer(frequency, positions) % length
    angles = (product.astype(np.float32) * np.float32(TWO_PI / length)).astype(np.float64)
    return np.cos(angles).astype(np.float32), np.sin(angles).astype(np.float32)


def bf16_constant(values):
    return jnp.asarray(np.asarray(values, np.float32).astype(ml_dtypes.bfloat16))


def phases(frequency, positions, length):
    product = frequency[:, None] * positions[None, :] % length
    angles = product.astype(jnp.float32) * (TWO_PI / length)
    return (jnp.cos(angles), jnp.sin(angles))


def forward_x(pencil, cos_table, sin_table):
    row_total = pencil.shape[0]
    modes = cos_table.shape[0]
    with_cos = jnp.einsum(
        "kxf,mx->kmf", pencil, cos_table, preferred_element_type=jnp.float32
    ).reshape(row_total, modes, 2, -1)
    with_sin = jnp.einsum(
        "kxf,mx->kmf", pencil, sin_table, preferred_element_type=jnp.float32
    ).reshape(row_total, modes, 2, -1)
    real_part = with_cos[:, :, 0] + with_sin[:, :, 1]
    imag_part = with_cos[:, :, 1] - with_sin[:, :, 0]
    return jnp.stack([real_part, imag_part], axis=2).reshape(row_total, modes, -1)


def inverse_x(spectra, cos_table, sin_table):
    row_total = spectra.shape[0]
    points = cos_table.shape[1]
    with_cos = jnp.einsum(
        "kmf,mx->kxf", spectra, cos_table, preferred_element_type=jnp.float32
    ).reshape(row_total, points, 2, -1)
    with_sin = jnp.einsum(
        "kmf,mx->kxf", spectra, sin_table, preferred_element_type=jnp.float32
    ).reshape(row_total, points, 2, -1)
    real_part = with_cos[:, :, 0] - with_sin[:, :, 1]
    imag_part = with_cos[:, :, 1] + with_sin[:, :, 0]
    return jnp.stack([real_part, imag_part], axis=2).reshape(row_total, points, -1)


def mixing(weights, values):
    return jnp.einsum("kmoi,kmiz->kmoz", weights, values, preferred_element_type=jnp.float32)


def greet_members(members):
    me = lax.axis_index("member")
    slab = lax.axis_index("slab")
    chips = members // 2
    chip, core = me // 2, me % 2
    mesh_kind = pl.DeviceIdType.MESH
    barrier = pltpu.get_barrier_semaphore()
    pl.semaphore_signal(barrier, inc=1, device_id=(chip * 2 + 1 - core, slab), device_id_type=mesh_kind)
    for step in range(1, chips):
        peer = lax.rem(chip + step, chips) * 2 + core
        pl.semaphore_signal(barrier, inc=1, device_id=(peer, slab), device_id_type=mesh_kind)
    return barrier


def layer_values(members, back_ref, table_ref, weight_ref, field_ref, bias, value, layer):
    modes, slab_rows, width = back_ref.shape
    channels = weight_ref.shape[0]
    planes = width // (2 * channels)
    length = table_ref.shape[1]
    block_rows = layer.shape[2]
    table_real = table_ref[:modes, :]
    table_imag = table_ref[modes:, :]
    padding = jnp.zeros((width - modes, width), jnp.float32)
    for row in range(slab_rows):
        pencil = back_ref[:, row, :].astype(jnp.float32)
        pencil_t = jnp.concatenate([pencil, padding], axis=0).T[:, :modes].astype(back_ref.dtype)
        for plane in range(planes):
            cell = row * planes + plane
            base = plane * 2 * channels
            lanes = pl.ds(cell * length, length)
            spectral = jnp.dot(
                pencil_t[base:base + channels], table_real, preferred_element_type=jnp.float32
            )
            spectral = spectral + jnp.dot(
                pencil_t[base + channels:base + 2 * channels], table_imag,
                preferred_element_type=jnp.float32,
            )
            pointwise = jnp.dot(weight_ref[...], field_ref[:, lanes], preferred_element_type=jnp.float32)
            value[:, lanes] = jax.nn.gelu(pointwise + bias + spectral, approximate=True)
    for block in range(members):
        rows = pl.ds(block * block_rows, block_rows)
        layer[block % 2, block // 2] = value[rows, :].astype(layer.dtype)


def member_total(members, out_ref, layer, near, part, far, near_sems, far_send, far_recv):
    me = lax.axis_index("member")
    slab = lax.axis_index("slab")
    chips = members // 2
    chip, core = me // 2, me % 2
    sibling = chip * 2 + 1 - core
    mesh_kind = pl.DeviceIdType.MESH
    on_chip = pltpu.make_async_remote_copy(
        src_ref=layer.at[1 - core],
        dst_ref=near,
        send_sem=near_sems.at[0],
        recv_sem=near_sems.at[1],
        device_id=(sibling, slab),
        device_id_type=mesh_kind,
    )
    on_chip.start()
    on_chip.wait_recv()
    for index in range(chips):
        pair = layer[core, index].astype(jnp.float32) + near[index].astype(jnp.float32)
        part[index] = pair.astype(part.dtype)
    on_chip.wait_send()

    def copy_of(source, target, peer_chip):
        return pltpu.make_async_remote_copy(
            src_ref=part.at[source],
            dst_ref=far.at[target],
            send_sem=far_send.at[source],
            recv_sem=far_recv.at[target],
            device_id=(peer_chip * 2 + core, slab),
            device_id_type=mesh_kind,
        )

    for step in range(1, chips):
        peer = lax.rem(chip + step, chips)
        copy_of(peer, chip, peer).start()
    total = part[chip].astype(jnp.float32)
    for step in range(1, chips):
        source = lax.rem(chip + chips - step, chips)
        copy_of(source, source, source).wait_recv()
        total = total + far[source].astype(jnp.float32)
    for step in range(1, chips):
        peer = lax.rem(chip + step, chips)
        copy_of(peer, chip, peer).wait_send()
    out_ref[...] = (total / members).astype(out_ref.dtype)


def layer_sum_kernel(members, back_ref, table_ref, weight_ref, field_ref, bias_ref, out_ref, value, layer,
                     near, part, far, near_sems, far_send, far_recv):
    barrier = greet_members(members)
    layer_values(members, back_ref, table_ref, weight_ref, field_ref, bias_ref[...], value, layer)
    pl.semaphore_wait(barrier, members // 2)
    member_total(members, out_ref, layer, near, part, far, near_sems, far_send, far_recv)


def layer_sum(back, table, weight, field, bias, members):
    channels, width = field.shape
    block_rows = channels // members
    chips = members // 2
    return pl.pallas_call(
        functools.partial(layer_sum_kernel, members),
        out_shape=jax.ShapeDtypeStruct((block_rows, width), jnp.bfloat16),
        in_specs=[pl.BlockSpec(memory_space=pltpu.VMEM)] * 5,
        out_specs=pl.BlockSpec(memory_space=pltpu.VMEM),
        scratch_shapes=[
            pltpu.VMEM((channels, width), jnp.float32),
            pltpu.VMEM((2, chips, block_rows, width), jnp.bfloat16),
            pltpu.VMEM((chips, block_rows, width), jnp.bfloat16),
            pltpu.VMEM((chips, block_rows, width), jnp.bfloat16),
            pltpu.VMEM((chips, block_rows, width), jnp.bfloat16),
            pltpu.SemaphoreType.DMA((2,)),
            pltpu.SemaphoreType.DMA((chips,)),
            pltpu.SemaphoreType.DMA((chips,)),
        ],
        compiler_params=pltpu.CompilerParams(collective_id=0, has_side_effects=True),
    )(back, table, weight, field, bias)


def greet_slab(parts):
    me = lax.axis_index("slab")
    member = lax.axis_index("member")
    barrier = pltpu.get_barrier_semaphore()
    for step in range(1, parts):
        peer = lax.rem(me + step, parts)
        pl.semaphore_signal(barrier, inc=1, device_id=(member, peer), device_id_type=pl.DeviceIdType.MESH)
    return barrier


def swap_blocks(parts, source_ref, out_ref, landed, send_sems, recv_sems):
    me = lax.axis_index("slab")
    member = lax.axis_index("member")

    def copy_of(source, target, peer):
        return pltpu.make_async_remote_copy(
            src_ref=source_ref.at[source],
            dst_ref=landed.at[target],
            send_sem=send_sems.at[source],
            recv_sem=recv_sems.at[target],
            device_id=(member, peer),
            device_id_type=pl.DeviceIdType.MESH,
        )

    for step in range(1, parts):
        peer = lax.rem(me + step, parts)
        copy_of(peer, me, peer).start()
    landed[me] = source_ref[me]
    for step in range(1, parts):
        source = lax.rem(me + parts - step, parts)
        copy_of(source, source, source).wait_recv()
    for step in range(1, parts):
        peer = lax.rem(me + step, parts)
        copy_of(peer, me, peer).wait_send()
    if out_ref is not None:
        out_ref[...] = landed[...]


def slab_exchange_kernel(parts, blocks_ref, out_ref, landed, send_sems, recv_sems):
    barrier = greet_slab(parts)
    pl.semaphore_wait(barrier, parts - 1)
    swap_blocks(parts, blocks_ref, out_ref, landed, send_sems, recv_sems)


def smem_column(ref, count):
    rows = lax.broadcasted_iota(jnp.int32, (count, 1), 0)
    column = jnp.zeros((count, 1), jnp.float32)
    for index in range(count):
        column = jnp.where(rows == index, ref[index], column)
    return column


def mode_mix_kernel(parts, members, base_ref, forcing_ref, table_ref, xcos_t_ref, xsin_t_ref, swap_t_ref,
                    weight_ref, count_ref, back_table_ref, point_weight_ref, load_ref, amplitude_ref,
                    level_ref, bias_ref, out_ref, field_ref, mixed_t, modes_out, first, blocks, landed,
                    first_send, first_recv, send_sems, recv_sems, value, layer, near, part, far, near_sems,
                    far_send, far_recv):
    barrier = greet_slab(parts)
    greet_members(members)
    channels, cells_width = field_ref.shape
    scale = smem_column(load_ref, channels) * amplitude_ref[level_ref[0]]
    bias = smem_column(bias_ref, channels)
    chunk = table_ref.shape[2]
    for start in range(0, cells_width, chunk):
        lanes = pl.ds(start, chunk)
        driven = base_ref[:, lanes].astype(jnp.float32) + scale * forcing_ref[:, lanes].astype(jnp.float32)
        field_ref[:, lanes] = (2.0 * jnp.tanh(0.5 * driven)).astype(field_ref.dtype)
    modes, slab_rows, width = modes_out.shape
    channels = field_ref.shape[0]
    planes = width // (2 * channels)
    length = table_ref.shape[2]
    lane = lax.broadcasted_iota(jnp.int32, (modes, width), 1)
    real_lanes = (lane // channels) % 2 == 0
    contract_last = (((1,), (1,)), ((), ()))
    for row in range(slab_rows):
        pieces = []
        for plane in range(planes):
            cell = row * planes + plane
            values = field_ref[:, pl.ds(cell * length, length)]
            pieces += [values, values]
        stack = jnp.concatenate(pieces, axis=0)
        real = lax.dot_general(table_ref[0], stack, contract_last, preferred_element_type=jnp.float32)
        imag = lax.dot_general(table_ref[1], stack, contract_last, preferred_element_type=jnp.float32)
        modes_out[:, row, :] = jnp.where(real_lanes, real, imag).astype(modes_out.dtype)
    pl.semaphore_wait(barrier, parts - 1 + members // 2)
    swap_blocks(parts, modes_out, None, first, first_send, first_recv)
    pencil = first[...].astype(jnp.float32)
    pencil = pencil.reshape(pencil.shape[0] * pencil.shape[1], pencil.shape[2])
    pencil_t = pencil.T.astype(modes_out.dtype)
    swap_t = swap_t_ref[...]
    swapped_t = jnp.dot(swap_t, pencil_t, preferred_element_type=jnp.float32).astype(pencil_t.dtype)
    spec_t = jnp.dot(pencil_t, xcos_t_ref[...], preferred_element_type=jnp.float32)
    spec_t = spec_t + jnp.dot(swapped_t, xsin_t_ref[...], preferred_element_type=jnp.float32)
    spec_t = spec_t.astype(pencil_t.dtype).astype(jnp.float32)
    outputs = weight_ref.shape[1]
    planes = spec_t.shape[0] // (2 * outputs)
    for plane in range(planes):
        base = plane * 2 * outputs
        real = spec_t[base:base + outputs, :]
        imag = spec_t[base + outputs:base + 2 * outputs, :]
        for out in range(outputs):
            weight_real = weight_ref[0, out].astype(jnp.float32)
            weight_imag = weight_ref[1, out].astype(jnp.float32)
            mixed_t[pl.ds(base + out, 1), :] = jnp.sum(
                weight_real * real - weight_imag * imag, axis=0, keepdims=True
            )
            mixed_t[pl.ds(base + outputs + out, 1), :] = jnp.sum(
                weight_imag * real + weight_real * imag, axis=0, keepdims=True
            )
    kept = (lax.axis_index("slab") < count_ref[0]).astype(jnp.float32)
    mixed = (mixed_t[...] * kept).astype(pencil_t.dtype)
    mixed_swapped = jnp.dot(swap_t, mixed, preferred_element_type=jnp.float32).astype(pencil_t.dtype)
    contract = (((1,), (1,)), ((), ()))
    back = lax.dot_general(xcos_t_ref[...], mixed, contract, preferred_element_type=jnp.float32)
    back = back - lax.dot_general(
        xsin_t_ref[...], mixed_swapped, contract, preferred_element_type=jnp.float32
    )
    blocks[...] = back.reshape(blocks.shape).astype(blocks.dtype)
    swap_blocks(parts, blocks, None, landed, send_sems, recv_sems)
    layer_values(members, landed, back_table_ref, point_weight_ref, field_ref, bias, value, layer)
    member_total(members, out_ref, layer, near, part, far, near_sems, far_send, far_recv)


def mode_mix_exchange(base, forcing, table, xcos_t, xsin_t, swap_t, weight, count, back_table, point_weight,
                      load, amplitudes, level, bias, parts, members):
    field = base
    channels, cells_width = field.shape
    modes, length = table.shape[1], table.shape[2]
    width = swap_t.shape[0]
    planes = width // (2 * channels)
    shape = (modes, cells_width // (planes * length), width)
    block_rows = channels // members
    chips = members // 2
    return pl.pallas_call(
        functools.partial(mode_mix_kernel, parts, members),
        out_shape=jax.ShapeDtypeStruct((block_rows, cells_width), jnp.bfloat16),
        in_specs=[pl.BlockSpec(memory_space=pltpu.VMEM)] * 7
        + [pl.BlockSpec(memory_space=pltpu.SMEM)]
        + [pl.BlockSpec(memory_space=pltpu.VMEM)] * 2
        + [pl.BlockSpec(memory_space=pltpu.SMEM)] * 4,
        out_specs=pl.BlockSpec(memory_space=pltpu.VMEM),
        scratch_shapes=[
            pltpu.VMEM((channels, cells_width), jnp.bfloat16),
            pltpu.VMEM((width, modes), jnp.float32),
            pltpu.VMEM(shape, field.dtype),
            pltpu.VMEM(shape, field.dtype),
            pltpu.VMEM(shape, field.dtype),
            pltpu.VMEM(shape, field.dtype),
            pltpu.SemaphoreType.DMA((parts,)),
            pltpu.SemaphoreType.DMA((parts,)),
            pltpu.SemaphoreType.DMA((parts,)),
            pltpu.SemaphoreType.DMA((parts,)),
            pltpu.VMEM((channels, cells_width), jnp.float32),
            pltpu.VMEM((2, chips, block_rows, cells_width), jnp.bfloat16),
            pltpu.VMEM((chips, block_rows, cells_width), jnp.bfloat16),
            pltpu.VMEM((chips, block_rows, cells_width), jnp.bfloat16),
            pltpu.VMEM((chips, block_rows, cells_width), jnp.bfloat16),
            pltpu.SemaphoreType.DMA((2,)),
            pltpu.SemaphoreType.DMA((chips,)),
            pltpu.SemaphoreType.DMA((chips,)),
        ],
        compiler_params=pltpu.CompilerParams(collective_id=2, has_side_effects=True),
    )(base, forcing, table, xcos_t, xsin_t, swap_t, weight, count, back_table, point_weight, load, amplitudes,
      level, bias)


def slab_exchange(blocks, parts, exchange_id):
    return pl.pallas_call(
        functools.partial(slab_exchange_kernel, parts),
        out_shape=jax.ShapeDtypeStruct(blocks.shape, blocks.dtype),
        in_specs=[pl.BlockSpec(memory_space=pltpu.VMEM)],
        out_specs=pl.BlockSpec(memory_space=pltpu.VMEM),
        scratch_shapes=[
            pltpu.VMEM(blocks.shape, blocks.dtype),
            pltpu.SemaphoreType.DMA((parts,)),
            pltpu.SemaphoreType.DMA((parts,)),
        ],
        compiler_params=pltpu.CompilerParams(collective_id=exchange_id, has_side_effects=True),
    )(blocks)


def local(
    base_field,
    forcing,
    load,
    amplitudes,
    amp_index,
    mode_count,
    point_weight,
    point_bias,
    spectral_weight,
):
    channels, slab_rows, plane_count, length_y = base_field.shape
    slab_count = lax.axis_size("slab")
    local_modes = spectral_weight.shape[0]
    modes_y = local_modes * slab_count
    modes_x = spectral_weight.shape[1]
    length_x = slab_rows * slab_count
    packed_width = 2 * channels * plane_count
    slab_index = lax.axis_index("slab")
    cells = slab_rows * plane_count
    base_rows = base_field.reshape(channels, cells * length_y)
    forcing_rows = forcing.reshape(1, cells * length_y)
    y_cos, y_sin = phase_tables(np.arange(modes_y), np.arange(length_y), length_y)
    forward_table = bf16_constant(np.stack([y_cos, -y_sin]))
    frequency_x = np.concatenate(
        [np.arange(modes_x // 2), np.arange(length_x - modes_x // 2, length_x)]
    )
    full_cos, full_sin = phase_tables(frequency_x, np.arange(length_x), length_x)
    lane = np.arange(packed_width)
    real_lane = (lane // channels) % 2 == 0
    swap = np.where(
        real_lane[None, :],
        (lane[:, None] == lane[None, :] + channels).astype(np.float32),
        -(lane[:, None] == lane[None, :] - channels).astype(np.float32),
    )
    weight = spectral_weight[0].transpose(1, 2, 3, 0)
    weights_y = np.where(np.arange(modes_y) == 0, 1.0, 2.0).astype(np.float32) / np.float32(
        length_x * length_y
    )
    table = bf16_constant(
        np.concatenate([weights_y[:, None] * y_cos, -(weights_y[:, None] * y_sin)], axis=0)
    )
    members = lax.axis_size("member")
    total = mode_mix_exchange(
        base_rows, forcing_rows, forward_table, bf16_constant(full_cos.T), bf16_constant(full_sin.T),
        bf16_constant(swap.T), weight, mode_count, table, point_weight, load, amplitudes, amp_index,
        point_bias, slab_count, members,
    )
    return total.reshape(channels // members, slab_rows, plane_count, length_y)


def solution(mesh):
    in_specs = (
        P(None, "slab", None, None),
        P("slab", None, None),
        P(),
        P(),
        P("member"),
        P("member"),
        P(),
        P(),
        P("slab", None, None, None, None),
    )
    out_specs = P("member", "slab", None, None)
    return jax.shard_map(local, mesh=mesh, in_specs=in_specs, out_specs=out_specs, check_vma=False)
```

```python
import functools
import math

import jax
import ml_dtypes
import numpy as np
import jax.numpy as jnp
from jax import lax
from jax.experimental import pallas as pl
from jax.experimental.pallas import tpu as pltpu
from jax.sharding import PartitionSpec as P

TWO_PI = 2.0 * math.pi


def phase_tables(frequency, positions, length):
    product = np.outer(frequency, positions) % length
    angles = (product.astype(np.float32) * np.float32(TWO_PI / length)).astype(np.float64)
    return np.cos(angles).astype(np.float32), np.sin(angles).astype(np.float32)


def bf16_constant(values):
    return jnp.asarray(np.asarray(values, np.float32).astype(ml_dtypes.bfloat16))


def phases(frequency, positions, length):
    product = frequency[:, None] * positions[None, :] % length
    angles = product.astype(jnp.float32) * (TWO_PI / length)
    return (jnp.cos(angles), jnp.sin(angles))


def forward_x(pencil, cos_table, sin_table):
    row_total = pencil.shape[0]
    modes = cos_table.shape[0]
    with_cos = jnp.einsum(
        "kxf,mx->kmf", pencil, cos_table, preferred_element_type=jnp.float32
    ).reshape(row_total, modes, 2, -1)
    with_sin = jnp.einsum(
        "kxf,mx->kmf", pencil, sin_table, preferred_element_type=jnp.float32
    ).reshape(row_total, modes, 2, -1)
    real_part = with_cos[:, :, 0] + with_sin[:, :, 1]
    imag_part = with_cos[:, :, 1] - with_sin[:, :, 0]
    return jnp.stack([real_part, imag_part], axis=2).reshape(row_total, modes, -1)


def inverse_x(spectra, cos_table, sin_table):
    row_total = spectra.shape[0]
    points = cos_table.shape[1]
    with_cos = jnp.einsum(
        "kmf,mx->kxf", spectra, cos_table, preferred_element_type=jnp.float32
    ).reshape(row_total, points, 2, -1)
    with_sin = jnp.einsum(
        "kmf,mx->kxf", spectra, sin_table, preferred_element_type=jnp.float32
    ).reshape(row_total, points, 2, -1)
    real_part = with_cos[:, :, 0] - with_sin[:, :, 1]
    imag_part = with_cos[:, :, 1] + with_sin[:, :, 0]
    return jnp.stack([real_part, imag_part], axis=2).reshape(row_total, points, -1)


def mixing(weights, values):
    return jnp.einsum("kmoi,kmiz->kmoz", weights, values, preferred_element_type=jnp.float32)


def greet_members(members):
    me = lax.axis_index("member")
    slab = lax.axis_index("slab")
    chips = members // 2
    chip, core = me // 2, me % 2
    mesh_kind = pl.DeviceIdType.MESH
    barrier = pltpu.get_barrier_semaphore()
    pl.semaphore_signal(barrier, inc=1, device_id=(chip * 2 + 1 - core, slab), device_id_type=mesh_kind)
    for step in range(1, chips):
        peer = lax.rem(chip + step, chips) * 2 + core
        pl.semaphore_signal(barrier, inc=1, device_id=(peer, slab), device_id_type=mesh_kind)
    return barrier


def layer_values(members, back_ref, table_ref, weight_ref, field_ref, bias, value, layer):
    modes, slab_rows, width = back_ref.shape
    channels = weight_ref.shape[0]
    planes = width // (2 * channels)
    length = table_ref.shape[1]
    block_rows = layer.shape[2]
    table_real = table_ref[:modes, :]
    table_imag = table_ref[modes:, :]
    padding = jnp.zeros((width - modes, width), jnp.float32)
    for row in range(slab_rows):
        pencil = back_ref[:, row, :].astype(jnp.float32)
        pencil_t = jnp.concatenate([pencil, padding], axis=0).T[:, :modes].astype(back_ref.dtype)
        for plane in range(planes):
            cell = row * planes + plane
            base = plane * 2 * channels
            lanes = pl.ds(cell * length, length)
            spectral = jnp.dot(
                pencil_t[base:base + channels], table_real, preferred_element_type=jnp.float32
            )
            spectral = spectral + jnp.dot(
                pencil_t[base + channels:base + 2 * channels], table_imag,
                preferred_element_type=jnp.float32,
            )
            pointwise = jnp.dot(weight_ref[...], field_ref[:, lanes], preferred_element_type=jnp.float32)
            value[:, lanes] = jax.nn.gelu(pointwise + bias + spectral, approximate=True)
    for block in range(members):
        rows = pl.ds(block * block_rows, block_rows)
        layer[block % 2, block // 2] = value[rows, :].astype(layer.dtype)


def member_total(members, out_ref, layer, near, part, far, near_sems, far_send, far_recv):
    me = lax.axis_index("member")
    slab = lax.axis_index("slab")
    chips = members // 2
    chip, core = me // 2, me % 2
    sibling = chip * 2 + 1 - core
    mesh_kind = pl.DeviceIdType.MESH
    on_chip = pltpu.make_async_remote_copy(
        src_ref=layer.at[1 - core],
        dst_ref=near,
        send_sem=near_sems.at[0],
        recv_sem=near_sems.at[1],
        device_id=(sibling, slab),
        device_id_type=mesh_kind,
    )
    on_chip.start()
    on_chip.wait_recv()
    for index in range(chips):
        pair = layer[core, index].astype(jnp.float32) + near[index].astype(jnp.float32)
        part[index] = pair.astype(part.dtype)
    on_chip.wait_send()

    def copy_of(source, target, peer_chip):
        return pltpu.make_async_remote_copy(
            src_ref=part.at[source],
            dst_ref=far.at[target],
            send_sem=far_send.at[source],
            recv_sem=far_recv.at[target],
            device_id=(peer_chip * 2 + core, slab),
            device_id_type=mesh_kind,
        )

    for step in range(1, chips):
        peer = lax.rem(chip + step, chips)
        copy_of(peer, chip, peer).start()
    total = part[chip].astype(jnp.float32)
    for step in range(1, chips):
        source = lax.rem(chip + chips - step, chips)
        copy_of(source, source, source).wait_recv()
        total = total + far[source].astype(jnp.float32)
    for step in range(1, chips):
        peer = lax.rem(chip + step, chips)
        copy_of(peer, chip, peer).wait_send()
    out_ref[...] = (total / members).astype(out_ref.dtype)


def layer_sum_kernel(members, back_ref, table_ref, weight_ref, field_ref, bias_ref, out_ref, value, layer,
                     near, part, far, near_sems, far_send, far_recv):
    barrier = greet_members(members)
    layer_values(members, back_ref, table_ref, weight_ref, field_ref, bias_ref[...], value, layer)
    pl.semaphore_wait(barrier, members // 2)
    member_total(members, out_ref, layer, near, part, far, near_sems, far_send, far_recv)


def layer_sum(back, table, weight, field, bias, members):
    channels, width = field.shape
    block_rows = channels // members
    chips = members // 2
    return pl.pallas_call(
        functools.partial(layer_sum_kernel, members),
        out_shape=jax.ShapeDtypeStruct((block_rows, width), jnp.bfloat16),
        in_specs=[pl.BlockSpec(memory_space=pltpu.VMEM)] * 5,
        out_specs=pl.BlockSpec(memory_space=pltpu.VMEM),
        scratch_shapes=[
            pltpu.VMEM((channels, width), jnp.float32),
            pltpu.VMEM((2, chips, block_rows, width), jnp.bfloat16),
            pltpu.VMEM((chips, block_rows, width), jnp.bfloat16),
            pltpu.VMEM((chips, block_rows, width), jnp.bfloat16),
            pltpu.VMEM((chips, block_rows, width), jnp.bfloat16),
            pltpu.SemaphoreType.DMA((2,)),
            pltpu.SemaphoreType.DMA((chips,)),
            pltpu.SemaphoreType.DMA((chips,)),
        ],
        compiler_params=pltpu.CompilerParams(collective_id=0, has_side_effects=True),
    )(back, table, weight, field, bias)


def greet_slab(parts):
    me = lax.axis_index("slab")
    member = lax.axis_index("member")
    barrier = pltpu.get_barrier_semaphore()
    for step in range(1, parts):
        peer = lax.rem(me + step, parts)
        pl.semaphore_signal(barrier, inc=1, device_id=(member, peer), device_id_type=pl.DeviceIdType.MESH)
    return barrier


def swap_blocks(parts, source_ref, out_ref, landed, send_sems, recv_sems):
    me = lax.axis_index("slab")
    member = lax.axis_index("member")

    def copy_of(source, target, peer):
        return pltpu.make_async_remote_copy(
            src_ref=source_ref.at[source],
            dst_ref=landed.at[target],
            send_sem=send_sems.at[source],
            recv_sem=recv_sems.at[target],
            device_id=(member, peer),
            device_id_type=pl.DeviceIdType.MESH,
        )

    for step in range(1, parts):
        peer = lax.rem(me + step, parts)
        copy_of(peer, me, peer).start()
    landed[me] = source_ref[me]
    for step in range(1, parts):
        source = lax.rem(me + parts - step, parts)
        copy_of(source, source, source).wait_recv()
    for step in range(1, parts):
        peer = lax.rem(me + step, parts)
        copy_of(peer, me, peer).wait_send()
    if out_ref is not None:
        out_ref[...] = landed[...]


def slab_exchange_kernel(parts, blocks_ref, out_ref, landed, send_sems, recv_sems):
    barrier = greet_slab(parts)
    pl.semaphore_wait(barrier, parts - 1)
    swap_blocks(parts, blocks_ref, out_ref, landed, send_sems, recv_sems)


def smem_column(ref, count):
    rows = lax.broadcasted_iota(jnp.int32, (count, 1), 0)
    column = jnp.zeros((count, 1), jnp.float32)
    for index in range(count):
        column = jnp.where(rows == index, ref[index], column)
    return column


def mode_mix_kernel(parts, members, base_ref, forcing_ref, table_ref, xcos_t_ref, xsin_t_ref, swap_t_ref,
                    weight_ref, count_ref, back_table_ref, point_weight_ref, load_ref, amplitude_ref,
                    level_ref, bias_ref, out_ref, field_ref, mixed_t, modes_out, first, blocks, landed,
                    first_send, first_recv, send_sems, recv_sems, value, layer, near, part, far, near_sems,
                    far_send, far_recv):
    barrier = greet_slab(parts)
    greet_members(members)
    channels, cells_width = field_ref.shape
    scale = smem_column(load_ref, channels) * amplitude_ref[level_ref[0]]
    bias = smem_column(bias_ref, channels)
    chunk = table_ref.shape[2]
    rows_here, planes_here = base_ref.shape[1], base_ref.shape[2]
    for row in range(rows_here):
        for plane in range(planes_here):
            lanes = pl.ds((row * planes_here + plane) * chunk, chunk)
            driven = base_ref[:, row, plane, :].astype(jnp.float32) + scale * forcing_ref[
                pl.ds(row, 1), plane, :
            ].astype(jnp.float32)
            field_ref[:, lanes] = (2.0 * jnp.tanh(0.5 * driven)).astype(field_ref.dtype)
    modes, slab_rows, width = modes_out.shape
    channels = field_ref.shape[0]
    planes = width // (2 * channels)
    length = table_ref.shape[2]
    lane = lax.broadcasted_iota(jnp.int32, (modes, width), 1)
    real_lanes = (lane // channels) % 2 == 0
    contract_last = (((1,), (1,)), ((), ()))
    for row in range(slab_rows):
        pieces = []
        for plane in range(planes):
            cell = row * planes + plane
            values = field_ref[:, pl.ds(cell * length, length)]
            pieces += [values, values]
        stack = jnp.concatenate(pieces, axis=0)
        real = lax.dot_general(table_ref[0], stack, contract_last, preferred_element_type=jnp.float32)
        imag = lax.dot_general(table_ref[1], stack, contract_last, preferred_element_type=jnp.float32)
        modes_out[:, row, :] = jnp.where(real_lanes, real, imag).astype(modes_out.dtype)
    pl.semaphore_wait(barrier, parts - 1 + members // 2)
    swap_blocks(parts, modes_out, None, first, first_send, first_recv)
    pencil = first[...].astype(jnp.float32)
    pencil = pencil.reshape(pencil.shape[0] * pencil.shape[1], pencil.shape[2])
    pencil_t = pencil.T.astype(modes_out.dtype)
    swap_t = swap_t_ref[...]
    swapped_t = jnp.dot(swap_t, pencil_t, preferred_element_type=jnp.float32).astype(pencil_t.dtype)
    spec_t = jnp.dot(pencil_t, xcos_t_ref[...], preferred_element_type=jnp.float32)
    spec_t = spec_t + jnp.dot(swapped_t, xsin_t_ref[...], preferred_element_type=jnp.float32)
    spec_t = spec_t.astype(pencil_t.dtype).astype(jnp.float32)
    outputs = weight_ref.shape[1]
    planes = spec_t.shape[0] // (2 * outputs)
    for plane in range(planes):
        base = plane * 2 * outputs
        real = spec_t[base:base + outputs, :]
        imag = spec_t[base + outputs:base + 2 * outputs, :]
        for out in range(outputs):
            weight_real = weight_ref[0, out].astype(jnp.float32)
            weight_imag = weight_ref[1, out].astype(jnp.float32)
            mixed_t[pl.ds(base + out, 1), :] = jnp.sum(
                weight_real * real - weight_imag * imag, axis=0, keepdims=True
            )
            mixed_t[pl.ds(base + outputs + out, 1), :] = jnp.sum(
                weight_imag * real + weight_real * imag, axis=0, keepdims=True
            )
    kept = (lax.axis_index("slab") < count_ref[0]).astype(jnp.float32)
    mixed = (mixed_t[...] * kept).astype(pencil_t.dtype)
    mixed_swapped = jnp.dot(swap_t, mixed, preferred_element_type=jnp.float32).astype(pencil_t.dtype)
    contract = (((1,), (1,)), ((), ()))
    back = lax.dot_general(xcos_t_ref[...], mixed, contract, preferred_element_type=jnp.float32)
    back = back - lax.dot_general(
        xsin_t_ref[...], mixed_swapped, contract, preferred_element_type=jnp.float32
    )
    blocks[...] = back.reshape(blocks.shape).astype(blocks.dtype)
    swap_blocks(parts, blocks, None, landed, send_sems, recv_sems)
    layer_values(members, landed, back_table_ref, point_weight_ref, field_ref, bias, value, layer)
    member_total(members, out_ref, layer, near, part, far, near_sems, far_send, far_recv)


def mode_mix_exchange(base, forcing, table, xcos_t, xsin_t, swap_t, weight, count, back_table, point_weight,
                      load, amplitudes, level, bias, parts, members):
    field = base
    channels = field.shape[0]
    cells_width = field.shape[1] * field.shape[2] * field.shape[3]
    modes, length = table.shape[1], table.shape[2]
    width = swap_t.shape[0]
    planes = width // (2 * channels)
    shape = (modes, cells_width // (planes * length), width)
    block_rows = channels // members
    chips = members // 2
    return pl.pallas_call(
        functools.partial(mode_mix_kernel, parts, members),
        out_shape=jax.ShapeDtypeStruct((block_rows, cells_width), jnp.bfloat16),
        in_specs=[pl.BlockSpec(memory_space=pltpu.VMEM)] * 7
        + [pl.BlockSpec(memory_space=pltpu.SMEM)]
        + [pl.BlockSpec(memory_space=pltpu.VMEM)] * 2
        + [pl.BlockSpec(memory_space=pltpu.SMEM)] * 4,
        out_specs=pl.BlockSpec(memory_space=pltpu.VMEM),
        scratch_shapes=[
            pltpu.VMEM((channels, cells_width), jnp.bfloat16),
            pltpu.VMEM((width, modes), jnp.float32),
            pltpu.VMEM(shape, field.dtype),
            pltpu.VMEM(shape, field.dtype),
            pltpu.VMEM(shape, field.dtype),
            pltpu.VMEM(shape, field.dtype),
            pltpu.SemaphoreType.DMA((parts,)),
            pltpu.SemaphoreType.DMA((parts,)),
            pltpu.SemaphoreType.DMA((parts,)),
            pltpu.SemaphoreType.DMA((parts,)),
            pltpu.VMEM((channels, cells_width), jnp.float32),
            pltpu.VMEM((2, chips, block_rows, cells_width), jnp.bfloat16),
            pltpu.VMEM((chips, block_rows, cells_width), jnp.bfloat16),
            pltpu.VMEM((chips, block_rows, cells_width), jnp.bfloat16),
            pltpu.VMEM((chips, block_rows, cells_width), jnp.bfloat16),
            pltpu.SemaphoreType.DMA((2,)),
            pltpu.SemaphoreType.DMA((chips,)),
            pltpu.SemaphoreType.DMA((chips,)),
        ],
        compiler_params=pltpu.CompilerParams(collective_id=2, has_side_effects=True),
    )(base, forcing, table, xcos_t, xsin_t, swap_t, weight, count, back_table, point_weight, load, amplitudes,
      level, bias)


def slab_exchange(blocks, parts, exchange_id):
    return pl.pallas_call(
        functools.partial(slab_exchange_kernel, parts),
        out_shape=jax.ShapeDtypeStruct(blocks.shape, blocks.dtype),
        in_specs=[pl.BlockSpec(memory_space=pltpu.VMEM)],
        out_specs=pl.BlockSpec(memory_space=pltpu.VMEM),
        scratch_shapes=[
            pltpu.VMEM(blocks.shape, blocks.dtype),
            pltpu.SemaphoreType.DMA((parts,)),
            pltpu.SemaphoreType.DMA((parts,)),
        ],
        compiler_params=pltpu.CompilerParams(collective_id=exchange_id, has_side_effects=True),
    )(blocks)


def local(
    base_field,
    forcing,
    load,
    amplitudes,
    amp_index,
    mode_count,
    point_weight,
    point_bias,
    spectral_weight,
):
    channels, slab_rows, plane_count, length_y = base_field.shape
    slab_count = lax.axis_size("slab")
    local_modes = spectral_weight.shape[0]
    modes_y = local_modes * slab_count
    modes_x = spectral_weight.shape[1]
    length_x = slab_rows * slab_count
    packed_width = 2 * channels * plane_count
    slab_index = lax.axis_index("slab")
    cells = slab_rows * plane_count
    y_cos, y_sin = phase_tables(np.arange(modes_y), np.arange(length_y), length_y)
    forward_table = bf16_constant(np.stack([y_cos, -y_sin]))
    frequency_x = np.concatenate(
        [np.arange(modes_x // 2), np.arange(length_x - modes_x // 2, length_x)]
    )
    full_cos, full_sin = phase_tables(frequency_x, np.arange(length_x), length_x)
    lane = np.arange(packed_width)
    real_lane = (lane // channels) % 2 == 0
    swap = np.where(
        real_lane[None, :],
        (lane[:, None] == lane[None, :] + channels).astype(np.float32),
        -(lane[:, None] == lane[None, :] - channels).astype(np.float32),
    )
    weight = spectral_weight[0].transpose(1, 2, 3, 0)
    weights_y = np.where(np.arange(modes_y) == 0, 1.0, 2.0).astype(np.float32) / np.float32(
        length_x * length_y
    )
    table = bf16_constant(
        np.concatenate([weights_y[:, None] * y_cos, -(weights_y[:, None] * y_sin)], axis=0)
    )
    members = lax.axis_size("member")
    total = mode_mix_exchange(
        base_field, forcing, forward_table, bf16_constant(full_cos.T), bf16_constant(full_sin.T),
        bf16_constant(swap.T), weight, mode_count, table, point_weight, load, amplitudes, amp_index,
        point_bias, slab_count, members,
    )
    return total.reshape(channels // members, slab_rows, plane_count, length_y)


def solution(mesh):
    in_specs = (
        P(None, "slab", None, None),
        P("slab", None, None),
        P(),
        P(),
        P("member"),
        P("member"),
        P(),
        P(),
        P("slab", None, None, None, None),
    )
    out_specs = P("member", "slab", None, None)
    return jax.shard_map(local, mesh=mesh, in_specs=in_specs, out_specs=out_specs, check_vma=False)
```

```python
import functools
import math

import jax
import ml_dtypes
import numpy as np
import jax.numpy as jnp
from jax import lax
from jax.experimental import pallas as pl
from jax.experimental.pallas import tpu as pltpu
from jax.sharding import PartitionSpec as P

TWO_PI = 2.0 * math.pi


def phase_tables(frequency, positions, length):
    product = np.outer(frequency, positions) % length
    angles = (product.astype(np.float32) * np.float32(TWO_PI / length)).astype(np.float64)
    return np.cos(angles).astype(np.float32), np.sin(angles).astype(np.float32)


def bf16_constant(values):
    return jnp.asarray(np.asarray(values, np.float32).astype(ml_dtypes.bfloat16))


def phases(frequency, positions, length):
    product = frequency[:, None] * positions[None, :] % length
    angles = product.astype(jnp.float32) * (TWO_PI / length)
    return (jnp.cos(angles), jnp.sin(angles))


def forward_x(pencil, cos_table, sin_table):
    row_total = pencil.shape[0]
    modes = cos_table.shape[0]
    with_cos = jnp.einsum(
        "kxf,mx->kmf", pencil, cos_table, preferred_element_type=jnp.float32
    ).reshape(row_total, modes, 2, -1)
    with_sin = jnp.einsum(
        "kxf,mx->kmf", pencil, sin_table, preferred_element_type=jnp.float32
    ).reshape(row_total, modes, 2, -1)
    real_part = with_cos[:, :, 0] + with_sin[:, :, 1]
    imag_part = with_cos[:, :, 1] - with_sin[:, :, 0]
    return jnp.stack([real_part, imag_part], axis=2).reshape(row_total, modes, -1)


def inverse_x(spectra, cos_table, sin_table):
    row_total = spectra.shape[0]
    points = cos_table.shape[1]
    with_cos = jnp.einsum(
        "kmf,mx->kxf", spectra, cos_table, preferred_element_type=jnp.float32
    ).reshape(row_total, points, 2, -1)
    with_sin = jnp.einsum(
        "kmf,mx->kxf", spectra, sin_table, preferred_element_type=jnp.float32
    ).reshape(row_total, points, 2, -1)
    real_part = with_cos[:, :, 0] - with_sin[:, :, 1]
    imag_part = with_cos[:, :, 1] + with_sin[:, :, 0]
    return jnp.stack([real_part, imag_part], axis=2).reshape(row_total, points, -1)


def mixing(weights, values):
    return jnp.einsum("kmoi,kmiz->kmoz", weights, values, preferred_element_type=jnp.float32)


def greet_members(members):
    me = lax.axis_index("member")
    slab = lax.axis_index("slab")
    chips = members // 2
    chip, core = me // 2, me % 2
    mesh_kind = pl.DeviceIdType.MESH
    barrier = pltpu.get_barrier_semaphore()
    pl.semaphore_signal(barrier, inc=1, device_id=(chip * 2 + 1 - core, slab), device_id_type=mesh_kind)
    for step in range(1, chips):
        peer = lax.rem(chip + step, chips) * 2 + core
        pl.semaphore_signal(barrier, inc=1, device_id=(peer, slab), device_id_type=mesh_kind)
    return barrier


def layer_values(members, back_ref, table_ref, weight_ref, field_ref, bias, value, layer):
    modes, slab_rows, width = back_ref.shape
    channels = weight_ref.shape[0]
    planes = width // (2 * channels)
    length = table_ref.shape[1]
    block_rows = layer.shape[2]
    table_real = table_ref[:modes, :]
    table_imag = table_ref[modes:, :]
    padding = jnp.zeros((width - modes, width), jnp.float32)
    for row in range(slab_rows):
        pencil = back_ref[:, row, :].astype(jnp.float32)
        pencil_t = jnp.concatenate([pencil, padding], axis=0).T[:, :modes].astype(back_ref.dtype)
        for plane in range(planes):
            cell = row * planes + plane
            base = plane * 2 * channels
            lanes = pl.ds(cell * length, length)
            spectral = jnp.dot(
                pencil_t[base:base + channels], table_real, preferred_element_type=jnp.float32
            )
            spectral = spectral + jnp.dot(
                pencil_t[base + channels:base + 2 * channels], table_imag,
                preferred_element_type=jnp.float32,
            )
            pointwise = jnp.dot(weight_ref[...], field_ref[:, lanes], preferred_element_type=jnp.float32)
            value[:, lanes] = jax.nn.gelu(pointwise + bias + spectral, approximate=True)
    for block in range(members):
        rows = pl.ds(block * block_rows, block_rows)
        layer[block % 2, block // 2] = value[rows, :].astype(layer.dtype)


def member_total(members, out_ref, layer, near, part, far, near_sems, far_send, far_recv):
    me = lax.axis_index("member")
    slab = lax.axis_index("slab")
    chips = members // 2
    chip, core = me // 2, me % 2
    sibling = chip * 2 + 1 - core
    mesh_kind = pl.DeviceIdType.MESH
    on_chip = pltpu.make_async_remote_copy(
        src_ref=layer.at[1 - core],
        dst_ref=near,
        send_sem=near_sems.at[0],
        recv_sem=near_sems.at[1],
        device_id=(sibling, slab),
        device_id_type=mesh_kind,
    )
    on_chip.start()
    on_chip.wait_recv()
    for index in range(chips):
        pair = layer[core, index].astype(jnp.float32) + near[index].astype(jnp.float32)
        part[index] = pair.astype(part.dtype)
    on_chip.wait_send()

    def copy_of(source, target, peer_chip):
        return pltpu.make_async_remote_copy(
            src_ref=part.at[source],
            dst_ref=far.at[target],
            send_sem=far_send.at[source],
            recv_sem=far_recv.at[target],
            device_id=(peer_chip * 2 + core, slab),
            device_id_type=mesh_kind,
        )

    for step in range(1, chips):
        peer = lax.rem(chip + step, chips)
        copy_of(peer, chip, peer).start()
    total = part[chip].astype(jnp.float32)
    for step in range(1, chips):
        source = lax.rem(chip + chips - step, chips)
        copy_of(source, source, source).wait_recv()
        total = total + far[source].astype(jnp.float32)
    for step in range(1, chips):
        peer = lax.rem(chip + step, chips)
        copy_of(peer, chip, peer).wait_send()
    mean = (total / members).astype(out_ref.dtype)
    if len(out_ref.shape) == 2:
        out_ref[...] = mean
    else:
        rows_out, planes_out, length_out = out_ref.shape[1], out_ref.shape[2], out_ref.shape[3]
        for row in range(rows_out):
            for plane in range(planes_out):
                cell = row * planes_out + plane
                out_ref[:, row, plane, :] = mean[:, cell * length_out:(cell + 1) * length_out]


def layer_sum_kernel(members, back_ref, table_ref, weight_ref, field_ref, bias_ref, out_ref, value, layer,
                     near, part, far, near_sems, far_send, far_recv):
    barrier = greet_members(members)
    layer_values(members, back_ref, table_ref, weight_ref, field_ref, bias_ref[...], value, layer)
    pl.semaphore_wait(barrier, members // 2)
    member_total(members, out_ref, layer, near, part, far, near_sems, far_send, far_recv)


def layer_sum(back, table, weight, field, bias, members):
    channels, width = field.shape
    block_rows = channels // members
    chips = members // 2
    return pl.pallas_call(
        functools.partial(layer_sum_kernel, members),
        out_shape=jax.ShapeDtypeStruct((block_rows, width), jnp.bfloat16),
        in_specs=[pl.BlockSpec(memory_space=pltpu.VMEM)] * 5,
        out_specs=pl.BlockSpec(memory_space=pltpu.VMEM),
        scratch_shapes=[
            pltpu.VMEM((channels, width), jnp.float32),
            pltpu.VMEM((2, chips, block_rows, width), jnp.bfloat16),
            pltpu.VMEM((chips, block_rows, width), jnp.bfloat16),
            pltpu.VMEM((chips, block_rows, width), jnp.bfloat16),
            pltpu.VMEM((chips, block_rows, width), jnp.bfloat16),
            pltpu.SemaphoreType.DMA((2,)),
            pltpu.SemaphoreType.DMA((chips,)),
            pltpu.SemaphoreType.DMA((chips,)),
        ],
        compiler_params=pltpu.CompilerParams(collective_id=0, has_side_effects=True),
    )(back, table, weight, field, bias)


def greet_slab(parts):
    me = lax.axis_index("slab")
    member = lax.axis_index("member")
    barrier = pltpu.get_barrier_semaphore()
    for step in range(1, parts):
        peer = lax.rem(me + step, parts)
        pl.semaphore_signal(barrier, inc=1, device_id=(member, peer), device_id_type=pl.DeviceIdType.MESH)
    return barrier


def swap_blocks(parts, source_ref, out_ref, landed, send_sems, recv_sems):
    me = lax.axis_index("slab")
    member = lax.axis_index("member")

    def copy_of(source, target, peer):
        return pltpu.make_async_remote_copy(
            src_ref=source_ref.at[source],
            dst_ref=landed.at[target],
            send_sem=send_sems.at[source],
            recv_sem=recv_sems.at[target],
            device_id=(member, peer),
            device_id_type=pl.DeviceIdType.MESH,
        )

    for step in range(1, parts):
        peer = lax.rem(me + step, parts)
        copy_of(peer, me, peer).start()
    landed[me] = source_ref[me]
    for step in range(1, parts):
        source = lax.rem(me + parts - step, parts)
        copy_of(source, source, source).wait_recv()
    for step in range(1, parts):
        peer = lax.rem(me + step, parts)
        copy_of(peer, me, peer).wait_send()
    if out_ref is not None:
        out_ref[...] = landed[...]


def slab_exchange_kernel(parts, blocks_ref, out_ref, landed, send_sems, recv_sems):
    barrier = greet_slab(parts)
    pl.semaphore_wait(barrier, parts - 1)
    swap_blocks(parts, blocks_ref, out_ref, landed, send_sems, recv_sems)


def smem_column(ref, count):
    rows = lax.broadcasted_iota(jnp.int32, (count, 1), 0)
    column = jnp.zeros((count, 1), jnp.float32)
    for index in range(count):
        column = jnp.where(rows == index, ref[index], column)
    return column


def mode_mix_kernel(parts, members, base_ref, forcing_ref, table_ref, xcos_t_ref, xsin_t_ref, swap_t_ref,
                    weight_ref, count_ref, back_table_ref, point_weight_ref, load_ref, amplitude_ref,
                    level_ref, bias_ref, out_ref, field_ref, mixed_t, modes_out, first, blocks, landed,
                    first_send, first_recv, send_sems, recv_sems, value, layer, near, part, far, near_sems,
                    far_send, far_recv):
    barrier = greet_slab(parts)
    greet_members(members)
    channels, cells_width = field_ref.shape
    scale = smem_column(load_ref, channels) * amplitude_ref[level_ref[0]]
    bias = smem_column(bias_ref, channels)
    chunk = table_ref.shape[2]
    rows_here, planes_here = base_ref.shape[1], base_ref.shape[2]
    for row in range(rows_here):
        for plane in range(planes_here):
            lanes = pl.ds((row * planes_here + plane) * chunk, chunk)
            driven = base_ref[:, row, plane, :].astype(jnp.float32) + scale * forcing_ref[
                pl.ds(row, 1), plane, :
            ].astype(jnp.float32)
            field_ref[:, lanes] = (2.0 * jnp.tanh(0.5 * driven)).astype(field_ref.dtype)
    modes, slab_rows, width = modes_out.shape
    channels = field_ref.shape[0]
    planes = width // (2 * channels)
    length = table_ref.shape[2]
    lane = lax.broadcasted_iota(jnp.int32, (modes, width), 1)
    real_lanes = (lane // channels) % 2 == 0
    contract_last = (((1,), (1,)), ((), ()))
    for row in range(slab_rows):
        pieces = []
        for plane in range(planes):
            cell = row * planes + plane
            values = field_ref[:, pl.ds(cell * length, length)]
            pieces += [values, values]
        stack = jnp.concatenate(pieces, axis=0)
        real = lax.dot_general(table_ref[0], stack, contract_last, preferred_element_type=jnp.float32)
        imag = lax.dot_general(table_ref[1], stack, contract_last, preferred_element_type=jnp.float32)
        modes_out[:, row, :] = jnp.where(real_lanes, real, imag).astype(modes_out.dtype)
    pl.semaphore_wait(barrier, parts - 1 + members // 2)
    swap_blocks(parts, modes_out, None, first, first_send, first_recv)
    pencil = first[...].astype(jnp.float32)
    pencil = pencil.reshape(pencil.shape[0] * pencil.shape[1], pencil.shape[2])
    pencil_t = pencil.T.astype(modes_out.dtype)
    swap_t = swap_t_ref[...]
    swapped_t = jnp.dot(swap_t, pencil_t, preferred_element_type=jnp.float32).astype(pencil_t.dtype)
    spec_t = jnp.dot(pencil_t, xcos_t_ref[...], preferred_element_type=jnp.float32)
    spec_t = spec_t + jnp.dot(swapped_t, xsin_t_ref[...], preferred_element_type=jnp.float32)
    spec_t = spec_t.astype(pencil_t.dtype).astype(jnp.float32)
    outputs = weight_ref.shape[1]
    planes = spec_t.shape[0] // (2 * outputs)
    for plane in range(planes):
        base = plane * 2 * outputs
        real = spec_t[base:base + outputs, :]
        imag = spec_t[base + outputs:base + 2 * outputs, :]
        for out in range(outputs):
            weight_real = weight_ref[0, out].astype(jnp.float32)
            weight_imag = weight_ref[1, out].astype(jnp.float32)
            mixed_t[pl.ds(base + out, 1), :] = jnp.sum(
                weight_real * real - weight_imag * imag, axis=0, keepdims=True
            )
            mixed_t[pl.ds(base + outputs + out, 1), :] = jnp.sum(
                weight_imag * real + weight_real * imag, axis=0, keepdims=True
            )
    kept = (lax.axis_index("slab") < count_ref[0]).astype(jnp.float32)
    mixed = (mixed_t[...] * kept).astype(pencil_t.dtype)
    mixed_swapped = jnp.dot(swap_t, mixed, preferred_element_type=jnp.float32).astype(pencil_t.dtype)
    contract = (((1,), (1,)), ((), ()))
    back = lax.dot_general(xcos_t_ref[...], mixed, contract, preferred_element_type=jnp.float32)
    back = back - lax.dot_general(
        xsin_t_ref[...], mixed_swapped, contract, preferred_element_type=jnp.float32
    )
    blocks[...] = back.reshape(blocks.shape).astype(blocks.dtype)
    swap_blocks(parts, blocks, None, landed, send_sems, recv_sems)
    layer_values(members, landed, back_table_ref, point_weight_ref, field_ref, bias, value, layer)
    member_total(members, out_ref, layer, near, part, far, near_sems, far_send, far_recv)


def mode_mix_exchange(base, forcing, table, xcos_t, xsin_t, swap_t, weight, count, back_table, point_weight,
                      load, amplitudes, level, bias, parts, members):
    field = base
    channels = field.shape[0]
    cells_width = field.shape[1] * field.shape[2] * field.shape[3]
    modes, length = table.shape[1], table.shape[2]
    width = swap_t.shape[0]
    planes = width // (2 * channels)
    shape = (modes, cells_width // (planes * length), width)
    block_rows = channels // members
    chips = members // 2
    return pl.pallas_call(
        functools.partial(mode_mix_kernel, parts, members),
        out_shape=jax.ShapeDtypeStruct((block_rows,) + base.shape[1:], jnp.bfloat16),
        in_specs=[pl.BlockSpec(memory_space=pltpu.VMEM)] * 7
        + [pl.BlockSpec(memory_space=pltpu.SMEM)]
        + [pl.BlockSpec(memory_space=pltpu.VMEM)] * 2
        + [pl.BlockSpec(memory_space=pltpu.SMEM)] * 4,
        out_specs=pl.BlockSpec(memory_space=pltpu.VMEM),
        scratch_shapes=[
            pltpu.VMEM((channels, cells_width), jnp.bfloat16),
            pltpu.VMEM((width, modes), jnp.float32),
            pltpu.VMEM(shape, field.dtype),
            pltpu.VMEM(shape, field.dtype),
            pltpu.VMEM(shape, field.dtype),
            pltpu.VMEM(shape, field.dtype),
            pltpu.SemaphoreType.DMA((parts,)),
            pltpu.SemaphoreType.DMA((parts,)),
            pltpu.SemaphoreType.DMA((parts,)),
            pltpu.SemaphoreType.DMA((parts,)),
            pltpu.VMEM((channels, cells_width), jnp.float32),
            pltpu.VMEM((2, chips, block_rows, cells_width), jnp.bfloat16),
            pltpu.VMEM((chips, block_rows, cells_width), jnp.bfloat16),
            pltpu.VMEM((chips, block_rows, cells_width), jnp.bfloat16),
            pltpu.VMEM((chips, block_rows, cells_width), jnp.bfloat16),
            pltpu.SemaphoreType.DMA((2,)),
            pltpu.SemaphoreType.DMA((chips,)),
            pltpu.SemaphoreType.DMA((chips,)),
        ],
        compiler_params=pltpu.CompilerParams(collective_id=2, has_side_effects=True),
    )(base, forcing, table, xcos_t, xsin_t, swap_t, weight, count, back_table, point_weight, load, amplitudes,
      level, bias)


def slab_exchange(blocks, parts, exchange_id):
    return pl.pallas_call(
        functools.partial(slab_exchange_kernel, parts),
        out_shape=jax.ShapeDtypeStruct(blocks.shape, blocks.dtype),
        in_specs=[pl.BlockSpec(memory_space=pltpu.VMEM)],
        out_specs=pl.BlockSpec(memory_space=pltpu.VMEM),
        scratch_shapes=[
            pltpu.VMEM(blocks.shape, blocks.dtype),
            pltpu.SemaphoreType.DMA((parts,)),
            pltpu.SemaphoreType.DMA((parts,)),
        ],
        compiler_params=pltpu.CompilerParams(collective_id=exchange_id, has_side_effects=True),
    )(blocks)


def local(
    base_field,
    forcing,
    load,
    amplitudes,
    amp_index,
    mode_count,
    point_weight,
    point_bias,
    spectral_weight,
):
    channels, slab_rows, plane_count, length_y = base_field.shape
    slab_count = lax.axis_size("slab")
    local_modes = spectral_weight.shape[0]
    modes_y = local_modes * slab_count
    modes_x = spectral_weight.shape[1]
    length_x = slab_rows * slab_count
    packed_width = 2 * channels * plane_count
    slab_index = lax.axis_index("slab")
    cells = slab_rows * plane_count
    y_cos, y_sin = phase_tables(np.arange(modes_y), np.arange(length_y), length_y)
    forward_table = bf16_constant(np.stack([y_cos, -y_sin]))
    frequency_x = np.concatenate(
        [np.arange(modes_x // 2), np.arange(length_x - modes_x // 2, length_x)]
    )
    full_cos, full_sin = phase_tables(frequency_x, np.arange(length_x), length_x)
    lane = np.arange(packed_width)
    real_lane = (lane // channels) % 2 == 0
    swap = np.where(
        real_lane[None, :],
        (lane[:, None] == lane[None, :] + channels).astype(np.float32),
        -(lane[:, None] == lane[None, :] - channels).astype(np.float32),
    )
    weight = spectral_weight[0].transpose(1, 2, 3, 0)
    weights_y = np.where(np.arange(modes_y) == 0, 1.0, 2.0).astype(np.float32) / np.float32(
        length_x * length_y
    )
    table = bf16_constant(
        np.concatenate([weights_y[:, None] * y_cos, -(weights_y[:, None] * y_sin)], axis=0)
    )
    members = lax.axis_size("member")
    total = mode_mix_exchange(
        base_field, forcing, forward_table, bf16_constant(full_cos.T), bf16_constant(full_sin.T),
        bf16_constant(swap.T), weight, mode_count, table, point_weight, load, amplitudes, amp_index,
        point_bias, slab_count, members,
    )
    return total


def solution(mesh):
    in_specs = (
        P(None, "slab", None, None),
        P("slab", None, None),
        P(),
        P(),
        P("member"),
        P("member"),
        P(),
        P(),
        P("slab", None, None, None, None),
    )
    out_specs = P("member", "slab", None, None)
    return jax.shard_map(local, mesh=mesh, in_specs=in_specs, out_specs=out_specs, check_vma=False)
```

```python
import functools
import math

import jax
import ml_dtypes
import numpy as np
import jax.numpy as jnp
from jax import lax
from jax.experimental import pallas as pl
from jax.experimental.pallas import tpu as pltpu
from jax.sharding import PartitionSpec as P

TWO_PI = 2.0 * math.pi


def phase_tables(frequency, positions, length):
    product = np.outer(frequency, positions) % length
    angles = (product.astype(np.float32) * np.float32(TWO_PI / length)).astype(np.float64)
    return np.cos(angles).astype(np.float32), np.sin(angles).astype(np.float32)


def bf16_constant(values):
    return jnp.asarray(np.asarray(values, np.float32).astype(ml_dtypes.bfloat16))


def phases(frequency, positions, length):
    product = frequency[:, None] * positions[None, :] % length
    angles = product.astype(jnp.float32) * (TWO_PI / length)
    return (jnp.cos(angles), jnp.sin(angles))


def forward_x(pencil, cos_table, sin_table):
    row_total = pencil.shape[0]
    modes = cos_table.shape[0]
    with_cos = jnp.einsum(
        "kxf,mx->kmf", pencil, cos_table, preferred_element_type=jnp.float32
    ).reshape(row_total, modes, 2, -1)
    with_sin = jnp.einsum(
        "kxf,mx->kmf", pencil, sin_table, preferred_element_type=jnp.float32
    ).reshape(row_total, modes, 2, -1)
    real_part = with_cos[:, :, 0] + with_sin[:, :, 1]
    imag_part = with_cos[:, :, 1] - with_sin[:, :, 0]
    return jnp.stack([real_part, imag_part], axis=2).reshape(row_total, modes, -1)


def inverse_x(spectra, cos_table, sin_table):
    row_total = spectra.shape[0]
    points = cos_table.shape[1]
    with_cos = jnp.einsum(
        "kmf,mx->kxf", spectra, cos_table, preferred_element_type=jnp.float32
    ).reshape(row_total, points, 2, -1)
    with_sin = jnp.einsum(
        "kmf,mx->kxf", spectra, sin_table, preferred_element_type=jnp.float32
    ).reshape(row_total, points, 2, -1)
    real_part = with_cos[:, :, 0] - with_sin[:, :, 1]
    imag_part = with_cos[:, :, 1] + with_sin[:, :, 0]
    return jnp.stack([real_part, imag_part], axis=2).reshape(row_total, points, -1)


def mixing(weights, values):
    return jnp.einsum("kmoi,kmiz->kmoz", weights, values, preferred_element_type=jnp.float32)


def greet_members(members):
    me = lax.axis_index("member")
    slab = lax.axis_index("slab")
    chips = members // 2
    chip, core = me // 2, me % 2
    mesh_kind = pl.DeviceIdType.MESH
    barrier = pltpu.get_barrier_semaphore()
    pl.semaphore_signal(barrier, inc=1, device_id=(chip * 2 + 1 - core, slab), device_id_type=mesh_kind)
    for step in range(1, chips):
        peer = lax.rem(chip + step, chips) * 2 + core
        pl.semaphore_signal(barrier, inc=1, device_id=(peer, slab), device_id_type=mesh_kind)
    return barrier


def layer_values(members, back_ref, table_ref, weight_ref, field_ref, bias, value, layer):
    modes, slab_rows, width = back_ref.shape
    channels = weight_ref.shape[0]
    planes = width // (2 * channels)
    length = table_ref.shape[1]
    block_rows = layer.shape[2]
    table_real = table_ref[:modes, :]
    table_imag = table_ref[modes:, :]
    padding = jnp.zeros((width - modes, width), jnp.float32)
    for row in range(slab_rows):
        pencil = back_ref[:, row, :].astype(jnp.float32)
        pencil_t = jnp.concatenate([pencil, padding], axis=0).T[:, :modes].astype(back_ref.dtype)
        for plane in range(planes):
            cell = row * planes + plane
            base = plane * 2 * channels
            lanes = pl.ds(cell * length, length)
            spectral = jnp.dot(
                pencil_t[base:base + channels], table_real, preferred_element_type=jnp.float32
            )
            spectral = spectral + jnp.dot(
                pencil_t[base + channels:base + 2 * channels], table_imag,
                preferred_element_type=jnp.float32,
            )
            pointwise = jnp.dot(weight_ref[...], field_ref[:, lanes], preferred_element_type=jnp.float32)
            value[:, lanes] = jax.nn.gelu(pointwise + bias + spectral, approximate=True)
    for block in range(members):
        rows = pl.ds(block * block_rows, block_rows)
        layer[block % 2, block // 2] = value[rows, :].astype(layer.dtype)


def member_total(members, out_ref, layer, near, part, far, near_sems, far_send, far_recv):
    me = lax.axis_index("member")
    slab = lax.axis_index("slab")
    chips = members // 2
    chip, core = me // 2, me % 2
    sibling = chip * 2 + 1 - core
    mesh_kind = pl.DeviceIdType.MESH
    on_chip = pltpu.make_async_remote_copy(
        src_ref=layer.at[1 - core],
        dst_ref=near,
        send_sem=near_sems.at[0],
        recv_sem=near_sems.at[1],
        device_id=(sibling, slab),
        device_id_type=mesh_kind,
    )
    on_chip.start()
    on_chip.wait_recv()
    for index in range(chips):
        pair = layer[core, index].astype(jnp.float32) + near[index].astype(jnp.float32)
        part[index] = pair.astype(part.dtype)
    on_chip.wait_send()

    def copy_of(source, target, peer_chip):
        return pltpu.make_async_remote_copy(
            src_ref=part.at[source],
            dst_ref=far.at[target],
            send_sem=far_send.at[source],
            recv_sem=far_recv.at[target],
            device_id=(peer_chip * 2 + core, slab),
            device_id_type=mesh_kind,
        )

    for step in range(1, chips):
        peer = lax.rem(chip + step, chips)
        copy_of(peer, chip, peer).start()
    total = part[chip].astype(jnp.float32)
    for step in range(1, chips):
        source = lax.rem(chip + chips - step, chips)
        copy_of(source, source, source).wait_recv()
        total = total + far[source].astype(jnp.float32)
    for step in range(1, chips):
        peer = lax.rem(chip + step, chips)
        copy_of(peer, chip, peer).wait_send()
    mean = (total / members).astype(out_ref.dtype)
    if len(out_ref.shape) == 2:
        out_ref[...] = mean
    else:
        rows_out, planes_out, length_out = out_ref.shape[1], out_ref.shape[2], out_ref.shape[3]
        for row in range(rows_out):
            for plane in range(planes_out):
                cell = row * planes_out + plane
                out_ref[:, row, plane, :] = mean[:, cell * length_out:(cell + 1) * length_out]


def layer_sum_kernel(members, back_ref, table_ref, weight_ref, field_ref, bias_ref, out_ref, value, layer,
                     near, part, far, near_sems, far_send, far_recv):
    barrier = greet_members(members)
    layer_values(members, back_ref, table_ref, weight_ref, field_ref, bias_ref[...], value, layer)
    pl.semaphore_wait(barrier, members // 2)
    member_total(members, out_ref, layer, near, part, far, near_sems, far_send, far_recv)


def layer_sum(back, table, weight, field, bias, members):
    channels, width = field.shape
    block_rows = channels // members
    chips = members // 2
    return pl.pallas_call(
        functools.partial(layer_sum_kernel, members),
        out_shape=jax.ShapeDtypeStruct((block_rows, width), jnp.bfloat16),
        in_specs=[pl.BlockSpec(memory_space=pltpu.VMEM)] * 5,
        out_specs=pl.BlockSpec(memory_space=pltpu.VMEM),
        scratch_shapes=[
            pltpu.VMEM((channels, width), jnp.float32),
            pltpu.VMEM((2, chips, block_rows, width), jnp.bfloat16),
            pltpu.VMEM((chips, block_rows, width), jnp.bfloat16),
            pltpu.VMEM((chips, block_rows, width), jnp.bfloat16),
            pltpu.VMEM((chips, block_rows, width), jnp.bfloat16),
            pltpu.SemaphoreType.DMA((2,)),
            pltpu.SemaphoreType.DMA((chips,)),
            pltpu.SemaphoreType.DMA((chips,)),
        ],
        compiler_params=pltpu.CompilerParams(collective_id=0, has_side_effects=True),
    )(back, table, weight, field, bias)


def greet_slab(parts):
    me = lax.axis_index("slab")
    member = lax.axis_index("member")
    barrier = pltpu.get_barrier_semaphore()
    for step in range(1, parts):
        peer = lax.rem(me + step, parts)
        pl.semaphore_signal(barrier, inc=1, device_id=(member, peer), device_id_type=pl.DeviceIdType.MESH)
    return barrier


def swap_blocks(parts, source_ref, out_ref, landed, send_sems, recv_sems):
    me = lax.axis_index("slab")
    member = lax.axis_index("member")

    def copy_of(source, target, peer):
        return pltpu.make_async_remote_copy(
            src_ref=source_ref.at[source],
            dst_ref=landed.at[target],
            send_sem=send_sems.at[source],
            recv_sem=recv_sems.at[target],
            device_id=(member, peer),
            device_id_type=pl.DeviceIdType.MESH,
        )

    for step in range(1, parts):
        peer = lax.rem(me + step, parts)
        copy_of(peer, me, peer).start()
    landed[me] = source_ref[me]
    for step in range(1, parts):
        source = lax.rem(me + parts - step, parts)
        copy_of(source, source, source).wait_recv()
    for step in range(1, parts):
        peer = lax.rem(me + step, parts)
        copy_of(peer, me, peer).wait_send()
    if out_ref is not None:
        out_ref[...] = landed[...]


def slab_exchange_kernel(parts, blocks_ref, out_ref, landed, send_sems, recv_sems):
    barrier = greet_slab(parts)
    pl.semaphore_wait(barrier, parts - 1)
    swap_blocks(parts, blocks_ref, out_ref, landed, send_sems, recv_sems)


def smem_column(ref, count):
    rows = lax.broadcasted_iota(jnp.int32, (count, 1), 0)
    column = jnp.zeros((count, 1), jnp.float32)
    for index in range(count):
        column = jnp.where(rows == index, ref[index], column)
    return column


def mode_mix_kernel(parts, members, base_ref, forcing_ref, table_ref, xcos_t_ref, xsin_t_ref, swap_t_ref,
                    weight_ref, count_ref, back_table_ref, point_weight_ref, load_ref, amplitude_ref,
                    level_ref, bias_ref, out_ref, field_ref, mixed_t, modes_out, first, blocks, landed,
                    first_send, first_recv, send_sems, recv_sems, value, layer, near, part, far, near_sems,
                    far_send, far_recv):
    barrier = greet_slab(parts)
    greet_members(members)
    channels, cells_width = field_ref.shape
    scale = smem_column(load_ref, channels) * amplitude_ref[level_ref[0]]
    bias = smem_column(bias_ref, channels)
    chunk = table_ref.shape[2]
    rows_here, planes_here = base_ref.shape[1], base_ref.shape[2]
    for row in range(rows_here):
        for plane in range(planes_here):
            lanes = pl.ds((row * planes_here + plane) * chunk, chunk)
            driven = base_ref[:, row, plane, :].astype(jnp.float32) + scale * forcing_ref[
                pl.ds(row, 1), plane, :
            ].astype(jnp.float32)
            field_ref[:, lanes] = (2.0 * jnp.tanh(0.5 * driven)).astype(field_ref.dtype)
    modes, slab_rows, width = modes_out.shape
    channels = field_ref.shape[0]
    planes = width // (2 * channels)
    length = table_ref.shape[2]
    lane = lax.broadcasted_iota(jnp.int32, (modes, width), 1)
    real_lanes = (lane // channels) % 2 == 0
    contract_last = (((1,), (1,)), ((), ()))
    for row in range(slab_rows):
        pieces = []
        for plane in range(planes):
            cell = row * planes + plane
            values = field_ref[:, pl.ds(cell * length, length)]
            pieces += [values, values]
        stack = jnp.concatenate(pieces, axis=0)
        real = lax.dot_general(table_ref[0], stack, contract_last, preferred_element_type=jnp.float32)
        imag = lax.dot_general(table_ref[1], stack, contract_last, preferred_element_type=jnp.float32)
        modes_out[:, row, :] = jnp.where(real_lanes, real, imag).astype(modes_out.dtype)
    pl.semaphore_wait(barrier, parts - 1 + members // 2)
    swap_blocks(parts, modes_out, None, first, first_send, first_recv)
    pencil = first[...].astype(jnp.float32)
    pencil = pencil.reshape(pencil.shape[0] * pencil.shape[1], pencil.shape[2])
    pencil_t = pencil.T.astype(modes_out.dtype)
    swap_t = swap_t_ref[...]
    swapped_t = jnp.dot(swap_t, pencil_t, preferred_element_type=jnp.float32).astype(pencil_t.dtype)
    spec_t = jnp.dot(pencil_t, xcos_t_ref[...], preferred_element_type=jnp.float32)
    spec_t = spec_t + jnp.dot(swapped_t, xsin_t_ref[...], preferred_element_type=jnp.float32)
    spec_t = spec_t.astype(pencil_t.dtype).astype(jnp.float32)
    outputs = weight_ref.shape[1]
    planes = spec_t.shape[0] // (2 * outputs)
    for plane in range(planes):
        base = plane * 2 * outputs
        real = spec_t[base:base + outputs, :]
        imag = spec_t[base + outputs:base + 2 * outputs, :]
        for out in range(outputs):
            weight_real = weight_ref[0, out].astype(jnp.float32)
            weight_imag = weight_ref[1, out].astype(jnp.float32)
            mixed_t[pl.ds(base + out, 1), :] = jnp.sum(
                weight_real * real - weight_imag * imag, axis=0, keepdims=True
            )
            mixed_t[pl.ds(base + outputs + out, 1), :] = jnp.sum(
                weight_imag * real + weight_real * imag, axis=0, keepdims=True
            )
    kept = (lax.axis_index("slab") < count_ref[0]).astype(jnp.float32)
    mixed = (mixed_t[...] * kept).astype(pencil_t.dtype)
    mixed_swapped = jnp.dot(swap_t, mixed, preferred_element_type=jnp.float32).astype(pencil_t.dtype)
    contract = (((1,), (1,)), ((), ()))
    me = lax.axis_index("slab")
    member = lax.axis_index("member")
    group = 8 if parts % 8 == 0 else 1
    groups = parts // group
    rows_per = blocks.shape[1]
    span = group * rows_per

    def copy_of(source, target, peer):
        return pltpu.make_async_remote_copy(
            src_ref=blocks.at[source],
            dst_ref=landed.at[target],
            send_sem=send_sems.at[source],
            recv_sem=recv_sems.at[target],
            device_id=(member, peer),
            device_id_type=pl.DeviceIdType.MESH,
        )

    for step in range(groups):
        chosen = lax.rem(me // group + step, groups)
        start = pl.multiple_of(chosen * span, span)
        back = lax.dot_general(
            xcos_t_ref[pl.ds(start, span), :], mixed, contract, preferred_element_type=jnp.float32
        )
        back = back - lax.dot_general(
            xsin_t_ref[pl.ds(start, span), :], mixed_swapped, contract,
            preferred_element_type=jnp.float32,
        )
        blocks[pl.ds(chosen * group, group)] = back.reshape(group, rows_per, -1).astype(blocks.dtype)
        for offset in range(group):
            peer = chosen * group + lax.rem(me + offset, group)

            @pl.when(peer != me)
            def _():
                copy_of(peer, me, peer).start()

    landed[me] = blocks[me]
    for step in range(1, parts):
        source = lax.rem(me + parts - step, parts)
        copy_of(source, source, source).wait_recv()
    for step in range(1, parts):
        peer = lax.rem(me + step, parts)
        copy_of(peer, me, peer).wait_send()
    layer_values(members, landed, back_table_ref, point_weight_ref, field_ref, bias, value, layer)
    member_total(members, out_ref, layer, near, part, far, near_sems, far_send, far_recv)


def mode_mix_exchange(base, forcing, table, xcos_t, xsin_t, swap_t, weight, count, back_table, point_weight,
                      load, amplitudes, level, bias, parts, members):
    field = base
    channels = field.shape[0]
    cells_width = field.shape[1] * field.shape[2] * field.shape[3]
    modes, length = table.shape[1], table.shape[2]
    width = swap_t.shape[0]
    planes = width // (2 * channels)
    shape = (modes, cells_width // (planes * length), width)
    block_rows = channels // members
    chips = members // 2
    return pl.pallas_call(
        functools.partial(mode_mix_kernel, parts, members),
        out_shape=jax.ShapeDtypeStruct((block_rows,) + base.shape[1:], jnp.bfloat16),
        in_specs=[pl.BlockSpec(memory_space=pltpu.VMEM)] * 7
        + [pl.BlockSpec(memory_space=pltpu.SMEM)]
        + [pl.BlockSpec(memory_space=pltpu.VMEM)] * 2
        + [pl.BlockSpec(memory_space=pltpu.SMEM)] * 4,
        out_specs=pl.BlockSpec(memory_space=pltpu.VMEM),
        scratch_shapes=[
            pltpu.VMEM((channels, cells_width), jnp.bfloat16),
            pltpu.VMEM((width, modes), jnp.float32),
            pltpu.VMEM(shape, field.dtype),
            pltpu.VMEM(shape, field.dtype),
            pltpu.VMEM(shape, field.dtype),
            pltpu.VMEM(shape, field.dtype),
            pltpu.SemaphoreType.DMA((parts,)),
            pltpu.SemaphoreType.DMA((parts,)),
            pltpu.SemaphoreType.DMA((parts,)),
            pltpu.SemaphoreType.DMA((parts,)),
            pltpu.VMEM((channels, cells_width), jnp.float32),
            pltpu.VMEM((2, chips, block_rows, cells_width), jnp.bfloat16),
            pltpu.VMEM((chips, block_rows, cells_width), jnp.bfloat16),
            pltpu.VMEM((chips, block_rows, cells_width), jnp.bfloat16),
            pltpu.VMEM((chips, block_rows, cells_width), jnp.bfloat16),
            pltpu.SemaphoreType.DMA((2,)),
            pltpu.SemaphoreType.DMA((chips,)),
            pltpu.SemaphoreType.DMA((chips,)),
        ],
        compiler_params=pltpu.CompilerParams(collective_id=2, has_side_effects=True),
    )(base, forcing, table, xcos_t, xsin_t, swap_t, weight, count, back_table, point_weight, load, amplitudes,
      level, bias)


def slab_exchange(blocks, parts, exchange_id):
    return pl.pallas_call(
        functools.partial(slab_exchange_kernel, parts),
        out_shape=jax.ShapeDtypeStruct(blocks.shape, blocks.dtype),
        in_specs=[pl.BlockSpec(memory_space=pltpu.VMEM)],
        out_specs=pl.BlockSpec(memory_space=pltpu.VMEM),
        scratch_shapes=[
            pltpu.VMEM(blocks.shape, blocks.dtype),
            pltpu.SemaphoreType.DMA((parts,)),
            pltpu.SemaphoreType.DMA((parts,)),
        ],
        compiler_params=pltpu.CompilerParams(collective_id=exchange_id, has_side_effects=True),
    )(blocks)


def local(
    base_field,
    forcing,
    load,
    amplitudes,
    amp_index,
    mode_count,
    point_weight,
    point_bias,
    spectral_weight,
):
    channels, slab_rows, plane_count, length_y = base_field.shape
    slab_count = lax.axis_size("slab")
    local_modes = spectral_weight.shape[0]
    modes_y = local_modes * slab_count
    modes_x = spectral_weight.shape[1]
    length_x = slab_rows * slab_count
    packed_width = 2 * channels * plane_count
    slab_index = lax.axis_index("slab")
    cells = slab_rows * plane_count
    y_cos, y_sin = phase_tables(np.arange(modes_y), np.arange(length_y), length_y)
    forward_table = bf16_constant(np.stack([y_cos, -y_sin]))
    frequency_x = np.concatenate(
        [np.arange(modes_x // 2), np.arange(length_x - modes_x // 2, length_x)]
    )
    full_cos, full_sin = phase_tables(frequency_x, np.arange(length_x), length_x)
    lane = np.arange(packed_width)
    real_lane = (lane // channels) % 2 == 0
    swap = np.where(
        real_lane[None, :],
        (lane[:, None] == lane[None, :] + channels).astype(np.float32),
        -(lane[:, None] == lane[None, :] - channels).astype(np.float32),
    )
    weight = spectral_weight[0].transpose(1, 2, 3, 0)
    weights_y = np.where(np.arange(modes_y) == 0, 1.0, 2.0).astype(np.float32) / np.float32(
        length_x * length_y
    )
    table = bf16_constant(
        np.concatenate([weights_y[:, None] * y_cos, -(weights_y[:, None] * y_sin)], axis=0)
    )
    members = lax.axis_size("member")
    total = mode_mix_exchange(
        base_field, forcing, forward_table, bf16_constant(full_cos.T), bf16_constant(full_sin.T),
        bf16_constant(swap.T), weight, mode_count, table, point_weight, load, amplitudes, amp_index,
        point_bias, slab_count, members,
    )
    return total


def solution(mesh):
    in_specs = (
        P(None, "slab", None, None),
        P("slab", None, None),
        P(),
        P(),
        P("member"),
        P("member"),
        P(),
        P(),
        P("slab", None, None, None, None),
    )
    out_specs = P("member", "slab", None, None)
    return jax.shard_map(local, mesh=mesh, in_specs=in_specs, out_specs=out_specs, check_vma=False)
```

```python
import functools
import math

import jax
import ml_dtypes
import numpy as np
import jax.numpy as jnp
from jax import lax
from jax.experimental import pallas as pl
from jax.experimental.pallas import tpu as pltpu
from jax.sharding import PartitionSpec as P

TWO_PI = 2.0 * math.pi


def phase_tables(frequency, positions, length):
    product = np.outer(frequency, positions) % length
    angles = (product.astype(np.float32) * np.float32(TWO_PI / length)).astype(np.float64)
    return np.cos(angles).astype(np.float32), np.sin(angles).astype(np.float32)


def bf16_constant(values):
    return jnp.asarray(np.asarray(values, np.float32).astype(ml_dtypes.bfloat16))


def phases(frequency, positions, length):
    product = frequency[:, None] * positions[None, :] % length
    angles = product.astype(jnp.float32) * (TWO_PI / length)
    return (jnp.cos(angles), jnp.sin(angles))


def forward_x(pencil, cos_table, sin_table):
    row_total = pencil.shape[0]
    modes = cos_table.shape[0]
    with_cos = jnp.einsum(
        "kxf,mx->kmf", pencil, cos_table, preferred_element_type=jnp.float32
    ).reshape(row_total, modes, 2, -1)
    with_sin = jnp.einsum(
        "kxf,mx->kmf", pencil, sin_table, preferred_element_type=jnp.float32
    ).reshape(row_total, modes, 2, -1)
    real_part = with_cos[:, :, 0] + with_sin[:, :, 1]
    imag_part = with_cos[:, :, 1] - with_sin[:, :, 0]
    return jnp.stack([real_part, imag_part], axis=2).reshape(row_total, modes, -1)


def inverse_x(spectra, cos_table, sin_table):
    row_total = spectra.shape[0]
    points = cos_table.shape[1]
    with_cos = jnp.einsum(
        "kmf,mx->kxf", spectra, cos_table, preferred_element_type=jnp.float32
    ).reshape(row_total, points, 2, -1)
    with_sin = jnp.einsum(
        "kmf,mx->kxf", spectra, sin_table, preferred_element_type=jnp.float32
    ).reshape(row_total, points, 2, -1)
    real_part = with_cos[:, :, 0] - with_sin[:, :, 1]
    imag_part = with_cos[:, :, 1] + with_sin[:, :, 0]
    return jnp.stack([real_part, imag_part], axis=2).reshape(row_total, points, -1)


def mixing(weights, values):
    return jnp.einsum("kmoi,kmiz->kmoz", weights, values, preferred_element_type=jnp.float32)


def greet_members(members):
    me = lax.axis_index("member")
    slab = lax.axis_index("slab")
    chips = members // 2
    chip, core = me // 2, me % 2
    mesh_kind = pl.DeviceIdType.MESH
    barrier = pltpu.get_barrier_semaphore()
    pl.semaphore_signal(barrier, inc=1, device_id=(chip * 2 + 1 - core, slab), device_id_type=mesh_kind)
    for step in range(1, chips):
        peer = lax.rem(chip + step, chips) * 2 + core
        pl.semaphore_signal(barrier, inc=1, device_id=(peer, slab), device_id_type=mesh_kind)
    return barrier


def layer_values(members, back_ref, table_ref, weight_ref, field_ref, bias, value, layer):
    modes, slab_rows, width = back_ref.shape
    channels = weight_ref.shape[0]
    planes = width // (2 * channels)
    length = table_ref.shape[1]
    block_rows = layer.shape[2]
    table_real = table_ref[:modes, :]
    table_imag = table_ref[modes:, :]
    padding = jnp.zeros((width - modes, width), jnp.float32)
    for row in range(slab_rows):
        pencil = back_ref[:, row, :].astype(jnp.float32)
        pencil_t = jnp.concatenate([pencil, padding], axis=0).T[:, :modes].astype(back_ref.dtype)
        for plane in range(planes):
            cell = row * planes + plane
            base = plane * 2 * channels
            lanes = pl.ds(cell * length, length)
            spectral = jnp.dot(
                pencil_t[base:base + channels], table_real, preferred_element_type=jnp.float32
            )
            spectral = spectral + jnp.dot(
                pencil_t[base + channels:base + 2 * channels], table_imag,
                preferred_element_type=jnp.float32,
            )
            pointwise = jnp.dot(weight_ref[...], field_ref[:, lanes], preferred_element_type=jnp.float32)
            value[:, lanes] = jax.nn.gelu(pointwise + bias + spectral, approximate=True)
    for block in range(members):
        rows = pl.ds(block * block_rows, block_rows)
        layer[block % 2, block // 2] = value[rows, :].astype(layer.dtype)


def member_total(members, out_ref, layer, near, part, far, near_sems, far_send, far_recv):
    me = lax.axis_index("member")
    slab = lax.axis_index("slab")
    chips = members // 2
    chip, core = me // 2, me % 2
    sibling = chip * 2 + 1 - core
    mesh_kind = pl.DeviceIdType.MESH
    on_chip = pltpu.make_async_remote_copy(
        src_ref=layer.at[1 - core],
        dst_ref=near,
        send_sem=near_sems.at[0],
        recv_sem=near_sems.at[1],
        device_id=(sibling, slab),
        device_id_type=mesh_kind,
    )
    on_chip.start()
    on_chip.wait_recv()
    for index in range(chips):
        pair = layer[core, index].astype(jnp.float32) + near[index].astype(jnp.float32)
        part[index] = pair.astype(part.dtype)
    on_chip.wait_send()

    def copy_of(source, target, peer_chip):
        return pltpu.make_async_remote_copy(
            src_ref=part.at[source],
            dst_ref=far.at[target],
            send_sem=far_send.at[source],
            recv_sem=far_recv.at[target],
            device_id=(peer_chip * 2 + core, slab),
            device_id_type=mesh_kind,
        )

    for step in range(1, chips):
        peer = lax.rem(chip + step, chips)
        copy_of(peer, chip, peer).start()
    total = part[chip].astype(jnp.float32)
    for step in range(1, chips):
        source = lax.rem(chip + chips - step, chips)
        copy_of(source, source, source).wait_recv()
        total = total + far[source].astype(jnp.float32)
    for step in range(1, chips):
        peer = lax.rem(chip + step, chips)
        copy_of(peer, chip, peer).wait_send()
    mean = (total / members).astype(out_ref.dtype)
    if len(out_ref.shape) == 2:
        out_ref[...] = mean
    else:
        rows_out, planes_out, length_out = out_ref.shape[1], out_ref.shape[2], out_ref.shape[3]
        for row in range(rows_out):
            for plane in range(planes_out):
                cell = row * planes_out + plane
                out_ref[:, row, plane, :] = mean[:, cell * length_out:(cell + 1) * length_out]


def layer_sum_kernel(members, back_ref, table_ref, weight_ref, field_ref, bias_ref, out_ref, value, layer,
                     near, part, far, near_sems, far_send, far_recv):
    barrier = greet_members(members)
    layer_values(members, back_ref, table_ref, weight_ref, field_ref, bias_ref[...], value, layer)
    pl.semaphore_wait(barrier, members // 2)
    member_total(members, out_ref, layer, near, part, far, near_sems, far_send, far_recv)


def layer_sum(back, table, weight, field, bias, members):
    channels, width = field.shape
    block_rows = channels // members
    chips = members // 2
    return pl.pallas_call(
        functools.partial(layer_sum_kernel, members),
        out_shape=jax.ShapeDtypeStruct((block_rows, width), jnp.bfloat16),
        in_specs=[pl.BlockSpec(memory_space=pltpu.VMEM)] * 5,
        out_specs=pl.BlockSpec(memory_space=pltpu.VMEM),
        scratch_shapes=[
            pltpu.VMEM((channels, width), jnp.float32),
            pltpu.VMEM((2, chips, block_rows, width), jnp.bfloat16),
            pltpu.VMEM((chips, block_rows, width), jnp.bfloat16),
            pltpu.VMEM((chips, block_rows, width), jnp.bfloat16),
            pltpu.VMEM((chips, block_rows, width), jnp.bfloat16),
            pltpu.SemaphoreType.DMA((2,)),
            pltpu.SemaphoreType.DMA((chips,)),
            pltpu.SemaphoreType.DMA((chips,)),
        ],
        compiler_params=pltpu.CompilerParams(collective_id=0, has_side_effects=True),
    )(back, table, weight, field, bias)


def greet_slab(parts):
    me = lax.axis_index("slab")
    member = lax.axis_index("member")
    barrier = pltpu.get_barrier_semaphore()
    for step in range(1, parts):
        peer = lax.rem(me + step, parts)
        pl.semaphore_signal(barrier, inc=1, device_id=(member, peer), device_id_type=pl.DeviceIdType.MESH)
    return barrier


def swap_blocks(parts, source_ref, out_ref, landed, send_sems, recv_sems):
    me = lax.axis_index("slab")
    member = lax.axis_index("member")

    def copy_of(source, target, peer):
        return pltpu.make_async_remote_copy(
            src_ref=source_ref.at[source],
            dst_ref=landed.at[target],
            send_sem=send_sems.at[source],
            recv_sem=recv_sems.at[target],
            device_id=(member, peer),
            device_id_type=pl.DeviceIdType.MESH,
        )

    for step in range(1, parts):
        peer = lax.rem(me + step, parts)
        copy_of(peer, me, peer).start()
    landed[me] = source_ref[me]
    for step in range(1, parts):
        source = lax.rem(me + parts - step, parts)
        copy_of(source, source, source).wait_recv()
    for step in range(1, parts):
        peer = lax.rem(me + step, parts)
        copy_of(peer, me, peer).wait_send()
    if out_ref is not None:
        out_ref[...] = landed[...]


def slab_exchange_kernel(parts, blocks_ref, out_ref, landed, send_sems, recv_sems):
    barrier = greet_slab(parts)
    pl.semaphore_wait(barrier, parts - 1)
    swap_blocks(parts, blocks_ref, out_ref, landed, send_sems, recv_sems)


def smem_column(ref, count):
    rows = lax.broadcasted_iota(jnp.int32, (count, 1), 0)
    column = jnp.zeros((count, 1), jnp.float32)
    for index in range(count):
        column = jnp.where(rows == index, ref[index], column)
    return column


def mode_mix_kernel(parts, members, base_ref, forcing_ref, table_ref, xcos_t_ref, xsin_t_ref, swap_t_ref,
                    weight_ref, count_ref, back_table_ref, point_weight_ref, load_ref, amplitude_ref,
                    level_ref, bias_ref, out_ref, field_ref, mixed_t, modes_out, first, blocks, landed,
                    first_send, first_recv, send_sems, recv_sems, value, layer, near, part, far, near_sems,
                    far_send, far_recv):
    barrier = greet_slab(parts)
    greet_members(members)
    channels, cells_width = field_ref.shape
    scale = smem_column(load_ref, channels) * amplitude_ref[level_ref[0]]
    bias = smem_column(bias_ref, channels)
    chunk = table_ref.shape[2]
    rows_here, planes_here = base_ref.shape[1], base_ref.shape[2]
    for row in range(rows_here):
        for plane in range(planes_here):
            lanes = pl.ds((row * planes_here + plane) * chunk, chunk)
            driven = base_ref[:, row, plane, :].astype(jnp.float32) + scale * forcing_ref[
                pl.ds(row, 1), plane, :
            ].astype(jnp.float32)
            field_ref[:, lanes] = (2.0 * jnp.tanh(0.5 * driven)).astype(field_ref.dtype)
    modes, slab_rows, width = modes_out.shape
    channels = field_ref.shape[0]
    planes = width // (2 * channels)
    length = table_ref.shape[2]
    lane = lax.broadcasted_iota(jnp.int32, (modes, width), 1)
    real_lanes = (lane // channels) % 2 == 0
    contract_last = (((1,), (1,)), ((), ()))
    for row in range(slab_rows):
        pieces = []
        for plane in range(planes):
            cell = row * planes + plane
            values = field_ref[:, pl.ds(cell * length, length)]
            pieces += [values, values]
        stack = jnp.concatenate(pieces, axis=0)
        real = lax.dot_general(table_ref[0], stack, contract_last, preferred_element_type=jnp.float32)
        imag = lax.dot_general(table_ref[1], stack, contract_last, preferred_element_type=jnp.float32)
        modes_out[:, row, :] = jnp.where(real_lanes, real, imag).astype(modes_out.dtype)
    pl.semaphore_wait(barrier, parts - 1 + members // 2)
    swap_blocks(parts, modes_out, None, first, first_send, first_recv)
    pencil = first[...].astype(jnp.float32)
    pencil = pencil.reshape(pencil.shape[0] * pencil.shape[1], pencil.shape[2])
    pencil_t = pencil.T.astype(modes_out.dtype)
    swap_t = swap_t_ref[...]
    swapped_t = jnp.dot(swap_t, pencil_t, preferred_element_type=jnp.float32).astype(pencil_t.dtype)
    spec_t = jnp.dot(pencil_t, xcos_t_ref[...], preferred_element_type=jnp.float32)
    spec_t = spec_t + jnp.dot(swapped_t, xsin_t_ref[...], preferred_element_type=jnp.float32)
    spec_t = spec_t.astype(pencil_t.dtype).astype(jnp.float32)
    outputs = weight_ref.shape[1]
    planes = spec_t.shape[0] // (2 * outputs)
    halves = [
        (spec_t[plane * 2 * outputs:plane * 2 * outputs + outputs, :],
         spec_t[plane * 2 * outputs + outputs:(plane + 1) * 2 * outputs, :])
        for plane in range(planes)
    ]
    for out in range(outputs):
        weight_real = weight_ref[0, out].astype(jnp.float32)
        weight_imag = weight_ref[1, out].astype(jnp.float32)
        for plane, (real, imag) in enumerate(halves):
            base = plane * 2 * outputs
            mixed_t[pl.ds(base + out, 1), :] = jnp.sum(
                weight_real * real - weight_imag * imag, axis=0, keepdims=True
            )
            mixed_t[pl.ds(base + outputs + out, 1), :] = jnp.sum(
                weight_imag * real + weight_real * imag, axis=0, keepdims=True
            )
    kept = (lax.axis_index("slab") < count_ref[0]).astype(jnp.float32)
    mixed = (mixed_t[...] * kept).astype(pencil_t.dtype)
    mixed_swapped = jnp.dot(swap_t, mixed, preferred_element_type=jnp.float32).astype(pencil_t.dtype)
    contract = (((1,), (1,)), ((), ()))
    back = lax.dot_general(xcos_t_ref[...], mixed, contract, preferred_element_type=jnp.float32)
    back = back - lax.dot_general(
        xsin_t_ref[...], mixed_swapped, contract, preferred_element_type=jnp.float32
    )
    blocks[...] = back.reshape(blocks.shape).astype(blocks.dtype)
    swap_blocks(parts, blocks, None, landed, send_sems, recv_sems)
    layer_values(members, landed, back_table_ref, point_weight_ref, field_ref, bias, value, layer)
    member_total(members, out_ref, layer, near, part, far, near_sems, far_send, far_recv)


def mode_mix_exchange(base, forcing, table, xcos_t, xsin_t, swap_t, weight, count, back_table, point_weight,
                      load, amplitudes, level, bias, parts, members):
    field = base
    channels = field.shape[0]
    cells_width = field.shape[1] * field.shape[2] * field.shape[3]
    modes, length = table.shape[1], table.shape[2]
    width = swap_t.shape[0]
    planes = width // (2 * channels)
    shape = (modes, cells_width // (planes * length), width)
    block_rows = channels // members
    chips = members // 2
    return pl.pallas_call(
        functools.partial(mode_mix_kernel, parts, members),
        out_shape=jax.ShapeDtypeStruct((block_rows,) + base.shape[1:], jnp.bfloat16),
        in_specs=[pl.BlockSpec(memory_space=pltpu.VMEM)] * 7
        + [pl.BlockSpec(memory_space=pltpu.SMEM)]
        + [pl.BlockSpec(memory_space=pltpu.VMEM)] * 2
        + [pl.BlockSpec(memory_space=pltpu.SMEM)] * 4,
        out_specs=pl.BlockSpec(memory_space=pltpu.VMEM),
        scratch_shapes=[
            pltpu.VMEM((channels, cells_width), jnp.bfloat16),
            pltpu.VMEM((width, modes), jnp.float32),
            pltpu.VMEM(shape, field.dtype),
            pltpu.VMEM(shape, field.dtype),
            pltpu.VMEM(shape, field.dtype),
            pltpu.VMEM(shape, field.dtype),
            pltpu.SemaphoreType.DMA((parts,)),
            pltpu.SemaphoreType.DMA((parts,)),
            pltpu.SemaphoreType.DMA((parts,)),
            pltpu.SemaphoreType.DMA((parts,)),
            pltpu.VMEM((channels, cells_width), jnp.float32),
            pltpu.VMEM((2, chips, block_rows, cells_width), jnp.bfloat16),
            pltpu.VMEM((chips, block_rows, cells_width), jnp.bfloat16),
            pltpu.VMEM((chips, block_rows, cells_width), jnp.bfloat16),
            pltpu.VMEM((chips, block_rows, cells_width), jnp.bfloat16),
            pltpu.SemaphoreType.DMA((2,)),
            pltpu.SemaphoreType.DMA((chips,)),
            pltpu.SemaphoreType.DMA((chips,)),
        ],
        compiler_params=pltpu.CompilerParams(collective_id=2, has_side_effects=True),
    )(base, forcing, table, xcos_t, xsin_t, swap_t, weight, count, back_table, point_weight, load, amplitudes,
      level, bias)


def slab_exchange(blocks, parts, exchange_id):
    return pl.pallas_call(
        functools.partial(slab_exchange_kernel, parts),
        out_shape=jax.ShapeDtypeStruct(blocks.shape, blocks.dtype),
        in_specs=[pl.BlockSpec(memory_space=pltpu.VMEM)],
        out_specs=pl.BlockSpec(memory_space=pltpu.VMEM),
        scratch_shapes=[
            pltpu.VMEM(blocks.shape, blocks.dtype),
            pltpu.SemaphoreType.DMA((parts,)),
            pltpu.SemaphoreType.DMA((parts,)),
        ],
        compiler_params=pltpu.CompilerParams(collective_id=exchange_id, has_side_effects=True),
    )(blocks)


def local(
    base_field,
    forcing,
    load,
    amplitudes,
    amp_index,
    mode_count,
    point_weight,
    point_bias,
    spectral_weight,
):
    channels, slab_rows, plane_count, length_y = base_field.shape
    slab_count = lax.axis_size("slab")
    local_modes = spectral_weight.shape[0]
    modes_y = local_modes * slab_count
    modes_x = spectral_weight.shape[1]
    length_x = slab_rows * slab_count
    packed_width = 2 * channels * plane_count
    slab_index = lax.axis_index("slab")
    cells = slab_rows * plane_count
    y_cos, y_sin = phase_tables(np.arange(modes_y), np.arange(length_y), length_y)
    forward_table = bf16_constant(np.stack([y_cos, -y_sin]))
    frequency_x = np.concatenate(
        [np.arange(modes_x // 2), np.arange(length_x - modes_x // 2, length_x)]
    )
    full_cos, full_sin = phase_tables(frequency_x, np.arange(length_x), length_x)
    lane = np.arange(packed_width)
    real_lane = (lane // channels) % 2 == 0
    swap = np.where(
        real_lane[None, :],
        (lane[:, None] == lane[None, :] + channels).astype(np.float32),
        -(lane[:, None] == lane[None, :] - channels).astype(np.float32),
    )
    weight = spectral_weight[0].transpose(1, 2, 3, 0)
    weights_y = np.where(np.arange(modes_y) == 0, 1.0, 2.0).astype(np.float32) / np.float32(
        length_x * length_y
    )
    table = bf16_constant(
        np.concatenate([weights_y[:, None] * y_cos, -(weights_y[:, None] * y_sin)], axis=0)
    )
    members = lax.axis_size("member")
    total = mode_mix_exchange(
        base_field, forcing, forward_table, bf16_constant(full_cos.T), bf16_constant(full_sin.T),
        bf16_constant(swap.T), weight, mode_count, table, point_weight, load, amplitudes, amp_index,
        point_bias, slab_count, members,
    )
    return total


def solution(mesh):
    in_specs = (
        P(None, "slab", None, None),
        P("slab", None, None),
        P(),
        P(),
        P("member"),
        P("member"),
        P(),
        P(),
        P("slab", None, None, None, None),
    )
    out_specs = P("member", "slab", None, None)
    return jax.shard_map(local, mesh=mesh, in_specs=in_specs, out_specs=out_specs, check_vma=False)
```

```python
import functools
import math

import jax
import ml_dtypes
import numpy as np
import jax.numpy as jnp
from jax import lax
from jax.experimental import pallas as pl
from jax.experimental.pallas import tpu as pltpu
from jax.sharding import PartitionSpec as P

TWO_PI = 2.0 * math.pi


def phase_tables(frequency, positions, length):
    product = np.outer(frequency, positions) % length
    angles = (product.astype(np.float32) * np.float32(TWO_PI / length)).astype(np.float64)
    return np.cos(angles).astype(np.float32), np.sin(angles).astype(np.float32)


def bf16_constant(values):
    return jnp.asarray(np.asarray(values, np.float32).astype(ml_dtypes.bfloat16))


def phases(frequency, positions, length):
    product = frequency[:, None] * positions[None, :] % length
    angles = product.astype(jnp.float32) * (TWO_PI / length)
    return (jnp.cos(angles), jnp.sin(angles))


def forward_x(pencil, cos_table, sin_table):
    row_total = pencil.shape[0]
    modes = cos_table.shape[0]
    with_cos = jnp.einsum(
        "kxf,mx->kmf", pencil, cos_table, preferred_element_type=jnp.float32
    ).reshape(row_total, modes, 2, -1)
    with_sin = jnp.einsum(
        "kxf,mx->kmf", pencil, sin_table, preferred_element_type=jnp.float32
    ).reshape(row_total, modes, 2, -1)
    real_part = with_cos[:, :, 0] + with_sin[:, :, 1]
    imag_part = with_cos[:, :, 1] - with_sin[:, :, 0]
    return jnp.stack([real_part, imag_part], axis=2).reshape(row_total, modes, -1)


def inverse_x(spectra, cos_table, sin_table):
    row_total = spectra.shape[0]
    points = cos_table.shape[1]
    with_cos = jnp.einsum(
        "kmf,mx->kxf", spectra, cos_table, preferred_element_type=jnp.float32
    ).reshape(row_total, points, 2, -1)
    with_sin = jnp.einsum(
        "kmf,mx->kxf", spectra, sin_table, preferred_element_type=jnp.float32
    ).reshape(row_total, points, 2, -1)
    real_part = with_cos[:, :, 0] - with_sin[:, :, 1]
    imag_part = with_cos[:, :, 1] + with_sin[:, :, 0]
    return jnp.stack([real_part, imag_part], axis=2).reshape(row_total, points, -1)


def mixing(weights, values):
    return jnp.einsum("kmoi,kmiz->kmoz", weights, values, preferred_element_type=jnp.float32)


def greet_members(members):
    me = lax.axis_index("member")
    slab = lax.axis_index("slab")
    chips = members // 2
    chip, core = me // 2, me % 2
    mesh_kind = pl.DeviceIdType.MESH
    barrier = pltpu.get_barrier_semaphore()
    pl.semaphore_signal(barrier, inc=1, device_id=(chip * 2 + 1 - core, slab), device_id_type=mesh_kind)
    for step in range(1, chips):
        peer = lax.rem(chip + step, chips) * 2 + core
        pl.semaphore_signal(barrier, inc=1, device_id=(peer, slab), device_id_type=mesh_kind)
    return barrier


def layer_values(members, back_ref, table_ref, weight_ref, field_ref, bias, value, layer):
    modes, slab_rows, width = back_ref.shape
    channels = weight_ref.shape[0]
    planes = width // (2 * channels)
    length = table_ref.shape[1]
    block_rows = layer.shape[2]
    table_real = table_ref[:modes, :]
    table_imag = table_ref[modes:, :]
    padding = jnp.zeros((width - modes, width), jnp.float32)
    for row in range(slab_rows):
        pencil = back_ref[:, row, :].astype(jnp.float32)
        pencil_t = jnp.concatenate([pencil, padding], axis=0).T[:, :modes].astype(back_ref.dtype)
        for plane in range(planes):
            cell = row * planes + plane
            base = plane * 2 * channels
            lanes = pl.ds(cell * length, length)
            spectral = jnp.dot(
                pencil_t[base:base + channels], table_real, preferred_element_type=jnp.float32
            )
            spectral = spectral + jnp.dot(
                pencil_t[base + channels:base + 2 * channels], table_imag,
                preferred_element_type=jnp.float32,
            )
            pointwise = jnp.dot(weight_ref[...], field_ref[:, lanes], preferred_element_type=jnp.float32)
            value[:, lanes] = jax.nn.gelu(pointwise + bias + spectral, approximate=True)
    for block in range(members):
        rows = pl.ds(block * block_rows, block_rows)
        layer[block % 2, block // 2] = value[rows, :].astype(layer.dtype)


def member_total(members, out_ref, layer, near, part, far, near_sems, far_send, far_recv):
    me = lax.axis_index("member")
    slab = lax.axis_index("slab")
    chips = members // 2
    chip, core = me // 2, me % 2
    sibling = chip * 2 + 1 - core
    mesh_kind = pl.DeviceIdType.MESH
    on_chip = pltpu.make_async_remote_copy(
        src_ref=layer.at[1 - core],
        dst_ref=near,
        send_sem=near_sems.at[0],
        recv_sem=near_sems.at[1],
        device_id=(sibling, slab),
        device_id_type=mesh_kind,
    )
    on_chip.start()
    on_chip.wait_recv()
    for index in range(chips):
        pair = layer[core, index].astype(jnp.float32) + near[index].astype(jnp.float32)
        part[index] = pair.astype(part.dtype)
    on_chip.wait_send()

    def copy_of(source, target, peer_chip):
        return pltpu.make_async_remote_copy(
            src_ref=part.at[source],
            dst_ref=far.at[target],
            send_sem=far_send.at[source],
            recv_sem=far_recv.at[target],
            device_id=(peer_chip * 2 + core, slab),
            device_id_type=mesh_kind,
        )

    for step in range(1, chips):
        peer = lax.rem(chip + step, chips)
        copy_of(peer, chip, peer).start()
    total = part[chip].astype(jnp.float32)
    for step in range(1, chips):
        source = lax.rem(chip + chips - step, chips)
        copy_of(source, source, source).wait_recv()
        total = total + far[source].astype(jnp.float32)
    for step in range(1, chips):
        peer = lax.rem(chip + step, chips)
        copy_of(peer, chip, peer).wait_send()
    mean = (total / members).astype(out_ref.dtype)
    if len(out_ref.shape) == 2:
        out_ref[...] = mean
    else:
        rows_out, planes_out, length_out = out_ref.shape[1], out_ref.shape[2], out_ref.shape[3]
        for row in range(rows_out):
            for plane in range(planes_out):
                cell = row * planes_out + plane
                out_ref[:, row, plane, :] = mean[:, cell * length_out:(cell + 1) * length_out]


def layer_sum_kernel(members, back_ref, table_ref, weight_ref, field_ref, bias_ref, out_ref, value, layer,
                     near, part, far, near_sems, far_send, far_recv):
    barrier = greet_members(members)
    layer_values(members, back_ref, table_ref, weight_ref, field_ref, bias_ref[...], value, layer)
    pl.semaphore_wait(barrier, members // 2)
    member_total(members, out_ref, layer, near, part, far, near_sems, far_send, far_recv)


def layer_sum(back, table, weight, field, bias, members):
    channels, width = field.shape
    block_rows = channels // members
    chips = members // 2
    return pl.pallas_call(
        functools.partial(layer_sum_kernel, members),
        out_shape=jax.ShapeDtypeStruct((block_rows, width), jnp.bfloat16),
        in_specs=[pl.BlockSpec(memory_space=pltpu.VMEM)] * 5,
        out_specs=pl.BlockSpec(memory_space=pltpu.VMEM),
        scratch_shapes=[
            pltpu.VMEM((channels, width), jnp.float32),
            pltpu.VMEM((2, chips, block_rows, width), jnp.bfloat16),
            pltpu.VMEM((chips, block_rows, width), jnp.bfloat16),
            pltpu.VMEM((chips, block_rows, width), jnp.bfloat16),
            pltpu.VMEM((chips, block_rows, width), jnp.bfloat16),
            pltpu.SemaphoreType.DMA((2,)),
            pltpu.SemaphoreType.DMA((chips,)),
            pltpu.SemaphoreType.DMA((chips,)),
        ],
        compiler_params=pltpu.CompilerParams(collective_id=0, has_side_effects=True),
    )(back, table, weight, field, bias)


def greet_slab(parts):
    me = lax.axis_index("slab")
    member = lax.axis_index("member")
    barrier = pltpu.get_barrier_semaphore()
    for step in range(1, parts):
        peer = lax.rem(me + step, parts)
        pl.semaphore_signal(barrier, inc=1, device_id=(member, peer), device_id_type=pl.DeviceIdType.MESH)
    return barrier


def swap_blocks(parts, source_ref, out_ref, landed, send_sems, recv_sems):
    me = lax.axis_index("slab")
    member = lax.axis_index("member")

    def copy_of(source, target, peer):
        return pltpu.make_async_remote_copy(
            src_ref=source_ref.at[source],
            dst_ref=landed.at[target],
            send_sem=send_sems.at[source],
            recv_sem=recv_sems.at[target],
            device_id=(member, peer),
            device_id_type=pl.DeviceIdType.MESH,
        )

    for step in range(1, parts):
        peer = lax.rem(me + step, parts)
        copy_of(peer, me, peer).start()
    landed[me] = source_ref[me]
    for step in range(1, parts):
        source = lax.rem(me + parts - step, parts)
        copy_of(source, source, source).wait_recv()
    for step in range(1, parts):
        peer = lax.rem(me + step, parts)
        copy_of(peer, me, peer).wait_send()
    if out_ref is not None:
        out_ref[...] = landed[...]


def slab_exchange_kernel(parts, blocks_ref, out_ref, landed, send_sems, recv_sems):
    barrier = greet_slab(parts)
    pl.semaphore_wait(barrier, parts - 1)
    swap_blocks(parts, blocks_ref, out_ref, landed, send_sems, recv_sems)


def swap_parts(rows, channels):
    pieces = []
    for start in range(0, rows.shape[0], 2 * channels):
        pieces += [rows[start + channels:start + 2 * channels], -rows[start:start + channels]]
    return jnp.concatenate(pieces, axis=0)


def smem_column(ref, count):
    rows = lax.broadcasted_iota(jnp.int32, (count, 1), 0)
    column = jnp.zeros((count, 1), jnp.float32)
    for index in range(count):
        column = jnp.where(rows == index, ref[index], column)
    return column


def mode_mix_kernel(parts, members, base_ref, forcing_ref, table_ref, xcos_t_ref, xsin_t_ref, swap_t_ref,
                    weight_ref, count_ref, back_table_ref, point_weight_ref, load_ref, amplitude_ref,
                    level_ref, bias_ref, out_ref, field_ref, mixed_t, modes_out, first, blocks, landed,
                    first_send, first_recv, send_sems, recv_sems, value, layer, near, part, far, near_sems,
                    far_send, far_recv):
    barrier = greet_slab(parts)
    greet_members(members)
    channels, cells_width = field_ref.shape
    scale = smem_column(load_ref, channels) * amplitude_ref[level_ref[0]]
    bias = smem_column(bias_ref, channels)
    chunk = table_ref.shape[2]
    rows_here, planes_here = base_ref.shape[1], base_ref.shape[2]
    for row in range(rows_here):
        for plane in range(planes_here):
            lanes = pl.ds((row * planes_here + plane) * chunk, chunk)
            driven = base_ref[:, row, plane, :].astype(jnp.float32) + scale * forcing_ref[
                pl.ds(row, 1), plane, :
            ].astype(jnp.float32)
            field_ref[:, lanes] = (2.0 * jnp.tanh(0.5 * driven)).astype(field_ref.dtype)
    modes, slab_rows, width = modes_out.shape
    channels = field_ref.shape[0]
    planes = width // (2 * channels)
    length = table_ref.shape[2]
    lane = lax.broadcasted_iota(jnp.int32, (modes, width), 1)
    real_lanes = (lane // channels) % 2 == 0
    contract_last = (((1,), (1,)), ((), ()))
    for row in range(slab_rows):
        pieces = []
        for plane in range(planes):
            cell = row * planes + plane
            values = field_ref[:, pl.ds(cell * length, length)]
            pieces += [values, values]
        stack = jnp.concatenate(pieces, axis=0)
        real = lax.dot_general(table_ref[0], stack, contract_last, preferred_element_type=jnp.float32)
        imag = lax.dot_general(table_ref[1], stack, contract_last, preferred_element_type=jnp.float32)
        modes_out[:, row, :] = jnp.where(real_lanes, real, imag).astype(modes_out.dtype)
    pl.semaphore_wait(barrier, parts - 1 + members // 2)
    swap_blocks(parts, modes_out, None, first, first_send, first_recv)
    pencil = first[...].astype(jnp.float32)
    pencil = pencil.reshape(pencil.shape[0] * pencil.shape[1], pencil.shape[2])
    pencil_t = pencil.T.astype(modes_out.dtype)
    swap_t = swap_t_ref[...]
    swapped_t = swap_parts(pencil_t.astype(jnp.float32), channels).astype(pencil_t.dtype)
    spec_t = jnp.dot(pencil_t, xcos_t_ref[...], preferred_element_type=jnp.float32)
    spec_t = spec_t + jnp.dot(swapped_t, xsin_t_ref[...], preferred_element_type=jnp.float32)
    spec_t = spec_t.astype(pencil_t.dtype).astype(jnp.float32)
    outputs = weight_ref.shape[1]
    planes = spec_t.shape[0] // (2 * outputs)
    halves = [
        (spec_t[plane * 2 * outputs:plane * 2 * outputs + outputs, :],
         spec_t[plane * 2 * outputs + outputs:(plane + 1) * 2 * outputs, :])
        for plane in range(planes)
    ]
    for out in range(outputs):
        weight_real = weight_ref[0, out].astype(jnp.float32)
        weight_imag = weight_ref[1, out].astype(jnp.float32)
        for plane, (real, imag) in enumerate(halves):
            base = plane * 2 * outputs
            mixed_t[pl.ds(base + out, 1), :] = jnp.sum(
                weight_real * real - weight_imag * imag, axis=0, keepdims=True
            )
            mixed_t[pl.ds(base + outputs + out, 1), :] = jnp.sum(
                weight_imag * real + weight_real * imag, axis=0, keepdims=True
            )
    kept = (lax.axis_index("slab") < count_ref[0]).astype(jnp.float32)
    mixed = (mixed_t[...] * kept).astype(pencil_t.dtype)
    mixed_swapped = swap_parts(mixed.astype(jnp.float32), channels).astype(pencil_t.dtype)
    contract = (((1,), (1,)), ((), ()))
    back = lax.dot_general(xcos_t_ref[...], mixed, contract, preferred_element_type=jnp.float32)
    back = back - lax.dot_general(
        xsin_t_ref[...], mixed_swapped, contract, preferred_element_type=jnp.float32
    )
    blocks[...] = back.reshape(blocks.shape).astype(blocks.dtype)
    swap_blocks(parts, blocks, None, landed, send_sems, recv_sems)
    layer_values(members, landed, back_table_ref, point_weight_ref, field_ref, bias, value, layer)
    member_total(members, out_ref, layer, near, part, far, near_sems, far_send, far_recv)


def mode_mix_exchange(base, forcing, table, xcos_t, xsin_t, swap_t, weight, count, back_table, point_weight,
                      load, amplitudes, level, bias, parts, members):
    field = base
    channels = field.shape[0]
    cells_width = field.shape[1] * field.shape[2] * field.shape[3]
    modes, length = table.shape[1], table.shape[2]
    width = swap_t.shape[0]
    planes = width // (2 * channels)
    shape = (modes, cells_width // (planes * length), width)
    block_rows = channels // members
    chips = members // 2
    return pl.pallas_call(
        functools.partial(mode_mix_kernel, parts, members),
        out_shape=jax.ShapeDtypeStruct((block_rows,) + base.shape[1:], jnp.bfloat16),
        in_specs=[pl.BlockSpec(memory_space=pltpu.VMEM)] * 7
        + [pl.BlockSpec(memory_space=pltpu.SMEM)]
        + [pl.BlockSpec(memory_space=pltpu.VMEM)] * 2
        + [pl.BlockSpec(memory_space=pltpu.SMEM)] * 4,
        out_specs=pl.BlockSpec(memory_space=pltpu.VMEM),
        scratch_shapes=[
            pltpu.VMEM((channels, cells_width), jnp.bfloat16),
            pltpu.VMEM((width, modes), jnp.float32),
            pltpu.VMEM(shape, field.dtype),
            pltpu.VMEM(shape, field.dtype),
            pltpu.VMEM(shape, field.dtype),
            pltpu.VMEM(shape, field.dtype),
            pltpu.SemaphoreType.DMA((parts,)),
            pltpu.SemaphoreType.DMA((parts,)),
            pltpu.SemaphoreType.DMA((parts,)),
            pltpu.SemaphoreType.DMA((parts,)),
            pltpu.VMEM((channels, cells_width), jnp.float32),
            pltpu.VMEM((2, chips, block_rows, cells_width), jnp.bfloat16),
            pltpu.VMEM((chips, block_rows, cells_width), jnp.bfloat16),
            pltpu.VMEM((chips, block_rows, cells_width), jnp.bfloat16),
            pltpu.VMEM((chips, block_rows, cells_width), jnp.bfloat16),
            pltpu.SemaphoreType.DMA((2,)),
            pltpu.SemaphoreType.DMA((chips,)),
            pltpu.SemaphoreType.DMA((chips,)),
        ],
        compiler_params=pltpu.CompilerParams(collective_id=2, has_side_effects=True),
    )(base, forcing, table, xcos_t, xsin_t, swap_t, weight, count, back_table, point_weight, load, amplitudes,
      level, bias)


def slab_exchange(blocks, parts, exchange_id):
    return pl.pallas_call(
        functools.partial(slab_exchange_kernel, parts),
        out_shape=jax.ShapeDtypeStruct(blocks.shape, blocks.dtype),
        in_specs=[pl.BlockSpec(memory_space=pltpu.VMEM)],
        out_specs=pl.BlockSpec(memory_space=pltpu.VMEM),
        scratch_shapes=[
            pltpu.VMEM(blocks.shape, blocks.dtype),
            pltpu.SemaphoreType.DMA((parts,)),
            pltpu.SemaphoreType.DMA((parts,)),
        ],
        compiler_params=pltpu.CompilerParams(collective_id=exchange_id, has_side_effects=True),
    )(blocks)


def local(
    base_field,
    forcing,
    load,
    amplitudes,
    amp_index,
    mode_count,
    point_weight,
    point_bias,
    spectral_weight,
):
    channels, slab_rows, plane_count, length_y = base_field.shape
    slab_count = lax.axis_size("slab")
    local_modes = spectral_weight.shape[0]
    modes_y = local_modes * slab_count
    modes_x = spectral_weight.shape[1]
    length_x = slab_rows * slab_count
    packed_width = 2 * channels * plane_count
    slab_index = lax.axis_index("slab")
    cells = slab_rows * plane_count
    y_cos, y_sin = phase_tables(np.arange(modes_y), np.arange(length_y), length_y)
    forward_table = bf16_constant(np.stack([y_cos, -y_sin]))
    frequency_x = np.concatenate(
        [np.arange(modes_x // 2), np.arange(length_x - modes_x // 2, length_x)]
    )
    full_cos, full_sin = phase_tables(frequency_x, np.arange(length_x), length_x)
    lane = np.arange(packed_width)
    real_lane = (lane // channels) % 2 == 0
    swap = np.where(
        real_lane[None, :],
        (lane[:, None] == lane[None, :] + channels).astype(np.float32),
        -(lane[:, None] == lane[None, :] - channels).astype(np.float32),
    )
    weight = spectral_weight[0].transpose(1, 2, 3, 0)
    weights_y = np.where(np.arange(modes_y) == 0, 1.0, 2.0).astype(np.float32) / np.float32(
        length_x * length_y
    )
    table = bf16_constant(
        np.concatenate([weights_y[:, None] * y_cos, -(weights_y[:, None] * y_sin)], axis=0)
    )
    members = lax.axis_size("member")
    total = mode_mix_exchange(
        base_field, forcing, forward_table, bf16_constant(full_cos.T), bf16_constant(full_sin.T),
        bf16_constant(swap.T), weight, mode_count, table, point_weight, load, amplitudes, amp_index,
        point_bias, slab_count, members,
    )
    return total


def solution(mesh):
    in_specs = (
        P(None, "slab", None, None),
        P("slab", None, None),
        P(),
        P(),
        P("member"),
        P("member"),
        P(),
        P(),
        P("slab", None, None, None, None),
    )
    out_specs = P("member", "slab", None, None)
    return jax.shard_map(local, mesh=mesh, in_specs=in_specs, out_specs=out_specs, check_vma=False)
```
